32 devices in a mesh: groups: 2 (over x), section: 16 (over z, y, core).
Axes of the slice: x: 2, y: 2, z: 4, core: 2. Of those that a mesh axis runs over, the one named last changes fastest.
Arguments:
- acts_down: bfloat16 [32, 128, 2048], P(('groups', 'section')), parts along dimension 0, may hold values from -6 to 6
- acts_up: bfloat16 [32, 128, 2048], P(('groups', 'section')), parts along dimension 0, may hold values from -6 to 6
- cotangent_down: bfloat16 [32, 128, 2048], P(('groups', 'section')), parts along dimension 0, may hold values from -6 to 6
- cotangent_up: bfloat16 [32, 128, 2048], P(('groups', 'section')), parts along dimension 0, may hold values from -6 to 6
- ln_gain: bfloat16 [16, 2048], P('section'), may hold values from 0.5 to 1.5
- w_qkv: bfloat16 [16, 2048, 768], P('section'), may hold values from -0.125 to 0.125
- w_out: bfloat16 [16, 256, 2048], P('section'), may hold values from -0.375 to 0.375
- band_offsets: int32 [4, 2], replicated, may hold values from 1 to 3
Outputs:
- out_down: bfloat16 [32, 128, 2048], P(('groups', 'section')), parts along dimension 0
- out_up: bfloat16 [32, 128, 2048], P(('groups', 'section')), parts along dimension 0
- back_down: bfloat16 [32, 128, 2048], P(('groups', 'section')), parts along dimension 0
- back_up: bfloat16 [32, 128, 2048], P(('groups', 'section')), parts along dimension 0
- grad_gain: bfloat16 [32, 2048], P(('groups', 'section')), parts along dimension 0
- grad_qkv: bfloat16 [32, 2048, 768], P(('groups', 'section')), parts along dimension 0
- grad_out: bfloat16 [32, 256, 2048], P(('groups', 'section')), parts along dimension 0
The draws below stay inside these ranges and needn't reach their ends.
There are 2 independent parts, one for each index of `groups`. The reference program is written for one: setup_inputs(seed, part) draws one part's arguments, and reference() takes and returns one part's arrays. A program takes and returns all parts, laid end to end along the dimension named above; an argument that names none is the same for every part. Nothing has to cross between parts.
Inputs may be any that keep to these rules, and one draw needn't show every extreme that they name: `band_offsets`: for block row r of a banded section, block r - o is read for each listed o with r - o >= 0.
All inputs are finite; a program needn't handle non-finite values.
Results may differ from the reference program's by a relative error of at most 0.024.
Values may be sent and summed in bfloat16 or wider, within the bound.
No kernel may reach another device: no remote copies, remote signals or barrier semaphores. Data moves between devices by JAX's collectives and lax.ppermute only.
A program may use at most 128 MiB of HBM per device.

```python
import math
import jax
import jax.numpy as jnp
from jax import lax

D = 2048
HEADS_DEV = 2
HEAD_DIM = 128
HD = 256
TOK_MB = 128
BLOCK = 32
NB = 4
BAND = 2
TICKS = 3
SECTIONS = 16


def place_ends(drawn, own_key, smallest, top_value):
    place = [jax.random.randint(jax.random.fold_in(own_key, axis), (), 0, length) for axis, length in enumerate(drawn.shape)]
    longest = drawn.shape.index(max(drawn.shape))
    next_to = place[:longest] + [(place[longest] + 1) % drawn.shape[longest]] + place[longest + 1:]
    return drawn.at[tuple(place)].set(smallest).at[tuple(next_to)].set(top_value)


def block_levels(own_key, dims, shards, smallest, top_value):
    def one(dim, parts):
        draws = jax.random.uniform(jax.random.fold_in(jax.random.fold_in(own_key, 6), dim), (parts,), jnp.float32, smallest / len(shards), top_value / len(shards))
        return jnp.repeat(jnp.exp(draws), dims[dim] // parts).reshape((-1,) + (1,) * (len(dims) - dim - 1))

    level = one(*shards[0])
    for cut in shards[1:]:
        level = level * one(*cut)
    return level


def noise(own_key, shape, deviation, most, split=(), kind=jnp.bfloat16):
    values = jax.random.normal(own_key, shape, jnp.float32) * deviation
    if len(split) > 0:
        values = block_levels(own_key, shape, split, -0.22, 0.18) * values
    return jnp.clip(values, min=-most, max=most).astype(kind)


def setup_inputs(seed: int = 0, part: int = 0) -> dict:
    streams_of = jax.random.split(jax.random.key(seed), 9)
    own_keys = jax.random.split(jax.random.fold_in(streams_of[8], part), 9)
    acts_down = noise(own_keys[0], (SECTIONS, TOK_MB, D), 1.0, 6.0, ((0, 16),))
    acts_up = noise(own_keys[1], (SECTIONS, TOK_MB, D), 1.0, 6.0, ((0, 16),))
    cotangent_down = noise(own_keys[2], (SECTIONS, TOK_MB, D), 1.0, 6.0, ((0, 16),))
    cotangent_up = noise(own_keys[3], (SECTIONS, TOK_MB, D), 1.0, 6.0, ((0, 16),))
    ln_gain = jnp.clip(1.0 + 0.1 * jax.random.normal(streams_of[4], (SECTIONS, D), jnp.float32), 0.5, 1.5).astype(jnp.bfloat16)
    w_qkv = noise(streams_of[5], (SECTIONS, D, 3 * HD), D ** -0.5, 0.125, ((0, 16),))
    w_out = noise(streams_of[6], (SECTIONS, HD, D), HD ** -0.5, 0.375, ((0, 16),))
    band_offsets = place_ends(jax.random.randint(streams_of[7], (NB, BAND), 1, NB), jax.random.fold_in(streams_of[7], 1), 1, NB - 1).astype(jnp.int32)
    return {"acts_down": acts_down, "acts_up": acts_up, "cotangent_down": cotangent_down, "cotangent_up": cotangent_up, "ln_gain": ln_gain, "w_qkv": w_qkv, "w_out": w_out, "band_offsets": band_offsets}


def rounded(value):
    return lax.optimization_barrier(value.astype(jnp.bfloat16)).astype(jnp.float32)

def allowed_mask(parity, band_offsets, row_count):
    block_ids = jnp.arange(row_count // BLOCK, dtype=jnp.int32)
    diagonal = block_ids[None, :] == block_ids[:, None]
    listed = jnp.any(block_ids[None, :, None] == block_ids[:, None, None] - band_offsets[:, None, :], axis=-1)
    causal_blocks = block_ids[None, :] <= block_ids[:, None]
    chosen = jnp.where(parity == 0, causal_blocks, diagonal | listed)
    expanded = jnp.repeat(jnp.repeat(chosen, BLOCK, axis=0), BLOCK, axis=1)
    positions = jnp.arange(row_count, dtype=jnp.int32)
    return expanded & (positions[None, :] <= positions[:, None])

def layer(hidden, gain_row, weight_in, weight_proj, allowed):
    row_count = hidden.shape[0]
    head_width = HEADS_DEV * HEAD_DIM
    wide_rows = hidden.astype(jnp.float32)
    row_mean = lax.optimization_barrier(jnp.mean(wide_rows, axis=-1, keepdims=True))
    centred = wide_rows - row_mean
    spread = lax.optimization_barrier(jnp.mean(centred * centred, axis=-1, keepdims=True))
    normed = (centred * lax.rsqrt(spread + 1e-05) * gain_row.astype(jnp.float32)).astype(jnp.bfloat16)
    packed = jnp.dot(normed, weight_in, preferred_element_type=jnp.float32).astype(jnp.bfloat16)
    queries = packed[:, :head_width].reshape(row_count, HEADS_DEV, HEAD_DIM)
    key_rows = packed[:, head_width:2 * head_width].reshape(row_count, HEADS_DEV, HEAD_DIM)
    value_rows = packed[:, 2 * head_width:].reshape(row_count, HEADS_DEV, HEAD_DIM)
    scores = jnp.einsum('qhd,khd->hqk', queries.astype(jnp.float32), key_rows.astype(jnp.float32)) * (1.0 / math.sqrt(HEAD_DIM))
    weighted = jnp.where(allowed[None], jnp.exp(scores), 0.0)
    attn_weights = (weighted / lax.optimization_barrier(jnp.sum(weighted, axis=-1, keepdims=True))).astype(jnp.bfloat16)
    attended = jnp.einsum('hqk,khd->qhd', attn_weights.astype(jnp.float32), value_rows.astype(jnp.float32))
    attended = attended.astype(jnp.bfloat16).reshape(row_count, head_width)
    return (wide_rows + jnp.dot(attended, weight_proj, preferred_element_type=jnp.float32)).astype(jnp.bfloat16)

def backward_one(hidden, cotangent, gain_row, weight_in, weight_proj, allowed):

    def local_layer(state_in, gain_in, first_weight, second_weight):
        return layer(state_in, gain_in, first_weight, second_weight, allowed)
    ignored, pullback = jax.vjp(local_layer, hidden, gain_row, weight_in, weight_proj)
    return pullback(cotangent)

def run_direction(inputs, cotangents, gain_rows, weights_in, weights_proj, masks, roll_by):
    saved_inputs = []
    hidden = inputs
    result = inputs
    for tick_index in range(TICKS):
        saved_inputs.append(hidden)
        result = lax.map(lambda packet: layer(*packet), (hidden, gain_rows, weights_in, weights_proj, masks))
        if tick_index < TICKS - 1:
            hidden = jnp.roll(result, roll_by, axis=0)
    carried = cotangents
    running = (jnp.zeros(gain_rows.shape, jnp.float32), jnp.zeros(weights_in.shape, jnp.float32), jnp.zeros(weights_proj.shape, jnp.float32))
    input_grads = cotangents
    for tick_index in reversed(range(TICKS)):
        use_grads = lax.map(lambda packet: backward_one(*packet), (saved_inputs[tick_index], carried, gain_rows, weights_in, weights_proj, masks))
        running = tuple((running_sum + rounded(piece_grad) for running_sum, piece_grad in zip(running, use_grads[1:])))
        input_grads = use_grads[0]
        carried = jnp.roll(input_grads, -roll_by, axis=0)
    return (result, input_grads, running)

def reference(acts_down, acts_up, cotangent_down, cotangent_up, ln_gain, w_qkv, w_out, band_offsets):
    sections = acts_down.shape[0]
    row_count = acts_down.shape[1]
    section_ids = jnp.arange(sections, dtype=jnp.int32)
    masks = jax.vmap(lambda parity: allowed_mask(parity, band_offsets, row_count))(section_ids % 2)
    out_down, back_down, down_sums = run_direction(acts_down, cotangent_down, ln_gain, w_qkv, w_out, masks, 1)
    out_up, back_up, up_sums = run_direction(acts_up, cotangent_up, ln_gain, w_qkv, w_out, masks, -1)
    totals = tuple(((rounded(first_sum) + rounded(second_sum)).astype(jnp.bfloat16) for first_sum, second_sum in zip(down_sums, up_sums)))
    return (out_down, out_up, back_down, back_up, totals[0], totals[1], totals[2])
```

```python
import functools
import math

import jax
import jax.numpy as jnp
from jax import lax
from jax.experimental import pallas as pl
from jax.experimental.pallas import tpu as pltpu
from jax.sharding import PartitionSpec as P

HEADS_DEV = 2
HEAD_DIM = 128
BLOCK = 32
CHUNK = 16
F32 = jnp.float32
BF16 = jnp.bfloat16
NT = (((1,), (1,)), ((), ()))
TN = (((0,), (0,)), ((), ()))
SCALE = 1.0 / math.sqrt(HEAD_DIM)
VM = pl.BlockSpec(memory_space=pltpu.VMEM)
SM = pl.BlockSpec(memory_space=pltpu.SMEM)
ANY = pl.BlockSpec(memory_space=pl.ANY)


def dot(a, b, dims=(((1,), (0,)), ((), ()))):
    return lax.dot_general(a, b, dims, preferred_element_type=F32)


def mask_body(parity, offs_ref, rows):
    row = lax.broadcasted_iota(jnp.int32, (rows, rows), 0)
    col = lax.broadcasted_iota(jnp.int32, (rows, rows), 1)
    row_block = row // BLOCK
    col_block = col // BLOCK
    near = row_block == col_block
    for block in range(offs_ref.shape[0]):
        for listed in range(offs_ref.shape[1]):
            near = near | ((row_block == block) & (col_block == block - offs_ref[block, listed]))
    keep = (col <= row) & (near | (parity == 0))
    return jnp.where(keep, 1.0, 0.0).astype(F32)


def forward_body(h_ref, gain_ref, wq_ref, wo_ref, mask_ref, out_ref, u_ref, qkv_ref, p_ref, att_ref, st_ref):
    rows, width = h_ref.shape
    hd = HEADS_DEV * HEAD_DIM
    gain = gain_ref[...].astype(F32)
    for start in range(0, rows, CHUNK):
        part = pl.ds(start, CHUNK)
        x = h_ref[part, :].astype(F32)
        mean = jnp.sum(x, axis=-1, keepdims=True) * (1.0 / width)
        centred = x - mean
        rstd = lax.rsqrt(jnp.sum(centred * centred, axis=-1, keepdims=True) * (1.0 / width) + 1e-05)
        u_ref[part, :] = (centred * rstd * gain).astype(BF16)
        st_ref[part, :] = jnp.concatenate(
            [jnp.broadcast_to(mean, (CHUNK, 128)), jnp.broadcast_to(rstd, (CHUNK, 128))], axis=1)
    for n in range(3):
        qkv_ref[:, n * hd:(n + 1) * hd] = dot(u_ref[...], wq_ref[:, n * hd:(n + 1) * hd]).astype(BF16)
    keep = mask_ref[...]
    for head in range(HEADS_DEV):
        at = head * HEAD_DIM
        q = qkv_ref[:, at:at + HEAD_DIM]
        k = qkv_ref[:, hd + at:hd + at + HEAD_DIM]
        v = qkv_ref[:, 2 * hd + at:2 * hd + at + HEAD_DIM]
        weighted = jnp.where(keep > 0.0, jnp.exp(dot(q, k, NT) * SCALE), 0.0)
        probs = weighted / jnp.sum(weighted, axis=-1, keepdims=True)
        p_ref[head] = probs
        att_ref[:, at:at + HEAD_DIM] = dot(probs.astype(BF16), v).astype(BF16)
    for n in range(0, width, 512):
        cols = pl.ds(n, 512)
        out_ref[:, cols] = (h_ref[:, cols].astype(F32) + dot(att_ref[...], wo_ref[:, cols])).astype(BF16)


def backward_body(g_ref, h_ref, gain_ref, wq_ref, wo_ref, qkv_ref, p_ref, st_ref, e_ref, dqkv_ref, dg_ref, du_ref):
    rows, width = h_ref.shape
    hd = HEADS_DEV * HEAD_DIM
    datt = dot(g_ref[...], wo_ref[...], NT).astype(BF16)
    for head in range(HEADS_DEV):
        at = head * HEAD_DIM
        q = qkv_ref[:, at:at + HEAD_DIM]
        k = qkv_ref[:, hd + at:hd + at + HEAD_DIM]
        v = qkv_ref[:, 2 * hd + at:2 * hd + at + HEAD_DIM]
        probs = p_ref[head]
        da = datt[:, at:at + HEAD_DIM]
        dp = dot(da, v, NT).astype(BF16).astype(F32)
        dqkv_ref[:, 2 * hd + at:2 * hd + at + HEAD_DIM] = dot(probs.astype(BF16), da, TN).astype(BF16)
        ds = probs * (dp - jnp.sum(dp * probs, axis=-1, keepdims=True)) * SCALE
        ds = ds.astype(BF16)
        dqkv_ref[:, at:at + HEAD_DIM] = dot(ds, k).astype(BF16)
        dqkv_ref[:, hd + at:hd + at + HEAD_DIM] = dot(ds, q, TN).astype(BF16)
    for n in range(0, width, 512):
        cols = pl.ds(n, 512)
        du_ref[:, cols] = dot(dqkv_ref[...], wq_ref[cols, :], NT).astype(BF16)
    gain = gain_ref[...].astype(F32)
    dgain = jnp.zeros((8, width), F32)
    for start in range(0, rows, CHUNK):
        part = pl.ds(start, CHUNK)
        mean = st_ref[part, 0:1]
        rstd = st_ref[part, 128:129]
        xhat = (h_ref[part, :].astype(F32) - mean) * rstd
        du = du_ref[part, :].astype(F32)
        prod = du * xhat
        for piece in range(0, CHUNK, 8):
            dgain = dgain + prod[piece:piece + 8]
        dx = du * gain
        first = jnp.sum(dx, axis=-1, keepdims=True) * (1.0 / width)
        second = jnp.sum(dx * xhat, axis=-1, keepdims=True) * (1.0 / width)
        e = rstd * (dx - first - xhat * second) + g_ref[part, :].astype(F32)
        e_ref[part, :] = e.astype(BF16)
    dg_ref[...] = dgain


def shape_v(shape, dtype):
    return pltpu.VMEM(shape, dtype)


def params(mib):
    return pltpu.CompilerParams(vmem_limit_bytes=mib << 20)


def cost(us):
    return pl.CostEstimate(flops=int(us * 1e9), bytes_accessed=int(us * 1e5), transcendentals=0)


def first_kernel(parity, offs, gain, wq, wo, h):
    rows, width = h.shape

    def body(parity_ref, offs_ref, gain_ref, wq_ref, wo_ref, h_ref, *outs):
        mask_ref = outs[0]
        mask_ref[...] = mask_body(parity_ref[0], offs_ref, rows)
        forward_body(h_ref, gain_ref, wq_ref, wo_ref, mask_ref, *outs[1:])

    return pl.pallas_call(
        body,
        in_specs=[SM, SM, VM, VM, VM, VM],
        out_specs=[VM] * 7,
        out_shape=[shape_v((rows, rows), F32)] + forward_outs(rows, width),
        compiler_params=params(24),
        cost_estimate=cost(2),
        name="first",
    )(parity, offs, gain, wq, wo, h)


def forward_outs(rows, width):
    hd = HEADS_DEV * HEAD_DIM
    return [
        shape_v((rows, width), BF16),
        shape_v((rows, width), BF16),
        shape_v((rows, 3 * hd), BF16),
        shape_v((HEADS_DEV, rows, rows), F32),
        shape_v((rows, hd), BF16),
        shape_v((rows, 256), F32),
    ]


def forward_kernel(h, gain, wq, wo, mask):
    rows, width = h.shape
    return pl.pallas_call(
        forward_body,
        in_specs=[VM] * 5,
        out_specs=[VM] * 6,
        out_shape=forward_outs(rows, width),
        compiler_params=params(24),
        cost_estimate=cost(2),
        name="forward",
    )(h, gain, wq, wo, mask)


def backward_kernel(g, h, gain, wq, wo, saved):
    rows, width = h.shape
    hd = HEADS_DEV * HEAD_DIM
    u, qkv, probs, att, stats = saved
    e, dqkv, dgain = pl.pallas_call(
        backward_body,
        in_specs=[VM] * 8,
        out_specs=[VM] * 3,
        out_shape=[shape_v((rows, width), BF16), shape_v((rows, 3 * hd), BF16), shape_v((8, width), F32)],
        scratch_shapes=[pltpu.VMEM((rows, width), BF16)],
        compiler_params=params(24),
        cost_estimate=cost(3),
        name="backward",
    )(g, h, gain, wq, wo, qkv, probs, stats)
    return e, (u, dqkv, att, g, dgain)


def weight_kernel(uses):
    rows, width = uses[0][0].shape
    hd = HEADS_DEV * HEAD_DIM
    count = len(uses)
    step = 256

    def body(*refs):
        ins, (gain_out, wq_out, wo_out) = refs[:5 * count], refs[5 * count:5 * count + 3]
        use = [ins[5 * i:5 * i + 5] for i in range(count)]
        total = use[0][4][...]
        for i in range(1, count):
            total = total + use[i][4][...]
        gain_out[...] = jnp.sum(total, axis=0, keepdims=True).astype(BF16)
        att = jnp.concatenate([r[2][...] for r in use], axis=0)
        for n in range(0, width, 512):
            g = jnp.concatenate([r[3][:, n:n + 512] for r in use], axis=0)
            wo_out[:, n:n + 512] = dot(att, g, TN).astype(BF16)
        dqkv = jnp.concatenate([r[1][...] for r in use], axis=0)
        for m in range(0, width, step):
            u = jnp.concatenate([r[0][:, m:m + step] for r in use], axis=0)
            wq_out[m:m + step, :] = dot(u, dqkv, TN).astype(BF16)

    flat = [leaf for use in uses for leaf in use]
    return pl.pallas_call(
        body,
        in_specs=[VM] * len(flat),
        out_specs=[VM] * 3,
        out_shape=[
            jax.ShapeDtypeStruct((1, width), BF16),
            jax.ShapeDtypeStruct((width, 3 * hd), BF16),
            jax.ShapeDtypeStruct((hd, width), BF16),
        ],
        compiler_params=params(32),
        cost_estimate=cost(4),
        name="weights",
    )(*flat)


def shards(acts_down, acts_up, cotangent_down, cotangent_up, ln_gain, w_qkv, w_out, band_offsets):
    sections = lax.axis_size("section")
    index = lax.axis_index("section")
    odd = index % 2 == 1
    parity = (index % 2).astype(jnp.int32).reshape(1)
    near = [(i, i ^ 1) for i in range(sections)]
    far = [(i, (i + (1 if i % 2 else -1)) % sections) for i in range(sections)]

    def swap_near(x):
        return lax.ppermute(x, "section", near)

    def swap_far(x):
        return lax.ppermute(x, "section", far)

    gain, wq, wo = ln_gain, w_qkv[0], w_out[0]
    a0 = jnp.where(odd, acts_down[0], acts_up[0])
    b0 = jnp.where(odd, acts_up[0], acts_down[0])
    cot_a = jnp.where(odd, cotangent_down[0], cotangent_up[0])
    cot_b = jnp.where(odd, cotangent_up[0], cotangent_down[0])

    mask, a1_out, *a0_saved = first_kernel(parity, band_offsets, gain, wq, wo, a0)
    a1 = swap_far(a1_out)
    b1_out, *b0_saved = forward_kernel(b0, gain, wq, wo, mask)
    b1 = swap_near(b1_out)
    b2_out, *b1_saved = forward_kernel(b1, gain, wq, wo, mask)
    b2 = swap_far(b2_out)
    a2_out, *a1_saved = forward_kernel(a1, gain, wq, wo, mask)
    a2 = swap_near(a2_out)
    out_a, *a2_saved = forward_kernel(a2, gain, wq, wo, mask)
    ea2, use_a2 = backward_kernel(cot_a, a2, gain, wq, wo, a2_saved)
    ca1 = swap_near(ea2)
    ea1, use_a1 = backward_kernel(ca1, a1, gain, wq, wo, a1_saved)
    ca0 = swap_far(ea1)
    out_b, *b2_saved = forward_kernel(b2, gain, wq, wo, mask)
    eb2, use_b2 = backward_kernel(cot_b, b2, gain, wq, wo, b2_saved)
    cb1 = swap_far(eb2)
    eb1, use_b1 = backward_kernel(cb1, b1, gain, wq, wo, b1_saved)
    cb0 = swap_near(eb1)
    ea0, use_a0 = backward_kernel(ca0, a0, gain, wq, wo, a0_saved)
    eb0, use_b0 = backward_kernel(cb0, b0, gain, wq, wo, b0_saved)
    d_gain, d_wq, d_wo = weight_kernel([use_a2, use_a1, use_b2, use_b1, use_a0, use_b0])
    out_down = jnp.where(odd, out_a, out_b)
    out_up = jnp.where(odd, out_b, out_a)
    back_down = jnp.where(odd, ea0, eb0)
    back_up = jnp.where(odd, eb0, ea0)
    return (
        out_down[None], out_up[None], back_down[None], back_up[None], d_gain, d_wq[None], d_wo[None],
    )


def solution(mesh):
    both = ("groups", "section")
    in_specs = (
        P(both, None, None), P(both, None, None), P(both, None, None), P(both, None, None),
        P("section", None), P("section", None, None), P("section", None, None), P(),
    )
    out_specs = (
        P(both, None, None), P(both, None, None), P(both, None, None), P(both, None, None),
        P(both, None), P(both, None, None), P(both, None, None),
    )
    return jax.shard_map(shards, mesh=mesh, in_specs=in_specs, out_specs=out_specs, check_vma=False)
```

```python
import math

import jax
import jax.numpy as jnp
from jax import lax
from jax.experimental import pallas as pl
from jax.experimental.pallas import tpu as pltpu
from jax.sharding import PartitionSpec as P

HEADS_DEV = 2
HEAD_DIM = 128
BLOCK = 32
CHUNK = 16
F32 = jnp.float32
BF16 = jnp.bfloat16
NT = (((1,), (1,)), ((), ()))
TN = (((0,), (0,)), ((), ()))
SCALE = 1.0 / math.sqrt(HEAD_DIM)
VM = pl.BlockSpec(memory_space=pltpu.VMEM)
FWD_COST = 0.002
BWD_COST = 0.003
W_COST = 0.004


def dot(a, b, dims=(((1,), (0,)), ((), ()))):
    return lax.dot_general(a, b, dims, preferred_element_type=F32)


def mask_body(odd, offs_ref, rows):
    row = lax.broadcasted_iota(jnp.int32, (rows, rows), 0)
    col = lax.broadcasted_iota(jnp.int32, (rows, rows), 1)
    row_block = row // BLOCK
    col_block = col // BLOCK
    near = row_block == col_block
    for block in range(offs_ref.shape[1]):
        for listed in range(offs_ref.shape[0]):
            near = near | ((row_block == block) & (col_block == block - offs_ref[listed, block]))
    keep = (col <= row) & (near | jnp.logical_not(odd))
    return jnp.where(keep, 1.0, 0.0).astype(F32)


def forward_body(h_ref, gain_ref, wq_ref, wo_ref, mask_ref, out_ref, u_ref, qkv_ref, p_ref, att_ref, st_ref, waits=None):
    rows, width = h_ref.shape
    hd = HEADS_DEV * HEAD_DIM
    gain = gain_ref[...].astype(F32)
    for start in range(0, rows, CHUNK):
        part = pl.ds(start, CHUNK)
        x = h_ref[part, :].astype(F32)
        mean = jnp.sum(x, axis=-1, keepdims=True) * (1.0 / width)
        centred = x - mean
        rstd = lax.rsqrt(jnp.sum(centred * centred, axis=-1, keepdims=True) * (1.0 / width) + 1e-05)
        u_ref[part, :] = (centred * rstd * gain).astype(BF16)
        st_ref[part, :] = jnp.concatenate(
            [jnp.broadcast_to(mean, (CHUNK, 128)), jnp.broadcast_to(rstd, (CHUNK, 128))], axis=1)
    for n in range(3):
        if waits:
            waits[n].wait()
        qkv_ref[:, n * hd:(n + 1) * hd] = dot(u_ref[...], wq_ref[:, n * hd:(n + 1) * hd]).astype(BF16)
    keep = mask_ref[...]
    for head in range(HEADS_DEV):
        at = head * HEAD_DIM
        q = qkv_ref[:, at:at + HEAD_DIM]
        k = qkv_ref[:, hd + at:hd + at + HEAD_DIM]
        v = qkv_ref[:, 2 * hd + at:2 * hd + at + HEAD_DIM]
        weighted = jnp.where(keep > 0.0, jnp.exp(dot(q, k, NT) * SCALE), 0.0)
        probs = weighted / jnp.sum(weighted, axis=-1, keepdims=True)
        p_ref[head] = probs
        att_ref[:, at:at + HEAD_DIM] = dot(probs.astype(BF16), v).astype(BF16)
    if waits:
        waits[3].wait()
    for n in range(0, width, 512):
        cols = pl.ds(n, 512)
        out_ref[:, cols] = (h_ref[:, cols].astype(F32) + dot(att_ref[...], wo_ref[:, cols])).astype(BF16)


def backward_body(g_ref, h_ref, gain_ref, wq_ref, wo_ref, qkv_ref, p_ref, st_ref, e_ref, dqkv_ref, dg_ref, du_ref):
    rows, width = h_ref.shape
    hd = HEADS_DEV * HEAD_DIM
    datt = dot(g_ref[...], wo_ref[...], NT).astype(BF16)
    for head in range(HEADS_DEV):
        at = head * HEAD_DIM
        q = qkv_ref[:, at:at + HEAD_DIM]
        k = qkv_ref[:, hd + at:hd + at + HEAD_DIM]
        v = qkv_ref[:, 2 * hd + at:2 * hd + at + HEAD_DIM]
        probs = p_ref[head]
        da = datt[:, at:at + HEAD_DIM]
        dp = dot(da, v, NT).astype(BF16).astype(F32)
        dqkv_ref[:, 2 * hd + at:2 * hd + at + HEAD_DIM] = dot(probs.astype(BF16), da, TN).astype(BF16)
        ds = probs * (dp - jnp.sum(dp * probs, axis=-1, keepdims=True)) * SCALE
        ds = ds.astype(BF16)
        dqkv_ref[:, at:at + HEAD_DIM] = dot(ds, k).astype(BF16)
        dqkv_ref[:, hd + at:hd + at + HEAD_DIM] = dot(ds, q, TN).astype(BF16)
    for n in range(0, width, 512):
        cols = pl.ds(n, 512)
        du_ref[:, cols] = dot(dqkv_ref[...], wq_ref[cols, :], NT).astype(BF16)
    gain = gain_ref[...].astype(F32)
    dgain = jnp.zeros((8, width), F32)
    for start in range(0, rows, CHUNK):
        part = pl.ds(start, CHUNK)
        mean = st_ref[part, 0:1]
        rstd = st_ref[part, 128:129]
        xhat = (h_ref[part, :].astype(F32) - mean) * rstd
        du = du_ref[part, :].astype(F32)
        prod = du * xhat
        for piece in range(0, CHUNK, 8):
            dgain = dgain + prod[piece:piece + 8]
        dx = du * gain
        first = jnp.sum(dx, axis=-1, keepdims=True) * (1.0 / width)
        second = jnp.sum(dx * xhat, axis=-1, keepdims=True) * (1.0 / width)
        e = rstd * (dx - first - xhat * second) + g_ref[part, :].astype(F32)
        e_ref[part, :] = e.astype(BF16)
    dg_ref[...] = dgain


def shape_v(shape, dtype):
    return pltpu.VMEM(shape, dtype)


def params(mib):
    return pltpu.CompilerParams(vmem_limit_bytes=mib << 20)


def cost(us):
    return pl.CostEstimate(flops=int(us * 1e9), bytes_accessed=int(us * 1e5), transcendentals=0)


def picked(odd, when_odd, when_even, target, sem):
    def start():
        @pl.when(odd)
        def _():
            pltpu.make_async_copy(when_odd, target, sem).start()

        @pl.when(jnp.logical_not(odd))
        def _():
            pltpu.make_async_copy(when_even, target, sem).start()

    def wait():
        pltpu.make_async_copy(when_odd, target, sem).wait()

    return start, wait


def placed(odd, source, when_odd, when_even, sem):
    def start():
        @pl.when(odd)
        def _():
            pltpu.make_async_copy(source, when_odd, sem).start()

        @pl.when(jnp.logical_not(odd))
        def _():
            pltpu.make_async_copy(source, when_even, sem).start()

    def wait():
        pltpu.make_async_copy(source, when_odd, sem).wait()

    return start, wait


def is_odd():
    return lax.axis_index("section") % 2 == 1


def first_kernel(offs, gain, wq, wo, down, up):
    _, rows, width = down.shape
    hd = HEADS_DEV * HEAD_DIM

    def body(offs_hbm, gain_hbm, wq_hbm, wo_hbm, down_hbm, up_hbm,
             a_ref, b_ref, gain_ref, wq_ref, wo_ref, mask_ref, *rest):
        outs, (offs_ref, sems) = rest[:6], rest[6:]
        odd = is_odd()
        a_start, a_wait = picked(odd, down_hbm.at[0], up_hbm.at[0], a_ref, sems.at[0])
        b_start, b_wait = picked(odd, up_hbm.at[0], down_hbm.at[0], b_ref, sems.at[1])
        offs_copy = pltpu.make_async_copy(offs_hbm, offs_ref, sems.at[2])
        gain_copy = pltpu.make_async_copy(gain_hbm, gain_ref, sems.at[3])
        wo_copy = pltpu.make_async_copy(wo_hbm.at[0], wo_ref, sems.at[4])
        cols = [pl.ds(n * hd, hd) for n in range(3)]
        wq_copies = [
            pltpu.make_async_copy(wq_hbm.at[0, :, cols[n]], wq_ref.at[:, cols[n]], sems.at[5 + n]) for n in range(3)
        ]
        a_start()
        gain_copy.start()
        offs_copy.start()
        for copy in wq_copies:
            copy.start()
        wo_copy.start()
        b_start()
        offs_copy.wait()
        mask_ref[...] = mask_body(odd, offs_ref, rows)
        a_wait()
        gain_copy.wait()
        forward_body(a_ref, gain_ref, wq_ref, wo_ref, mask_ref, *outs, waits=wq_copies + [wo_copy])
        b_wait()

    hbm = pl.BlockSpec(memory_space=pltpu.HBM)
    return pl.pallas_call(
        body,
        in_specs=[hbm] * 6,
        out_specs=[VM] * 12,
        out_shape=[
            shape_v((rows, width), BF16),
            shape_v((rows, width), BF16),
            shape_v(gain.shape, BF16),
            shape_v(wq.shape[1:], BF16),
            shape_v(wo.shape[1:], BF16),
            shape_v((rows, rows), F32),
        ] + forward_outs(rows, width),
        scratch_shapes=[pltpu.SMEM(offs.shape, jnp.int32), pltpu.SemaphoreType.DMA((8,))],
        compiler_params=params(24),
        cost_estimate=cost(FWD_COST),
        name="first",
    )(offs, gain, wq, wo, down, up)


def forward_outs(rows, width):
    hd = HEADS_DEV * HEAD_DIM
    return [
        shape_v((rows, width), BF16),
        shape_v((rows, width), BF16),
        shape_v((rows, 3 * hd), BF16),
        shape_v((HEADS_DEV, rows, rows), F32),
        shape_v((rows, hd), BF16),
        shape_v((rows, 256), F32),
    ]


def forward_kernel(h, gain, wq, wo, mask):
    rows, width = h.shape
    return pl.pallas_call(
        forward_body,
        in_specs=[VM] * 5,
        out_specs=[VM] * 6,
        out_shape=forward_outs(rows, width),
        compiler_params=params(24),
        cost_estimate=cost(FWD_COST),
        name="forward",
    )(h, gain, wq, wo, mask)


def turn_kernel(h, gain, wq, wo, mask, when_odd, when_even, out_odd=None, out_even=None):
    rows, width = h.shape
    hd = HEADS_DEV * HEAD_DIM
    again = out_odd is not None

    def body(h_ref, gain_ref, wq_ref, wo_ref, mask_ref, odd_hbm, even_hbm, *rest):
        rest = rest[2:] if again else rest
        to_odd, to_even, e_ref, g_ref, u_ref, dqkv_ref, att_ref, dg_ref = rest[:8]
        out_ref, qkv_ref, p_ref, st_ref, du_ref, sems = rest[8:]
        odd = is_odd()
        g_start, g_wait = picked(odd, odd_hbm.at[0], even_hbm.at[0], g_ref, sems.at[0])
        out_start, out_wait = placed(odd, out_ref, to_odd.at[0], to_even.at[0], sems.at[1])
        g_start()
        forward_body(h_ref, gain_ref, wq_ref, wo_ref, mask_ref, out_ref, u_ref, qkv_ref, p_ref, att_ref, st_ref)
        out_start()
        g_wait()
        backward_body(g_ref, h_ref, gain_ref, wq_ref, wo_ref, qkv_ref, p_ref, st_ref, e_ref, dqkv_ref, dg_ref, du_ref)
        out_wait()

    hbm = pl.BlockSpec(memory_space=pltpu.HBM)
    operands = [h, gain, wq, wo, mask, when_odd, when_even] + ([out_odd, out_even] if again else [])
    to_odd, to_even, e, g, u, dqkv, att, dgain = pl.pallas_call(
        body,
        in_specs=[VM] * 5 + [hbm] * (len(operands) - 5),
        out_specs=[hbm] * 2 + [VM] * 6,
        out_shape=[jax.ShapeDtypeStruct((1, rows, width), BF16)] * 2 + [
            shape_v((rows, width), BF16),
            shape_v((rows, width), BF16),
            shape_v((rows, width), BF16),
            shape_v((rows, 3 * hd), BF16),
            shape_v((rows, hd), BF16),
            shape_v((8, width), F32),
        ],
        scratch_shapes=[
            pltpu.VMEM((rows, width), BF16),
            pltpu.VMEM((rows, 3 * hd), BF16),
            pltpu.VMEM((HEADS_DEV, rows, rows), F32),
            pltpu.VMEM((rows, 256), F32),
            pltpu.VMEM((rows, width), BF16),
            pltpu.SemaphoreType.DMA((2,)),
        ],
        input_output_aliases={7: 0, 8: 1} if again else {},
        compiler_params=params(24),
        cost_estimate=cost(FWD_COST + BWD_COST),
        name="turn",
    )(*operands)
    return to_odd, to_even, e, (u, dqkv, att, g, dgain)


def backward_kernel(g, h, gain, wq, wo, saved):
    rows, width = h.shape
    hd = HEADS_DEV * HEAD_DIM
    u, qkv, probs, att, stats = saved
    e, dqkv, dgain = pl.pallas_call(
        backward_body,
        in_specs=[VM] * 8,
        out_specs=[VM] * 3,
        out_shape=[shape_v((rows, width), BF16), shape_v((rows, 3 * hd), BF16), shape_v((8, width), F32)],
        scratch_shapes=[pltpu.VMEM((rows, width), BF16)],
        compiler_params=params(24),
        cost_estimate=cost(BWD_COST),
        name="backward",
    )(g, h, gain, wq, wo, qkv, probs, stats)
    return e, (u, dqkv, att, g, dgain)


def last_backward_kernel(g, h, gain, wq, wo, saved, out_odd=None, out_even=None):
    rows, width = h.shape
    hd = HEADS_DEV * HEAD_DIM
    u, qkv, probs, att, stats = saved
    again = out_odd is not None

    def body(*refs):
        ins, rest = refs[:8], refs[10 if again else 8:]
        to_odd, to_even, dqkv_ref, dg_ref, e_ref, du_ref, sem = rest
        start, wait = placed(is_odd(), e_ref, to_odd.at[0], to_even.at[0], sem)
        backward_body(*ins, e_ref, dqkv_ref, dg_ref, du_ref)
        start()
        wait()

    hbm = pl.BlockSpec(memory_space=pltpu.HBM)
    extra = [out_odd, out_even] if again else []
    to_odd, to_even, dqkv, dgain = pl.pallas_call(
        body,
        in_specs=[VM] * 8 + [hbm] * len(extra),
        out_specs=[hbm] * 2 + [VM] * 2,
        out_shape=[jax.ShapeDtypeStruct((1, rows, width), BF16)] * 2
        + [shape_v((rows, 3 * hd), BF16), shape_v((8, width), F32)],
        scratch_shapes=[
            pltpu.VMEM((rows, width), BF16), pltpu.VMEM((rows, width), BF16), pltpu.SemaphoreType.DMA,
        ],
        input_output_aliases={8: 0, 9: 1} if again else {},
        compiler_params=params(24),
        cost_estimate=cost(BWD_COST),
        name="last_backward",
    )(g, h, gain, wq, wo, qkv, probs, stats, *extra)
    return to_odd, to_even, (u, dqkv, att, g, dgain)


def weight_sums(use, width, hd, put_gain, put_wo, put_wq):
    total = use[0][4][...]
    for part in use[1:]:
        total = total + part[4][...]
    put_gain(total)
    att = jnp.concatenate([r[2][...] for r in use], axis=0)
    for n in range(0, width, 512):
        g = jnp.concatenate([r[3][:, n:n + 512] for r in use], axis=0)
        put_wo(pl.ds(n, 512), dot(att, g, TN))
    dqkv = jnp.concatenate([r[1][...] for r in use], axis=0)
    for m in range(0, width, 256):
        u = jnp.concatenate([r[0][:, m:m + 256] for r in use], axis=0)
        put_wq(pl.ds(m, 256), dot(u, dqkv, TN))


def early_weights(uses):
    rows, width = uses[0][0].shape
    hd = HEADS_DEV * HEAD_DIM
    count = len(uses)

    def body(*refs):
        gain_out, wo_out, wq_out = refs[5 * count:]

        def put_gain(value):
            gain_out[...] = value

        def put_wo(cols, value):
            wo_out[:, cols] = value

        def put_wq(at, value):
            wq_out[at, :] = value

        weight_sums([refs[5 * i:5 * i + 5] for i in range(count)], width, hd, put_gain, put_wo, put_wq)

    flat = [leaf for use in uses for leaf in use]
    return pl.pallas_call(
        body,
        in_specs=[VM] * len(flat),
        out_specs=[VM] * 3,
        out_shape=[shape_v((8, width), F32), shape_v((hd, width), F32), shape_v((width, 3 * hd), F32)],
        compiler_params=params(24),
        cost_estimate=cost(W_COST),
        name="early_weights",
    )(*flat)


def last_weights(uses, sums):
    rows, width = uses[0][0].shape
    hd = HEADS_DEV * HEAD_DIM
    count = len(uses)

    def body(*refs):
        gain_sum, wo_sum, wq_sum = refs[5 * count:5 * count + 3]
        gain_out, wo_hbm, wq_hbm, wo_buf, wq_buf, sems = refs[5 * count + 3:]
        copies = []

        def put_gain(value):
            gain_out[...] = jnp.sum(gain_sum[...] + value, axis=0, keepdims=True).astype(BF16)

        def put_wo(cols, value):
            wo_buf[:, cols] = (wo_sum[:, cols] + value).astype(BF16)
            copy = pltpu.make_async_copy(wo_buf.at[:, cols], wo_hbm.at[0, :, cols], sems.at[len(copies)])
            copy.start()
            copies.append(copy)

        def put_wq(at, value):
            wq_buf[at, :] = (wq_sum[at, :] + value).astype(BF16)
            copy = pltpu.make_async_copy(wq_buf.at[at], wq_hbm.at[0, at], sems.at[len(copies)])
            copy.start()
            copies.append(copy)

        weight_sums([refs[5 * i:5 * i + 5] for i in range(count)], width, hd, put_gain, put_wo, put_wq)
        for copy in copies:
            copy.wait()

    flat = [leaf for use in uses for leaf in use] + list(sums)
    hbm = pl.BlockSpec(memory_space=pltpu.HBM)
    return pl.pallas_call(
        body,
        in_specs=[VM] * len(flat),
        out_specs=[VM, hbm, hbm],
        out_shape=[
            jax.ShapeDtypeStruct((1, width), BF16),
            jax.ShapeDtypeStruct((1, hd, width), BF16),
            jax.ShapeDtypeStruct((1, width, 3 * hd), BF16),
        ],
        scratch_shapes=[
            pltpu.VMEM((hd, width), BF16),
            pltpu.VMEM((width, 3 * hd), BF16),
            pltpu.SemaphoreType.DMA((width // 512 + width // 256,)),
        ],
        compiler_params=params(24),
        cost_estimate=cost(W_COST),
        name="last_weights",
    )(*flat)


def shards(acts_down, acts_up, cotangent_down, cotangent_up, ln_gain, w_qkv, w_out, band_offsets):
    sections = lax.axis_size("section")
    near = [(i, i ^ 1) for i in range(sections)]
    far = [(i, (i + (1 if i % 2 else -1)) % sections) for i in range(sections)]

    def swap_near(x):
        return lax.ppermute(x, "section", near)

    def swap_far(x):
        return lax.ppermute(x, "section", far)

    def after(x, *others):
        return lax.optimization_barrier((x, *others))[0]

    def in_hbm(*arrays):
        return [pltpu.with_memory_space_constraint(x, pltpu.HBM) for x in arrays]

    cotangent_down, cotangent_up = in_hbm(cotangent_down, cotangent_up)
    a0, b0, gain, wq, wo, mask, a1_out, *a0_saved = first_kernel(
        *in_hbm(band_offsets.T, ln_gain, w_qkv, w_out, acts_down, acts_up))
    a1 = swap_far(a1_out)
    b1_out, *b0_saved = forward_kernel(after(b0, a0_saved[4]), gain, wq, wo, mask)
    b1 = swap_near(b1_out)
    b2_out, *b1_saved = forward_kernel(after(b1, b0_saved[4]), gain, wq, wo, mask)
    a1, b2_out = lax.optimization_barrier((a1, b2_out))
    b2 = swap_far(b2_out)
    a2_out, *a1_saved = forward_kernel(a1, gain, wq, wo, mask)
    a2 = swap_near(a2_out)
    out_odd, out_even, ea2, use_a2 = turn_kernel(
        after(a2, a1_saved[4]), gain, wq, wo, mask, cotangent_down, cotangent_up)
    ca1 = swap_near(ea2)
    ea1, use_a1 = backward_kernel(after(ca1, use_a2[4]), a1, gain, wq, wo, a1_saved)
    ca0 = swap_far(ea1)
    out_even, out_odd, eb2, use_b2 = turn_kernel(
        after(b2, use_a1[4]), gain, wq, wo, mask, cotangent_up, cotangent_down, out_even, out_odd)
    cb1 = swap_far(eb2)
    sums = early_weights([use_a2, use_a1, (after(use_b2[0], use_b2[4]), *use_b2[1:])])
    eb1, use_b1 = backward_kernel(after(cb1, sums[0]), b1, gain, wq, wo, b1_saved)
    cb0 = swap_near(eb1)
    back_odd, back_even, use_a0 = last_backward_kernel(after(ca0, use_b1[4]), a0, gain, wq, wo, a0_saved)
    back_even, back_odd, use_b0 = last_backward_kernel(
        after(cb0, use_a0[4]), b0, gain, wq, wo, b0_saved, back_even, back_odd)
    d_gain, d_wo, d_wq = last_weights([use_b1, use_a0, use_b0], sums)
    return out_odd, out_even, back_odd, back_even, d_gain, d_wq, d_wo


def solution(mesh):
    both = ("groups", "section")
    in_specs = (
        P(both, None, None), P(both, None, None), P(both, None, None), P(both, None, None),
        P("section", None), P("section", None, None), P("section", None, None), P(),
    )
    out_specs = (
        P(both, None, None), P(both, None, None), P(both, None, None), P(both, None, None),
        P(both, None), P(both, None, None), P(both, None, None),
    )
    return jax.shard_map(shards, mesh=mesh, in_specs=in_specs, out_specs=out_specs, check_vma=False)
```

```python
import math

import jax
import jax.numpy as jnp
from jax import lax
from jax.experimental import pallas as pl
from jax.experimental.pallas import tpu as pltpu
from jax.sharding import PartitionSpec as P

HEADS_DEV = 2
HEAD_DIM = 128
BLOCK = 32
CHUNK = 16
F32 = jnp.float32
BF16 = jnp.bfloat16
NT = (((1,), (1,)), ((), ()))
TN = (((0,), (0,)), ((), ()))
SCALE = 1.0 / math.sqrt(HEAD_DIM)
VM = pl.BlockSpec(memory_space=pltpu.VMEM)
NEAR_PARTS = 2


def dot(a, b, dims=(((1,), (0,)), ((), ()))):
    return lax.dot_general(a, b, dims, preferred_element_type=F32)


def mask_body(odd, offs_ref, rows):
    row = lax.broadcasted_iota(jnp.int32, (rows, rows), 0)
    col = lax.broadcasted_iota(jnp.int32, (rows, rows), 1)
    row_block = row // BLOCK
    col_block = col // BLOCK
    near = row_block == col_block
    for block in range(offs_ref.shape[1]):
        for listed in range(offs_ref.shape[0]):
            near = near | ((row_block == block) & (col_block == block - offs_ref[listed, block]))
    keep = (col <= row) & (near | jnp.logical_not(odd))
    return jnp.where(keep, 1.0, 0.0).astype(F32)


def read(refs, at, size, cols=slice(None)):
    held = refs[0].shape[0]
    return refs[at // held][pl.ds(at % held, size), cols]


def write(refs, at, size, value, cols=slice(None)):
    held = refs[0].shape[0]
    refs[at // held][pl.ds(at % held, size), cols] = value


def whole(refs, cols=slice(None)):
    return jnp.concatenate([ref[:, cols] for ref in refs], axis=0)


def forward_body(h, gain_ref, wq_ref, wo_ref, mask_ref, out, u_ref, qkv_ref, p_ref, att_ref, st_ref, waits=None):
    rows, width = u_ref.shape
    hd = HEADS_DEV * HEAD_DIM
    gain = gain_ref[...].astype(F32)
    for start in range(0, rows, CHUNK):
        part = pl.ds(start, CHUNK)
        x = read(h, start, CHUNK).astype(F32)
        mean = jnp.sum(x, axis=-1, keepdims=True) * (1.0 / width)
        centred = x - mean
        rstd = lax.rsqrt(jnp.sum(centred * centred, axis=-1, keepdims=True) * (1.0 / width) + 1e-05)
        u_ref[part, :] = (centred * rstd * gain).astype(BF16)
        st_ref[part, :] = jnp.concatenate(
            [jnp.broadcast_to(mean, (CHUNK, 128)), jnp.broadcast_to(rstd, (CHUNK, 128))], axis=1)
    for n in range(3):
        if waits:
            waits[n].wait()
        qkv_ref[:, n * hd:(n + 1) * hd] = dot(u_ref[...], wq_ref[:, n * hd:(n + 1) * hd]).astype(BF16)
    keep = mask_ref[...]
    for head in range(HEADS_DEV):
        at = head * HEAD_DIM
        q = qkv_ref[:, at:at + HEAD_DIM]
        k = qkv_ref[:, hd + at:hd + at + HEAD_DIM]
        v = qkv_ref[:, 2 * hd + at:2 * hd + at + HEAD_DIM]
        weighted = jnp.where(keep > 0.0, jnp.exp(dot(q, k, NT) * SCALE), 0.0)
        probs = weighted / jnp.sum(weighted, axis=-1, keepdims=True)
        p_ref[head] = probs
        att_ref[:, at:at + HEAD_DIM] = dot(probs.astype(BF16), v).astype(BF16)
    if waits:
        waits[3].wait()
    for n in range(0, width, 512):
        cols = pl.ds(n, 512)
        value = dot(att_ref[...], wo_ref[:, cols])
        size = min(out[0].shape[0], h[0].shape[0])
        for at in range(0, rows, size):
            write(out, at, size, (read(h, at, size, cols).astype(F32) + value[at:at + size]).astype(BF16), cols)


def backward_body(g, h, gain_ref, wq_ref, wo_ref, qkv_ref, p_ref, st_ref, e, dqkv_ref, dg_ref, du_ref, done=None):
    rows, width = du_ref.shape
    hd = HEADS_DEV * HEAD_DIM
    datt = dot(whole(g), wo_ref[...], NT).astype(BF16)
    for head in range(HEADS_DEV):
        at = head * HEAD_DIM
        q = qkv_ref[:, at:at + HEAD_DIM]
        k = qkv_ref[:, hd + at:hd + at + HEAD_DIM]
        v = qkv_ref[:, 2 * hd + at:2 * hd + at + HEAD_DIM]
        probs = p_ref[head]
        da = datt[:, at:at + HEAD_DIM]
        dp = dot(da, v, NT).astype(BF16).astype(F32)
        dqkv_ref[:, 2 * hd + at:2 * hd + at + HEAD_DIM] = dot(probs.astype(BF16), da, TN).astype(BF16)
        ds = probs * (dp - jnp.sum(dp * probs, axis=-1, keepdims=True)) * SCALE
        ds = ds.astype(BF16)
        dqkv_ref[:, at:at + HEAD_DIM] = dot(ds, k).astype(BF16)
        dqkv_ref[:, hd + at:hd + at + HEAD_DIM] = dot(ds, q, TN).astype(BF16)
    for n in range(0, width, 512):
        cols = pl.ds(n, 512)
        du_ref[:, cols] = dot(dqkv_ref[...], wq_ref[cols, :], NT).astype(BF16)
    gain = gain_ref[...].astype(F32)
    dgain = jnp.zeros((8, width), F32)
    for start in range(0, rows, CHUNK):
        part = pl.ds(start, CHUNK)
        mean = st_ref[part, 0:1]
        rstd = st_ref[part, 128:129]
        xhat = (read(h, start, CHUNK).astype(F32) - mean) * rstd
        du = du_ref[part, :].astype(F32)
        prod = du * xhat
        for piece in range(0, CHUNK, 8):
            dgain = dgain + prod[piece:piece + 8]
        dx = du * gain
        first = jnp.sum(dx, axis=-1, keepdims=True) * (1.0 / width)
        second = jnp.sum(dx * xhat, axis=-1, keepdims=True) * (1.0 / width)
        value = rstd * (dx - first - xhat * second) + read(g, start, CHUNK).astype(F32)
        write(e, start, CHUNK, value.astype(BF16))
        if done:
            done(part)
    dg_ref[...] = dgain


def params(mib):
    return pltpu.CompilerParams(vmem_limit_bytes=mib << 20)


def cost(us):
    return pl.CostEstimate(flops=int(us * 1e9), bytes_accessed=int(us * 1e5), transcendentals=0)


def by_place(odd, when_odd, when_even):
    def start():
        pl.when(odd)(when_odd.start)
        pl.when(jnp.logical_not(odd))(when_even.start)

    return start, when_odd.wait


def is_odd():
    return lax.axis_index("section") % 2 == 1


def call(name, body, operands, outs, scratch=(), hbm=(), alias=(), us=0.002, mib=24):
    flat_in, tree_in = jax.tree.flatten(operands, is_leaf=lambda x: isinstance(x, Far))
    flat_out, tree_out = jax.tree.flatten(outs, is_leaf=lambda x: isinstance(x, (jax.ShapeDtypeStruct, Mem)))

    def kernel(*refs):
        a, b = len(flat_in), len(flat_in) + len(flat_out)
        body(jax.tree.unflatten(tree_in, refs[:a]), jax.tree.unflatten(tree_out, refs[a:b]), refs[b:])

    far = pl.BlockSpec(memory_space=pltpu.HBM)
    result = pl.pallas_call(
        kernel,
        in_specs=[far if isinstance(x, Far) else VM for x in flat_in],
        out_specs=[far if isinstance(x, jax.ShapeDtypeStruct) else VM for x in flat_out],
        out_shape=[x if isinstance(x, jax.ShapeDtypeStruct) else pltpu.VMEM(x.shape, x.dtype) for x in flat_out],
        scratch_shapes=list(scratch),
        input_output_aliases=dict(alias),
        compiler_params=params(mib),
        cost_estimate=cost(us),
        name=name,
    )(*[x.array if isinstance(x, Far) else x for x in flat_in])
    return jax.tree.unflatten(tree_out, result)


class Far:
    def __init__(self, array):
        self.array = pltpu.with_memory_space_constraint(array, pltpu.HBM)


class Mem:
    def __init__(self, shape, dtype):
        self.shape, self.dtype = shape, dtype


def stream(rows, width, parts):
    return [Mem((rows // parts, width), BF16) for _ in range(parts)]


def saved_outs(rows, width):
    hd = HEADS_DEV * HEAD_DIM
    return [
        Mem((rows, width), BF16),
        Mem((rows, 3 * hd), BF16),
        Mem((HEADS_DEV, rows, rows), F32),
        Mem((rows, hd), BF16),
        Mem((rows, 256), F32),
    ]


def first_kernel(offs, gain, wq, wo, down, up, parts):
    _, rows, width = down.shape
    hd = HEADS_DEV * HEAD_DIM

    def body(ins, outs, scratch):
        offs_hbm, gain_hbm, wq_hbm, wo_hbm, down_hbm, up_hbm = ins
        (a_ref,), (b_ref,), gain_ref, wq_ref, wo_ref, mask_ref, out, saved = outs
        offs_ref, sems = scratch
        odd = is_odd()

        def pick(source, target, sem):
            return pltpu.make_async_copy(source, target, sems.at[sem])

        a_start, a_wait = by_place(odd, pick(down_hbm.at[0], a_ref, 0), pick(up_hbm.at[0], a_ref, 0))
        b_start, b_wait = by_place(odd, pick(up_hbm.at[0], b_ref, 1), pick(down_hbm.at[0], b_ref, 1))
        offs_copy = pick(offs_hbm, offs_ref, 2)
        gain_copy = pick(gain_hbm, gain_ref, 3)
        wo_copy = pick(wo_hbm.at[0], wo_ref, 4)
        cols = [pl.ds(n * hd, hd) for n in range(3)]
        wq_copies = [pick(wq_hbm.at[0, :, cols[n]], wq_ref.at[:, cols[n]], 5 + n) for n in range(3)]
        a_start()
        gain_copy.start()
        offs_copy.start()
        for copy in wq_copies:
            copy.start()
        wo_copy.start()
        b_start()
        offs_copy.wait()
        mask_ref[...] = mask_body(odd, offs_ref, rows)
        a_wait()
        gain_copy.wait()
        forward_body([a_ref], gain_ref, wq_ref, wo_ref, mask_ref, out, *saved, waits=wq_copies + [wo_copy])
        b_wait()

    return call(
        "first", body, [Far(x) for x in (offs, gain, wq, wo, down, up)],
        [
            stream(rows, width, 1), stream(rows, width, 1), Mem(gain.shape, BF16), Mem(wq.shape[1:], BF16),
            Mem(wo.shape[1:], BF16), Mem((rows, rows), F32), stream(rows, width, parts), saved_outs(rows, width),
        ],
        [pltpu.SMEM(offs.shape, jnp.int32), pltpu.SemaphoreType.DMA((8,))],
    )


def forward_kernel(h, fixed, mask, parts, us=0.002):
    rows, width = h[0].shape[0] * len(h), h[0].shape[1]

    def body(ins, outs, scratch):
        h, fixed, mask_ref = ins
        out, saved = outs
        forward_body(h, *fixed, mask_ref, out, *saved)

    return call("forward", body, [h, fixed, mask], [stream(rows, width, parts), saved_outs(rows, width)], us=us)


def turn_kernel(h, fixed, mask, when_odd, when_even, parts, so_far=()):
    rows, width = h[0].shape[0] * len(h), h[0].shape[1]
    hd = HEADS_DEV * HEAD_DIM

    def body(ins, outs, scratch):
        h, fixed, mask_ref, (odd_hbm, even_hbm), _ = ins
        (to_odd, to_even), e, (u_ref, dqkv_ref, att_ref, (g_ref,), dg_ref) = outs
        out_ref, qkv_ref, p_ref, st_ref, du_ref, sems = scratch
        odd = is_odd()
        g_start, g_wait = by_place(
            odd, pltpu.make_async_copy(odd_hbm.at[0], g_ref, sems.at[0]),
            pltpu.make_async_copy(even_hbm.at[0], g_ref, sems.at[0]))
        out_start, out_wait = by_place(
            odd, pltpu.make_async_copy(out_ref, to_odd.at[0], sems.at[1]),
            pltpu.make_async_copy(out_ref, to_even.at[0], sems.at[1]))
        g_start()
        forward_body(h, *fixed, mask_ref, [out_ref], u_ref, qkv_ref, p_ref, att_ref, st_ref)
        out_start()
        g_wait()
        backward_body([g_ref], h, *fixed, qkv_ref, p_ref, st_ref, e, dqkv_ref, dg_ref, du_ref)
        out_wait()

    operands = [h, fixed, mask, [Far(when_odd), Far(when_even)], [Far(x) for x in so_far]]
    first = len(jax.tree.leaves(operands[:3])) + 2
    return call(
        "turn", body, operands,
        [
            [jax.ShapeDtypeStruct((1, rows, width), BF16)] * 2,
            stream(rows, width, parts),
            [Mem((rows, width), BF16), Mem((rows, 3 * hd), BF16), Mem((rows, hd), BF16), stream(rows, width, 1),
             Mem((8, width), F32)],
        ],
        [
            pltpu.VMEM((rows, width), BF16),
            pltpu.VMEM((rows, 3 * hd), BF16),
            pltpu.VMEM((HEADS_DEV, rows, rows), F32),
            pltpu.VMEM((rows, 256), F32),
            pltpu.VMEM((rows, width), BF16),
            pltpu.SemaphoreType.DMA((2,)),
        ],
        alias=[(first, 0), (first + 1, 1)] if so_far else [],
    )


def backward_kernel(g, h, fixed, saved, parts):
    rows, width = saved[0].shape
    u, qkv, probs, att, stats = saved

    def body(ins, outs, scratch):
        g, h, fixed, (qkv_ref, p_ref, st_ref) = ins
        e, dqkv_ref, dg_ref = outs
        backward_body(g, h, *fixed, qkv_ref, p_ref, st_ref, e, dqkv_ref, dg_ref, *scratch)

    e, dqkv, dgain = call(
        "backward", body, [g, h, fixed, [qkv, probs, stats]],
        [stream(rows, width, parts), Mem(qkv.shape, BF16), Mem((8, width), F32)],
        [pltpu.VMEM((rows, width), BF16)],
    )
    return e, (u, dqkv, att, g, dgain)


def end_kernel(g, h, fixed, saved):
    rows, width = saved[0].shape
    u, qkv, probs, att, stats = saved

    def body(ins, outs, scratch):
        g, h, fixed, (qkv_ref, p_ref, st_ref) = ins
        (to_odd, to_even), dqkv_ref, dg_ref = outs
        e_ref, du_ref, sem = scratch
        start, wait = by_place(
            is_odd(), pltpu.make_async_copy(e_ref, to_odd.at[0], sem), pltpu.make_async_copy(e_ref, to_even.at[0], sem))
        backward_body(g, h, *fixed, qkv_ref, p_ref, st_ref, [e_ref], dqkv_ref, dg_ref, du_ref)
        start()
        wait()

    outs, dqkv, dgain = call(
        "end", body, [g, h, fixed, [qkv, probs, stats]],
        [[jax.ShapeDtypeStruct((1, rows, width), BF16)] * 2, Mem(qkv.shape, BF16), Mem((8, width), F32)],
        [pltpu.VMEM((rows, width), BF16), pltpu.VMEM((rows, width), BF16), pltpu.SemaphoreType.DMA],
    )
    return outs, (u, dqkv, att, g, dgain)


def weight_sums(uses, width, put_gain, put_wo, put_wq):
    total = uses[0][4][...]
    for use in uses[1:]:
        total = total + use[4][...]
    put_gain(total)
    att = jnp.concatenate([use[2][...] for use in uses], axis=0)
    for n in range(0, width, 512):
        cols = pl.ds(n, 512)
        put_wo(cols, dot(att, jnp.concatenate([whole(use[3], cols) for use in uses], axis=0), TN))
    dqkv = jnp.concatenate([use[1][...] for use in uses], axis=0)
    for m in range(0, width, 256):
        u = jnp.concatenate([use[0][:, m:m + 256] for use in uses], axis=0)
        put_wq(pl.ds(m, 256), dot(u, dqkv, TN))


def early_weights(uses):
    width = uses[0][0].shape[1]
    hd = HEADS_DEV * HEAD_DIM

    def body(ins, outs, scratch):
        gain_out, wo_out, wq_out = outs

        def put_gain(value):
            gain_out[...] = value

        def put_wo(cols, value):
            wo_out[:, cols] = value

        def put_wq(at, value):
            wq_out[at, :] = value

        weight_sums(ins, width, put_gain, put_wo, put_wq)

    return call(
        "early_weights", body, list(uses), [Mem((8, width), F32), Mem((hd, width), F32), Mem((width, 3 * hd), F32)])


def finish_kernel(g, h, fixed, saved, so_far, uses, sums):
    rows, width = saved[0].shape
    hd = HEADS_DEV * HEAD_DIM
    u, qkv, probs, att, stats = saved

    def body(ins, outs, scratch):
        g, h, fixed, (u_ref, qkv_ref, p_ref, att_ref, st_ref), _, uses, (gain_sum, wo_sum, wq_sum) = ins
        (to_odd, to_even), gain_out, wo_hbm, wq_hbm = outs
        e_ref, du_ref, dqkv_ref, dg_ref, wo_buf, wq_buf, sems = scratch
        copies = []
        odd = is_odd()

        def push(source, target):
            copy = pltpu.make_async_copy(source, target, sems.at[len(copies)])
            copies.append(copy.wait)
            copy.start()

        def put_gain(value):
            gain_out[...] = jnp.sum(gain_sum[...] + value, axis=0, keepdims=True).astype(BF16)

        def put_wo(cols, value):
            wo_buf[:, cols] = (wo_sum[:, cols] + value).astype(BF16)
            push(wo_buf.at[:, cols], wo_hbm.at[0, :, cols])

        def put_wq(at, value):
            wq_buf[at, :] = (wq_sum[at, :] + value).astype(BF16)
            push(wq_buf.at[at], wq_hbm.at[0, at])

        backward_body(g, h, *fixed, qkv_ref, p_ref, st_ref, [e_ref], dqkv_ref, dg_ref, du_ref)
        start, wait = by_place(
            odd, pltpu.make_async_copy(e_ref, to_odd.at[0], sems.at[0]),
            pltpu.make_async_copy(e_ref, to_even.at[0], sems.at[0]))
        start()
        copies.append(wait)
        weight_sums([*uses, (u_ref, dqkv_ref, att_ref, g, dg_ref)], width, put_gain, put_wo, put_wq)
        for wait in copies:
            wait()

    operands = [g, h, fixed, list(saved), [Far(x) for x in so_far], list(uses), list(sums)]
    first = len(jax.tree.leaves(operands[:4]))
    return call(
        "finish", body, operands,
        [
            [jax.ShapeDtypeStruct((1, rows, width), BF16)] * 2,
            Mem((1, width), BF16),
            jax.ShapeDtypeStruct((1, hd, width), BF16),
            jax.ShapeDtypeStruct((1, width, 3 * hd), BF16),
        ],
        [
            pltpu.VMEM((rows, width), BF16),
            pltpu.VMEM((rows, width), BF16),
            pltpu.VMEM(qkv.shape, BF16),
            pltpu.VMEM((8, width), F32),
            pltpu.VMEM((hd, width), BF16),
            pltpu.VMEM((width, 3 * hd), BF16),
            pltpu.SemaphoreType.DMA((1 + width // 512 + width // 256,)),
        ],
        alias=[(first, 0), (first + 1, 1)],
    )


def shards(acts_down, acts_up, cotangent_down, cotangent_up, ln_gain, w_qkv, w_out, band_offsets):
    sections = lax.axis_size("section")
    near = [(i, i ^ 1) for i in range(sections)]
    far = [(i, (i + (1 if i % 2 else -1)) % sections) for i in range(sections)]

    def swap_near(x):
        return [lax.ppermute(part, "section", near) for part in x]

    def swap_far(x):
        return [lax.ppermute(part, "section", far) for part in x]

    def after(x, other):
        return lax.optimization_barrier((x, other))[0]

    a0, b0, gain, wq, wo, mask, a1_out, a0_saved = first_kernel(
        band_offsets.T, ln_gain, w_qkv, w_out, acts_down, acts_up, 1)
    fixed = [gain, wq, wo]
    a1 = swap_far(a1_out)
    b1_out, b0_saved = forward_kernel(after(b0, a0_saved[4]), fixed, mask, NEAR_PARTS)
    b1 = swap_near(b1_out)
    b2_out, b1_saved = forward_kernel(after(b1, b0_saved[4]), fixed, mask, 1)
    b2 = swap_far(b2_out)
    a2_out, a1_saved = forward_kernel(after(a1, b1_saved[4]), fixed, mask, NEAR_PARTS, us=8)
    a2 = swap_near(a2_out)
    (out_even, out_odd), eb2, use_b2 = turn_kernel(
        after(b2, a1_saved[4]), fixed, mask, cotangent_up, cotangent_down, 1)
    cb1 = swap_far(eb2)
    (out_odd, out_even), ea2, use_a2 = turn_kernel(
        after(a2, use_b2[4]), fixed, mask, cotangent_down, cotangent_up, NEAR_PARTS, (out_odd, out_even))
    ca1 = swap_near(ea2)
    ea1, use_a1 = backward_kernel(after(ca1, use_a2[4]), a1, fixed, a1_saved, 1)
    ca0 = swap_far(ea1)
    eb1, use_b1 = backward_kernel(after(cb1, use_a1[4]), b1, fixed, b1_saved, NEAR_PARTS)
    cb0 = swap_near(eb1)
    sums = early_weights([use_b2, use_a2, use_a1, after(use_b1, use_b1[4])])
    (back_even, back_odd), use_b0 = end_kernel(after(cb0, sums[0]), b0, fixed, b0_saved)
    (back_odd, back_even), d_gain, d_wo, d_wq = finish_kernel(
        after(ca0, use_b0[4]), a0, fixed, a0_saved, (back_odd, back_even), [use_b0], sums)
    return out_odd, out_even, back_odd, back_even, d_gain, d_wq, d_wo


def solution(mesh):
    both = ("groups", "section")
    in_specs = (
        P(both, None, None), P(both, None, None), P(both, None, None), P(both, None, None),
        P("section", None), P("section", None, None), P("section", None, None), P(),
    )
    out_specs = (
        P(both, None, None), P(both, None, None), P(both, None, None), P(both, None, None),
        P(both, None), P(both, None, None), P(both, None, None),
    )
    return jax.shard_map(shards, mesh=mesh, in_specs=in_specs, out_specs=out_specs, check_vma=False)
```

```python
import math

import jax
import jax.numpy as jnp
from jax import lax
from jax.experimental import pallas as pl
from jax.experimental.pallas import tpu as pltpu
from jax.sharding import PartitionSpec as P

HEADS_DEV = 2
HEAD_DIM = 128
BLOCK = 32
CHUNK = 16
F32 = jnp.float32
BF16 = jnp.bfloat16
NT = (((1,), (1,)), ((), ()))
TN = (((0,), (0,)), ((), ()))
SCALE = 1.0 / math.sqrt(HEAD_DIM)
VM = pl.BlockSpec(memory_space=pltpu.VMEM)
NEAR_PARTS = 2


def dot(a, b, dims=(((1,), (0,)), ((), ()))):
    return lax.dot_general(a, b, dims, preferred_element_type=F32)


def mask_body(odd, offs_ref, rows):
    row = lax.broadcasted_iota(jnp.int32, (rows, rows), 0)
    col = lax.broadcasted_iota(jnp.int32, (rows, rows), 1)
    row_block = row // BLOCK
    col_block = col // BLOCK
    near = row_block == col_block
    for block in range(offs_ref.shape[1]):
        for listed in range(offs_ref.shape[0]):
            near = near | ((row_block == block) & (col_block == block - offs_ref[listed, block]))
    keep = (col <= row) & (near | jnp.logical_not(odd))
    return jnp.where(keep, 1.0, 0.0).astype(F32)


def read(refs, at, size, cols=slice(None)):
    held = refs[0].shape[0]
    return refs[at // held][pl.ds(at % held, size), cols]


def write(refs, at, size, value, cols=slice(None)):
    held = refs[0].shape[0]
    refs[at // held][pl.ds(at % held, size), cols] = value


def whole(refs, cols=slice(None)):
    return jnp.concatenate([ref[:, cols] for ref in refs], axis=0)


def forward_body(h, gain_ref, wq_ref, wo_ref, mask_ref, out, u_ref, qkv_ref, p_ref, att_ref, st_ref, waits=None):
    rows, width = u_ref.shape
    hd = HEADS_DEV * HEAD_DIM
    gain = gain_ref[...].astype(F32)
    for start in range(0, rows, CHUNK):
        part = pl.ds(start, CHUNK)
        x = read(h, start, CHUNK).astype(F32)
        mean = jnp.sum(x, axis=-1, keepdims=True) * (1.0 / width)
        centred = x - mean
        rstd = lax.rsqrt(jnp.sum(centred * centred, axis=-1, keepdims=True) * (1.0 / width) + 1e-05)
        u_ref[part, :] = (centred * rstd * gain).astype(BF16)
        st_ref[part, :] = jnp.concatenate(
            [jnp.broadcast_to(mean, (CHUNK, 128)), jnp.broadcast_to(rstd, (CHUNK, 128))], axis=1)
    for n in range(3):
        if waits:
            waits[n].wait()
        qkv_ref[:, n * hd:(n + 1) * hd] = dot(u_ref[...], wq_ref[:, n * hd:(n + 1) * hd]).astype(BF16)
    keep = mask_ref[...]
    heads = [pl.ds(head * HEAD_DIM, HEAD_DIM) for head in range(HEADS_DEV)]
    scores = [dot(qkv_ref[:, cols], qkv_ref[:, pl.ds(hd + cols.start, HEAD_DIM)], NT) for cols in heads]
    weighted = [jnp.where(keep > 0.0, jnp.exp(score * SCALE), 0.0) for score in scores]
    inverse = [1.0 / jnp.sum(value, axis=-1, keepdims=True) for value in weighted]
    probs = [value * scale for value, scale in zip(weighted, inverse)]
    mixed = [
        dot(value.astype(BF16), qkv_ref[:, pl.ds(2 * hd + cols.start, HEAD_DIM)]) for value, cols in zip(probs, heads)
    ]
    for head, cols in enumerate(heads):
        p_ref[head] = probs[head]
        att_ref[:, cols] = mixed[head].astype(BF16)
    if waits:
        waits[3].wait()
    for n in range(0, width, 512):
        cols = pl.ds(n, 512)
        value = dot(att_ref[...], wo_ref[:, cols])
        size = min(out[0].shape[0], h[0].shape[0])
        for at in range(0, rows, size):
            write(out, at, size, (read(h, at, size, cols).astype(F32) + value[at:at + size]).astype(BF16), cols)


def attention_reverse(g, wot_ref, qkv_ref, p_ref, dqkv_ref):
    hd = HEADS_DEV * HEAD_DIM
    datt = dot(whole(g), wot_ref[...]).astype(BF16)
    heads = [pl.ds(head * HEAD_DIM, HEAD_DIM) for head in range(HEADS_DEV)]
    keys = [pl.ds(hd + cols.start, HEAD_DIM) for cols in heads]
    values = [pl.ds(2 * hd + cols.start, HEAD_DIM) for cols in heads]
    das = [datt[:, cols.start:cols.start + HEAD_DIM] for cols in heads]
    probs = [p_ref[head] for head in range(HEADS_DEV)]
    dps = [dot(da, qkv_ref[:, cols], NT).astype(BF16).astype(F32) for da, cols in zip(das, values)]
    dvs = [dot(prob.astype(BF16), da, TN) for prob, da in zip(probs, das)]
    totals = [jnp.sum(dp * prob, axis=-1, keepdims=True) for dp, prob in zip(dps, probs)]
    dss = [(prob * (dp - total) * SCALE).astype(BF16) for prob, dp, total in zip(probs, dps, totals)]
    dqs = [dot(ds, qkv_ref[:, cols]) for ds, cols in zip(dss, keys)]
    dks = [dot(ds, qkv_ref[:, cols], TN) for ds, cols in zip(dss, heads)]
    for head in range(HEADS_DEV):
        dqkv_ref[:, values[head]] = dvs[head].astype(BF16)
        dqkv_ref[:, heads[head]] = dqs[head].astype(BF16)
        dqkv_ref[:, keys[head]] = dks[head].astype(BF16)


def lanes(column):
    return jnp.broadcast_to(column, (column.shape[0], 128))


def norm_reverse(g, h, gain_ref, wqt_ref, wg_ref, qkv_ref, st_ref, e, dqkv_ref, dg_ref, done=None):
    rows, width = dqkv_ref.shape[0], wqt_ref.shape[1]
    dqkv32 = dqkv_ref[...].astype(F32)
    first = jnp.sum(dqkv32 * wg_ref[...], axis=-1, keepdims=True) * (1.0 / width)
    second = jnp.sum(dqkv32 * qkv_ref[...].astype(F32), axis=-1, keepdims=True) * (1.0 / width)
    mean, rstd = st_ref[:, 0:128], st_ref[:, 128:256]
    first, second = lanes(first) * rstd, lanes(second) * rstd
    for block in range(0, width, 512):
        wide = dot(dqkv_ref[...], wqt_ref[:, block:block + 512])
        for n in range(0, 512, 128):
            cols = pl.ds(block + n, 128)
            du = wide[:, n:n + 128]
            xhat = (whole(h, cols).astype(F32) - mean) * rstd
            dg_ref[:, cols] = jnp.sum((du * xhat).reshape(rows // 8, 8, 128), axis=0)
            gain = gain_ref[:, cols].astype(F32)
            value = (du * gain) * rstd - first - xhat * second + whole(g, cols).astype(F32)
            size = e[0].shape[0]
            for part in range(len(e)):
                e[part][:, cols] = value[part * size:(part + 1) * size].astype(BF16)
        if done:
            done(pl.ds(block, 512))


def backward_body(g, h, gain_ref, wqt_ref, wot_ref, wg_ref, qkv_ref, p_ref, st_ref, e, dqkv_ref, dg_ref):
    attention_reverse(g, wot_ref, qkv_ref, p_ref, dqkv_ref)
    norm_reverse(g, h, gain_ref, wqt_ref, wg_ref, qkv_ref, st_ref, e, dqkv_ref, dg_ref)


def params(mib):
    return pltpu.CompilerParams(vmem_limit_bytes=mib << 20)


def cost(us):
    return pl.CostEstimate(flops=int(us * 1e9), bytes_accessed=int(us * 1e5), transcendentals=0)


def by_place(odd, when_odd, when_even):
    def start():
        pl.when(odd)(when_odd.start)
        pl.when(jnp.logical_not(odd))(when_even.start)

    return start, when_odd.wait


def is_odd():
    return lax.axis_index("section") % 2 == 1


def call(name, body, operands, outs, scratch=(), hbm=(), alias=(), us=0.002, mib=24):
    flat_in, tree_in = jax.tree.flatten(operands, is_leaf=lambda x: isinstance(x, Far))
    flat_out, tree_out = jax.tree.flatten(outs, is_leaf=lambda x: isinstance(x, (jax.ShapeDtypeStruct, Mem)))

    def kernel(*refs):
        a, b = len(flat_in), len(flat_in) + len(flat_out)
        body(jax.tree.unflatten(tree_in, refs[:a]), jax.tree.unflatten(tree_out, refs[a:b]), refs[b:])

    far = pl.BlockSpec(memory_space=pltpu.HBM)
    result = pl.pallas_call(
        kernel,
        in_specs=[far if isinstance(x, Far) else VM for x in flat_in],
        out_specs=[far if isinstance(x, jax.ShapeDtypeStruct) else VM for x in flat_out],
        out_shape=[x if isinstance(x, jax.ShapeDtypeStruct) else pltpu.VMEM(x.shape, x.dtype) for x in flat_out],
        scratch_shapes=list(scratch),
        input_output_aliases=dict(alias),
        compiler_params=params(mib),
        cost_estimate=cost(us),
        name=name,
    )(*[x.array if isinstance(x, Far) else x for x in flat_in])
    return jax.tree.unflatten(tree_out, result)


class Far:
    def __init__(self, array):
        self.array = pltpu.with_memory_space_constraint(array, pltpu.HBM)


class Mem:
    def __init__(self, shape, dtype):
        self.shape, self.dtype = shape, dtype


def stream(rows, width, parts):
    return [Mem((rows // parts, width), BF16) for _ in range(parts)]


def saved_outs(rows, width):
    hd = HEADS_DEV * HEAD_DIM
    return [
        Mem((rows, width), BF16),
        Mem((rows, 3 * hd), BF16),
        Mem((HEADS_DEV, rows, rows), F32),
        Mem((rows, hd), BF16),
        Mem((rows, 256), F32),
    ]


def first_kernel(offs, gain, wq, wo, down, up, parts):
    _, rows, width = down.shape
    hd = HEADS_DEV * HEAD_DIM

    def body(ins, outs, scratch):
        offs_hbm, gain_hbm, wq_hbm, wo_hbm, down_hbm, up_hbm = ins
        (a_ref,), (b_ref,), gain_ref, wq_ref, wo_ref, mask_ref, out, saved = outs
        offs_ref, sems = scratch
        odd = is_odd()

        def pick(source, target, sem):
            return pltpu.make_async_copy(source, target, sems.at[sem])

        a_start, a_wait = by_place(odd, pick(down_hbm.at[0], a_ref, 0), pick(up_hbm.at[0], a_ref, 0))
        b_start, b_wait = by_place(odd, pick(up_hbm.at[0], b_ref, 1), pick(down_hbm.at[0], b_ref, 1))
        offs_copy = pick(offs_hbm, offs_ref, 2)
        gain_copy = pick(gain_hbm, gain_ref, 3)
        wo_copy = pick(wo_hbm.at[0], wo_ref, 4)
        cols = [pl.ds(n * hd, hd) for n in range(3)]
        wq_copies = [pick(wq_hbm.at[0, :, cols[n]], wq_ref.at[:, cols[n]], 5 + n) for n in range(3)]
        a_start()
        gain_copy.start()
        offs_copy.start()
        for copy in wq_copies:
            copy.start()
        wo_copy.start()
        b_start()
        offs_copy.wait()
        mask_ref[...] = mask_body(odd, offs_ref, rows)
        a_wait()
        gain_copy.wait()
        forward_body([a_ref], gain_ref, wq_ref, wo_ref, mask_ref, out, *saved, waits=wq_copies + [wo_copy])
        b_wait()

    return call(
        "first", body, [Far(x) for x in (offs, gain, wq, wo, down, up)],
        [
            stream(rows, width, 1), stream(rows, width, 1), Mem(gain.shape, BF16), Mem(wq.shape[1:], BF16),
            Mem(wo.shape[1:], BF16), Mem((rows, rows), F32), stream(rows, width, parts), saved_outs(rows, width),
        ],
        [pltpu.SMEM(offs.shape, jnp.int32), pltpu.SemaphoreType.DMA((8,))],
    )


def forward_kernel(h, fixed, mask, parts, us=0.002):
    rows, width = h[0].shape[0] * len(h), h[0].shape[1]

    def body(ins, outs, scratch):
        h, fixed, mask_ref = ins
        out, saved = outs
        forward_body(h, *fixed, mask_ref, out, *saved)

    return call("forward", body, [h, fixed, mask], [stream(rows, width, parts), saved_outs(rows, width)], us=us)


def prepare_kernel(gain, wq, wo, tie, down, up):
    _, rows, width = down.shape
    hd = HEADS_DEV * HEAD_DIM

    def body(ins, outs, scratch):
        gain_ref, wq_ref, wo_ref, _, down_hbm, up_hbm = ins
        wqt_ref, wot_ref, wg_ref, (a_ref,), (b_ref,) = outs
        (sems,) = scratch
        odd = is_odd()

        def pick(source, target, sem):
            return pltpu.make_async_copy(source.at[0], target, sems.at[sem])

        a_start, a_wait = by_place(odd, pick(down_hbm, a_ref, 0), pick(up_hbm, a_ref, 0))
        b_start, b_wait = by_place(odd, pick(up_hbm, b_ref, 1), pick(down_hbm, b_ref, 1))
        a_start()
        b_start()
        for at in range(0, width, 256):
            wqt_ref[:, at:at + 256] = wq_ref[at:at + 256, :].T
            wot_ref[at:at + 256, :] = wo_ref[:, at:at + 256].T
        wg_ref[...] = dot(gain_ref[...], wq_ref[...])
        a_wait()
        b_wait()

    return call(
        "prepare", body, [gain, wq, wo, tie, Far(down), Far(up)],
        [Mem((3 * hd, width), BF16), Mem((width, hd), BF16), Mem((1, 3 * hd), F32),
         stream(rows, width, 1), stream(rows, width, 1)],
        [pltpu.SemaphoreType.DMA((2,))],
    )


def turn_kernel(h, g, fixed, mask, turned, parts):
    rows, width = h[0].shape[0] * len(h), h[0].shape[1]
    hd = HEADS_DEV * HEAD_DIM

    def body(ins, outs, scratch):
        h, g, fixed, mask_ref, turned = ins
        out, e, (u_ref, dqkv_ref, att_ref, dg_ref) = outs
        qkv_ref, p_ref, st_ref = scratch
        forward_body(h, *fixed, mask_ref, out, u_ref, qkv_ref, p_ref, att_ref, st_ref)
        backward_body(g, h, fixed[0], *turned, qkv_ref, p_ref, st_ref, e, dqkv_ref, dg_ref)

    out, e, (u, dqkv, att, dgain) = call(
        "turn", body, [h, g, fixed, mask, turned],
        [
            stream(rows, width, 1),
            stream(rows, width, parts),
            [Mem((rows, width), BF16), Mem((rows, 3 * hd), BF16), Mem((rows, hd), BF16), Mem((8, width), F32)],
        ],
        [
            pltpu.VMEM((rows, 3 * hd), BF16),
            pltpu.VMEM((HEADS_DEV, rows, rows), F32),
            pltpu.VMEM((rows, 256), F32),
        ],
    )
    return out, e, (u, dqkv, att, g, dgain)


def backward_kernel(g, h, gain, turned, saved, parts):
    rows, width = saved[0].shape
    u, qkv, probs, att, stats = saved

    def body(ins, outs, scratch):
        g, h, gain_ref, turned, (qkv_ref, p_ref, st_ref) = ins
        e, dqkv_ref, dg_ref = outs
        backward_body(g, h, gain_ref, *turned, qkv_ref, p_ref, st_ref, e, dqkv_ref, dg_ref)

    e, dqkv, dgain = call(
        "backward", body, [g, h, gain, turned, [qkv, probs, stats]],
        [stream(rows, width, parts), Mem(qkv.shape, BF16), Mem((8, width), F32)],
    )
    return e, (u, dqkv, att, g, dgain)


def out_weights(uses, width, put):
    att = jnp.concatenate([use[2][...] for use in uses], axis=0)
    for n in range(0, width, 512):
        cols = pl.ds(n, 512)
        put(cols, dot(att, jnp.concatenate([whole(use[3], cols) for use in uses], axis=0), TN))


def in_weights(uses, width, put):
    dqkv = jnp.concatenate([use[1][...] for use in uses], axis=0)
    for m in range(0, width, 256):
        put(pl.ds(m, 256), dot(jnp.concatenate([use[0][:, m:m + 256] for use in uses], axis=0), dqkv, TN))


def gain_sum(uses):
    total = uses[0][4][...]
    for use in uses[1:]:
        total = total + use[4][...]
    return total


class Copies:
    def __init__(self, sems, odd):
        self.sems, self.odd, self.waits = sems, odd, []

    def push(self, source, target, other=None):
        sem = self.sems.at[len(self.waits)]
        copy = pltpu.make_async_copy(source, target, sem)
        if other is None:
            copy.start()
        else:
            by_place(self.odd, copy, pltpu.make_async_copy(source, other, sem))[0]()
        self.waits.append(copy.wait)

    def wait(self):
        for wait in self.waits:
            wait()


def early_weights(uses, out_a, out_b):
    rows, width = uses[0][0].shape
    hd = HEADS_DEV * HEAD_DIM

    def body(ins, outs, scratch):
        uses, (a_ref,), (b_ref,) = ins
        (down, up), gain_out, wo_out, wq_out = outs
        copies = Copies(scratch[0], is_odd())
        copies.push(a_ref, down.at[0], up.at[0])
        copies.push(b_ref, up.at[0], down.at[0])
        gain_out[...] = gain_sum(uses)

        def put_wo(cols, value):
            wo_out[:, cols] = value

        def put_wq(at, value):
            wq_out[at, :] = value

        out_weights(uses, width, put_wo)
        in_weights(uses, width, put_wq)
        copies.wait()

    outs, *sums = call(
        "early_weights", body, [list(uses), out_a, out_b],
        [[jax.ShapeDtypeStruct((1, rows, width), BF16)] * 2,
         Mem((8, width), F32), Mem((hd, width), F32), Mem((width, 3 * hd), F32)],
        [pltpu.SemaphoreType.DMA((2,))],
    )
    return outs, sums


def finish_kernel(g, h, gain, turned, saved, back_b, uses, sums):
    rows, width = saved[0].shape
    hd = HEADS_DEV * HEAD_DIM
    u, qkv, probs, att, stats = saved

    def body(ins, outs, scratch):
        g, h, gain_ref, (wqt_ref, wot_ref, wg_ref), (u_ref, qkv_ref, p_ref, att_ref, st_ref), (b_ref,), uses, sums = ins
        gain_total, wo_sum, wq_sum = sums
        (down, up), gain_hbm, wo_hbm, wq_hbm = outs
        e_ref, dqkv_ref, dg_ref, wo_buf, wq_buf, gain_buf, sems = scratch
        copies = Copies(sems, is_odd())
        copies.push(b_ref, up.at[0], down.at[0])
        uses = [*uses, (u_ref, dqkv_ref, att_ref, g, dg_ref)]

        def put_wo(cols, value):
            wo_buf[:, cols] = (wo_sum[:, cols] + value).astype(BF16)
            copies.push(wo_buf.at[:, cols], wo_hbm.at[0, :, cols])

        def put_wq(at, value):
            wq_buf[at, :] = (wq_sum[at, :] + value).astype(BF16)
            copies.push(wq_buf.at[at], wq_hbm.at[0, at])

        def done(cols):
            copies.push(e_ref.at[:, cols], down.at[0, :, cols], up.at[0, :, cols])

        attention_reverse(g, wot_ref, qkv_ref, p_ref, dqkv_ref)
        out_weights(uses, width, put_wo)
        in_weights(uses, width, put_wq)
        norm_reverse(g, h, gain_ref, wqt_ref, wg_ref, qkv_ref, st_ref, [e_ref], dqkv_ref, dg_ref, done)
        gain_buf[...] = jnp.sum(gain_total[...] + gain_sum(uses), axis=0, keepdims=True).astype(BF16)
        copies.push(gain_buf, gain_hbm)
        copies.wait()

    return call(
        "finish", body, [g, h, gain, turned, list(saved), back_b, list(uses), list(sums)],
        [
            [jax.ShapeDtypeStruct((1, rows, width), BF16)] * 2,
            jax.ShapeDtypeStruct((1, width), BF16),
            jax.ShapeDtypeStruct((1, hd, width), BF16),
            jax.ShapeDtypeStruct((1, width, 3 * hd), BF16),
        ],
        [
            pltpu.VMEM((rows, width), BF16),
            pltpu.VMEM(qkv.shape, BF16),
            pltpu.VMEM((8, width), F32),
            pltpu.VMEM((hd, width), BF16),
            pltpu.VMEM((width, 3 * hd), BF16),
            pltpu.VMEM((1, width), BF16),
            pltpu.SemaphoreType.DMA((2 + width // 512 * 2 + width // 256,)),
        ],
    )


def shards(acts_down, acts_up, cotangent_down, cotangent_up, ln_gain, w_qkv, w_out, band_offsets):
    sections = lax.axis_size("section")
    near = [(i, i ^ 1) for i in range(sections)]
    far = [(i, (i + (1 if i % 2 else -1)) % sections) for i in range(sections)]

    def swap_near(x):
        return [lax.ppermute(part, "section", near) for part in x]

    def swap_far(x):
        return [lax.ppermute(part, "section", far) for part in x]

    def after(x, other):
        return lax.optimization_barrier((x, other))[0]

    a0, b0, gain, wq, wo, mask, a1_out, a0_saved = first_kernel(
        band_offsets.T, ln_gain, w_qkv, w_out, acts_down, acts_up, 1)
    fixed = [gain, wq, wo]
    a1 = swap_far(a1_out)
    b1_out, b0_saved = forward_kernel(after(b0, a0_saved[4]), fixed, mask, NEAR_PARTS)
    b1 = swap_near(b1_out)
    b2_out, b1_saved = forward_kernel(after(b1, b0_saved[4]), fixed, mask, 1)
    b2 = swap_far(b2_out)
    *turned, cot_a, cot_b = prepare_kernel(gain, wq, wo, b1_saved[4], cotangent_down, cotangent_up)
    a2_out, a1_saved = forward_kernel(after(a1, turned[2]), fixed, mask, NEAR_PARTS, us=8)
    a2 = swap_near(a2_out)
    out_b, eb2, use_b2 = turn_kernel(after(b2, a1_saved[4]), cot_b, fixed, mask, turned, 1)
    cb1 = swap_far(eb2)
    out_a, ea2, use_a2 = turn_kernel(after(a2, use_b2[4]), cot_a, fixed, mask, turned, NEAR_PARTS)
    ca1 = swap_near(ea2)
    ea1, use_a1 = backward_kernel(after(ca1, use_a2[4]), a1, gain, turned, a1_saved, 1)
    ca0 = swap_far(ea1)
    eb1, use_b1 = backward_kernel(after(cb1, use_a1[4]), b1, gain, turned, b1_saved, NEAR_PARTS)
    cb0 = swap_near(eb1)
    (out_down, out_up), sums = early_weights([use_b2, use_a2, use_a1, after(use_b1, use_b1[4])], out_a, out_b)
    back_b, use_b0 = backward_kernel(after(cb0, sums[0]), b0, gain, turned, b0_saved, 1)
    (back_down, back_up), d_gain, d_wo, d_wq = finish_kernel(
        after(ca0, use_b0[4]), a0, gain, turned, a0_saved, back_b, [use_b0], sums)
    return out_down, out_up, back_down, back_up, d_gain, d_wq, d_wo


def solution(mesh):
    both = ("groups", "section")
    in_specs = (
        P(both, None, None), P(both, None, None), P(both, None, None), P(both, None, None),
        P("section", None), P("section", None, None), P("section", None, None), P(),
    )
    out_specs = (
        P(both, None, None), P(both, None, None), P(both, None, None), P(both, None, None),
        P(both, None), P(both, None, None), P(both, None, None),
    )
    return jax.shard_map(shards, mesh=mesh, in_specs=in_specs, out_specs=out_specs, check_vma=False)
```

```python
import math

import jax
import jax.numpy as jnp
from jax import lax
from jax.experimental import pallas as pl
from jax.experimental.pallas import tpu as pltpu
from jax.sharding import PartitionSpec as P

HEADS_DEV = 2
HEAD_DIM = 128
BLOCK = 32
CHUNK = 16
F32 = jnp.float32
BF16 = jnp.bfloat16
NT = (((1,), (1,)), ((), ()))
TN = (((0,), (0,)), ((), ()))
SCALE = 1.0 / math.sqrt(HEAD_DIM)
VM = pl.BlockSpec(memory_space=pltpu.VMEM)
NEAR_PARTS = 2
FAR_SHARES = (3, 5)


def dot(a, b, dims=(((1,), (0,)), ((), ()))):
    return lax.dot_general(a, b, dims, preferred_element_type=F32)


def mask_body(odd, offs_ref, rows):
    row = lax.broadcasted_iota(jnp.int32, (rows, rows), 0)
    col = lax.broadcasted_iota(jnp.int32, (rows, rows), 1)
    row_block = row // BLOCK
    col_block = col // BLOCK
    near = row_block == col_block
    for block in range(offs_ref.shape[1]):
        for listed in range(offs_ref.shape[0]):
            near = near | ((row_block == block) & (col_block == block - offs_ref[listed, block]))
    keep = (col <= row) & (near | jnp.logical_not(odd))
    return jnp.where(keep, 1.0, 0.0).astype(F32)


def held(refs, at):
    for ref in refs:
        if at < ref.shape[0]:
            return ref, at
        at -= ref.shape[0]


def read(refs, at, size, cols=slice(None)):
    ref, at = held(refs, at)
    return ref[pl.ds(at, size), cols]


def write(refs, at, size, value, cols=slice(None)):
    ref, at = held(refs, at)
    ref[pl.ds(at, size), cols] = value


def pieces(*arrays):
    cuts = {0}
    for refs in arrays:
        at = 0
        for ref in refs:
            at += ref.shape[0]
            cuts.add(at)
    cuts = sorted(cuts)
    return list(zip(cuts[:-1], cuts[1:]))


def whole(refs, cols=slice(None)):
    return jnp.concatenate([ref[:, cols] for ref in refs], axis=0)


def forward_body(h, gain_ref, wq_ref, wo_ref, mask_ref, out, u_ref, qkv_ref, p_ref, att_ref, st_ref, waits=None):
    rows, width = u_ref.shape
    hd = HEADS_DEV * HEAD_DIM
    gain = gain_ref[...].astype(F32)
    for start in range(0, rows, CHUNK):
        part = pl.ds(start, CHUNK)
        x = read(h, start, CHUNK).astype(F32)
        mean = jnp.sum(x, axis=-1, keepdims=True) * (1.0 / width)
        centred = x - mean
        rstd = lax.rsqrt(jnp.sum(centred * centred, axis=-1, keepdims=True) * (1.0 / width) + 1e-05)
        u_ref[part, :] = (centred * rstd * gain).astype(BF16)
        st_ref[part, :] = jnp.concatenate(
            [jnp.broadcast_to(mean, (CHUNK, 128)), jnp.broadcast_to(rstd, (CHUNK, 128))], axis=1)
    for n in range(3):
        if waits:
            waits[n].wait()
        qkv_ref[:, n * hd:(n + 1) * hd] = dot(u_ref[...], wq_ref[:, n * hd:(n + 1) * hd]).astype(BF16)
    keep = mask_ref[...]
    heads = [pl.ds(head * HEAD_DIM, HEAD_DIM) for head in range(HEADS_DEV)]
    scores = [dot(qkv_ref[:, cols], qkv_ref[:, pl.ds(hd + cols.start, HEAD_DIM)], NT) for cols in heads]
    weighted = [jnp.where(keep > 0.0, jnp.exp(score * SCALE), 0.0) for score in scores]
    mixed = [
        dot(value.astype(BF16), qkv_ref[:, pl.ds(2 * hd + cols.start, HEAD_DIM)]) for value, cols in zip(weighted, heads)
    ]
    inverse = [1.0 / jnp.sum(value, axis=-1, keepdims=True) for value in weighted]
    for head, cols in enumerate(heads):
        att_ref[:, cols] = (mixed[head] * inverse[head]).astype(BF16)
        p_ref[head] = weighted[head] * inverse[head]
    if waits:
        waits[3].wait()
    for n in range(0, width, 512):
        cols = pl.ds(n, 512)
        value = dot(att_ref[...], wo_ref[:, cols])
        for at, end in pieces(out, h):
            size = end - at
            write(out, at, size, (read(h, at, size, cols).astype(F32) + value[at:end]).astype(BF16), cols)


def attention_reverse(g, wot_ref, qkv_ref, p_ref, dqkv_ref):
    hd = HEADS_DEV * HEAD_DIM
    datt = dot(whole(g), wot_ref[...]).astype(BF16)
    heads = [pl.ds(head * HEAD_DIM, HEAD_DIM) for head in range(HEADS_DEV)]
    keys = [pl.ds(hd + cols.start, HEAD_DIM) for cols in heads]
    values = [pl.ds(2 * hd + cols.start, HEAD_DIM) for cols in heads]
    das = [datt[:, cols.start:cols.start + HEAD_DIM] for cols in heads]
    probs = [p_ref[head] for head in range(HEADS_DEV)]
    dps = [dot(da, qkv_ref[:, cols], NT).astype(BF16).astype(F32) for da, cols in zip(das, values)]
    dvs = [dot(prob.astype(BF16), da, TN) for prob, da in zip(probs, das)]
    totals = [jnp.sum(dp * prob, axis=-1, keepdims=True) for dp, prob in zip(dps, probs)]
    dss = [(prob * (dp - total) * SCALE).astype(BF16) for prob, dp, total in zip(probs, dps, totals)]
    dqs = [dot(ds, qkv_ref[:, cols]) for ds, cols in zip(dss, keys)]
    dks = [dot(ds, qkv_ref[:, cols], TN) for ds, cols in zip(dss, heads)]
    for head in range(HEADS_DEV):
        dqkv_ref[:, values[head]] = dvs[head].astype(BF16)
        dqkv_ref[:, heads[head]] = dqs[head].astype(BF16)
        dqkv_ref[:, keys[head]] = dks[head].astype(BF16)


def lanes(column):
    return jnp.broadcast_to(column, (column.shape[0], 128))


def norm_reverse(g, h, gain_ref, wqt_ref, wg_ref, qkv_ref, st_ref, e, dqkv_ref, dg_ref, done=None):
    rows, width = dqkv_ref.shape[0], wqt_ref.shape[1]
    dqkv32 = dqkv_ref[...].astype(F32)
    first = jnp.sum(dqkv32 * wg_ref[...], axis=-1, keepdims=True) * (1.0 / width)
    second = jnp.sum(dqkv32 * qkv_ref[...].astype(F32), axis=-1, keepdims=True) * (1.0 / width)
    mean, rstd = st_ref[:, 0:128], st_ref[:, 128:256]
    first, second = lanes(first) * rstd, lanes(second) * rstd
    for block in range(0, width, 512):
        wide = dot(dqkv_ref[...], wqt_ref[:, block:block + 512])
        for n in range(0, 512, 128):
            cols = pl.ds(block + n, 128)
            du = wide[:, n:n + 128]
            xhat = (whole(h, cols).astype(F32) - mean) * rstd
            dg_ref[:, cols] = jnp.sum((du * xhat).reshape(rows // 8, 8, 128), axis=0)
            gain = gain_ref[:, cols].astype(F32)
            value = (du * gain) * rstd - first - xhat * second + whole(g, cols).astype(F32)
            for at, end in pieces(e):
                write(e, at, end - at, value[at:end].astype(BF16), cols)
        if done:
            done(pl.ds(block, 512))


def backward_body(g, h, gain_ref, wqt_ref, wot_ref, wg_ref, qkv_ref, p_ref, st_ref, e, dqkv_ref, dg_ref):
    attention_reverse(g, wot_ref, qkv_ref, p_ref, dqkv_ref)
    norm_reverse(g, h, gain_ref, wqt_ref, wg_ref, qkv_ref, st_ref, e, dqkv_ref, dg_ref)


def params(mib):
    return pltpu.CompilerParams(vmem_limit_bytes=mib << 20)


def cost(us):
    return pl.CostEstimate(flops=int(us * 1e9), bytes_accessed=int(us * 1e5), transcendentals=0)


def by_place(odd, when_odd, when_even):
    def start():
        pl.when(odd)(when_odd.start)
        pl.when(jnp.logical_not(odd))(when_even.start)

    return start, when_odd.wait


def is_odd():
    return lax.axis_index("section") % 2 == 1


def call(name, body, operands, outs, scratch=(), hbm=(), alias=(), us=0.002, mib=24):
    flat_in, tree_in = jax.tree.flatten(operands, is_leaf=lambda x: isinstance(x, Far))
    flat_out, tree_out = jax.tree.flatten(outs, is_leaf=lambda x: isinstance(x, (jax.ShapeDtypeStruct, Mem)))

    def kernel(*refs):
        a, b = len(flat_in), len(flat_in) + len(flat_out)
        body(jax.tree.unflatten(tree_in, refs[:a]), jax.tree.unflatten(tree_out, refs[a:b]), refs[b:])

    far = pl.BlockSpec(memory_space=pltpu.HBM)
    result = pl.pallas_call(
        kernel,
        in_specs=[far if isinstance(x, Far) else VM for x in flat_in],
        out_specs=[far if isinstance(x, jax.ShapeDtypeStruct) else VM for x in flat_out],
        out_shape=[x if isinstance(x, jax.ShapeDtypeStruct) else pltpu.VMEM(x.shape, x.dtype) for x in flat_out],
        scratch_shapes=list(scratch),
        input_output_aliases=dict(alias),
        compiler_params=params(mib),
        cost_estimate=cost(us),
        name=name,
    )(*[x.array if isinstance(x, Far) else x for x in flat_in])
    return jax.tree.unflatten(tree_out, result)


class Far:
    def __init__(self, array):
        self.array = pltpu.with_memory_space_constraint(array, pltpu.HBM)


class Mem:
    def __init__(self, shape, dtype):
        self.shape, self.dtype = shape, dtype


def stream(rows, width, parts=1):
    shares = parts if isinstance(parts, tuple) else (1,) * parts
    return [Mem((rows * share // sum(shares), width), BF16) for share in shares]


def saved_outs(rows, width):
    hd = HEADS_DEV * HEAD_DIM
    return [
        Mem((rows, width), BF16),
        Mem((rows, 3 * hd), BF16),
        Mem((HEADS_DEV, rows, rows), F32),
        Mem((rows, hd), BF16),
        Mem((rows, 256), F32),
    ]


def first_kernel(offs, gain, wq, wo, down, up, parts):
    _, rows, width = down.shape
    hd = HEADS_DEV * HEAD_DIM

    def body(ins, outs, scratch):
        offs_hbm, gain_hbm, wq_hbm, wo_hbm, down_hbm, up_hbm = ins
        (a_ref,), (b_ref,), gain_ref, wq_ref, wo_ref, mask_ref, out, saved = outs
        offs_ref, sems = scratch
        odd = is_odd()

        def pick(source, target, sem):
            return pltpu.make_async_copy(source, target, sems.at[sem])

        a_start, a_wait = by_place(odd, pick(down_hbm.at[0], a_ref, 0), pick(up_hbm.at[0], a_ref, 0))
        b_start, b_wait = by_place(odd, pick(up_hbm.at[0], b_ref, 1), pick(down_hbm.at[0], b_ref, 1))
        offs_copy = pick(offs_hbm, offs_ref, 2)
        gain_copy = pick(gain_hbm, gain_ref, 3)
        wo_copy = pick(wo_hbm.at[0], wo_ref, 4)
        cols = [pl.ds(n * hd, hd) for n in range(3)]
        wq_copies = [pick(wq_hbm.at[0, :, cols[n]], wq_ref.at[:, cols[n]], 5 + n) for n in range(3)]
        a_start()
        gain_copy.start()
        offs_copy.start()
        for copy in wq_copies:
            copy.start()
        wo_copy.start()
        b_start()
        offs_copy.wait()
        mask_ref[...] = mask_body(odd, offs_ref, rows)
        a_wait()
        gain_copy.wait()
        forward_body([a_ref], gain_ref, wq_ref, wo_ref, mask_ref, out, *saved, waits=wq_copies + [wo_copy])
        b_wait()

    return call(
        "first", body, [Far(x) for x in (offs, gain, wq, wo, down, up)],
        [
            stream(rows, width, 1), stream(rows, width, 1), Mem(gain.shape, BF16), Mem(wq.shape[1:], BF16),
            Mem(wo.shape[1:], BF16), Mem((rows, rows), F32), stream(rows, width, parts), saved_outs(rows, width),
        ],
        [pltpu.SMEM(offs.shape, jnp.int32), pltpu.SemaphoreType.DMA((8,))],
    )


def forward_kernel(h, fixed, mask, parts, us=0.002):
    rows, width = sum(x.shape[0] for x in h), h[0].shape[1]

    def body(ins, outs, scratch):
        h, fixed, mask_ref = ins
        out, saved = outs
        forward_body(h, *fixed, mask_ref, out, *saved)

    return call("forward", body, [h, fixed, mask], [stream(rows, width, parts), saved_outs(rows, width)], us=us)


def prepare_kernel(gain, wq, wo, tie, down, up):
    _, rows, width = down.shape
    hd = HEADS_DEV * HEAD_DIM

    def body(ins, outs, scratch):
        gain_ref, wq_ref, wo_ref, _, down_hbm, up_hbm = ins
        wqt_ref, wot_ref, wg_ref, (a_ref,), (b_ref,) = outs
        (sems,) = scratch
        odd = is_odd()

        def pick(source, target, sem):
            return pltpu.make_async_copy(source.at[0], target, sems.at[sem])

        a_start, a_wait = by_place(odd, pick(down_hbm, a_ref, 0), pick(up_hbm, a_ref, 0))
        b_start, b_wait = by_place(odd, pick(up_hbm, b_ref, 1), pick(down_hbm, b_ref, 1))
        a_start()
        b_start()
        for at in range(0, width, 256):
            wqt_ref[:, at:at + 256] = wq_ref[at:at + 256, :].T
            wot_ref[at:at + 256, :] = wo_ref[:, at:at + 256].T
        wg_ref[...] = dot(gain_ref[...], wq_ref[...])
        a_wait()
        b_wait()

    return call(
        "prepare", body, [gain, wq, wo, tie, Far(down), Far(up)],
        [Mem((3 * hd, width), BF16), Mem((width, hd), BF16), Mem((1, 3 * hd), F32),
         stream(rows, width, 1), stream(rows, width, 1)],
        [pltpu.SemaphoreType.DMA((2,))],
    )


def turn_kernel(h, g, fixed, mask, turned, parts):
    rows, width = sum(x.shape[0] for x in h), h[0].shape[1]
    hd = HEADS_DEV * HEAD_DIM

    def body(ins, outs, scratch):
        h, g, fixed, mask_ref, turned = ins
        out, e, (u_ref, dqkv_ref, att_ref, dg_ref) = outs
        qkv_ref, p_ref, st_ref = scratch
        forward_body(h, *fixed, mask_ref, out, u_ref, qkv_ref, p_ref, att_ref, st_ref)
        backward_body(g, h, fixed[0], *turned, qkv_ref, p_ref, st_ref, e, dqkv_ref, dg_ref)

    out, e, (u, dqkv, att, dgain) = call(
        "turn", body, [h, g, fixed, mask, turned],
        [
            stream(rows, width, 1),
            stream(rows, width, parts),
            [Mem((rows, width), BF16), Mem((rows, 3 * hd), BF16), Mem((rows, hd), BF16), Mem((8, width), F32)],
        ],
        [
            pltpu.VMEM((rows, 3 * hd), BF16),
            pltpu.VMEM((HEADS_DEV, rows, rows), F32),
            pltpu.VMEM((rows, 256), F32),
        ],
    )
    return out, e, (u, dqkv, att, g, dgain)


def backward_kernel(g, h, gain, turned, saved, parts):
    rows, width = saved[0].shape
    u, qkv, probs, att, stats = saved

    def body(ins, outs, scratch):
        g, h, gain_ref, turned, (qkv_ref, p_ref, st_ref) = ins
        e, dqkv_ref, dg_ref = outs
        backward_body(g, h, gain_ref, *turned, qkv_ref, p_ref, st_ref, e, dqkv_ref, dg_ref)

    e, dqkv, dgain = call(
        "backward", body, [g, h, gain, turned, [qkv, probs, stats]],
        [stream(rows, width, parts), Mem(qkv.shape, BF16), Mem((8, width), F32)],
    )
    return e, (u, dqkv, att, g, dgain)


def out_weights(uses, width, put):
    att = jnp.concatenate([use[2][...] for use in uses], axis=0)
    for n in range(0, width, 512):
        cols = pl.ds(n, 512)
        put(cols, dot(att, jnp.concatenate([whole(use[3], cols) for use in uses], axis=0), TN))


def in_weights(uses, width, put):
    dqkv = jnp.concatenate([use[1][...] for use in uses], axis=0)
    for m in range(0, width, 256):
        put(pl.ds(m, 256), dot(jnp.concatenate([use[0][:, m:m + 256] for use in uses], axis=0), dqkv, TN))


def gain_sum(uses):
    total = uses[0][4][...]
    for use in uses[1:]:
        total = total + use[4][...]
    return total


class Copies:
    def __init__(self, sems, odd):
        self.sems, self.odd, self.waits = sems, odd, []

    def push(self, source, target, other=None):
        sem = self.sems.at[len(self.waits)]
        copy = pltpu.make_async_copy(source, target, sem)
        if other is None:
            copy.start()
        else:
            by_place(self.odd, copy, pltpu.make_async_copy(source, other, sem))[0]()
        self.waits.append(copy.wait)

    def wait(self):
        for wait in self.waits:
            wait()


def early_weights(uses, out_a, out_b, us):
    rows, width = uses[0][0].shape
    hd = HEADS_DEV * HEAD_DIM

    def body(ins, outs, scratch):
        uses, (a_ref,), (b_ref,) = ins
        (down, up), gain_out, wo_out, wq_out = outs
        copies = Copies(scratch[0], is_odd())
        copies.push(a_ref, down.at[0], up.at[0])
        copies.push(b_ref, up.at[0], down.at[0])
        gain_out[...] = gain_sum(uses)

        def put_wo(cols, value):
            wo_out[:, cols] = value

        def put_wq(at, value):
            wq_out[at, :] = value

        out_weights(uses, width, put_wo)
        in_weights(uses, width, put_wq)
        copies.wait()

    outs, *sums = call(
        "early_weights", body, [list(uses), out_a, out_b],
        [[jax.ShapeDtypeStruct((1, rows, width), BF16)] * 2,
         Mem((8, width), F32), Mem((hd, width), F32), Mem((width, 3 * hd), F32)],
        [pltpu.SemaphoreType.DMA((2,))], us=us,
    )
    return outs, sums


def more_weights(uses, sums):
    width = uses[0][0].shape[1]

    def body(ins, outs, scratch):
        uses, (gain_in, wo_in, wq_in) = ins
        gain_out, wo_out, wq_out = outs
        gain_out[...] = gain_in[...] + gain_sum(uses)

        def put_wo(cols, value):
            wo_out[:, cols] = wo_in[:, cols] + value

        def put_wq(at, value):
            wq_out[at, :] = wq_in[at, :] + value

        out_weights(uses, width, put_wo)
        in_weights(uses, width, put_wq)

    return call("more_weights", body, [list(uses), list(sums)], [Mem(x.shape, F32) for x in sums])


def finish_kernel(g, h, gain, turned, saved, back_b, uses, sums):
    rows, width = saved[0].shape
    hd = HEADS_DEV * HEAD_DIM
    u, qkv, probs, att, stats = saved

    def body(ins, outs, scratch):
        g, h, gain_ref, (wqt_ref, wot_ref, wg_ref), (u_ref, qkv_ref, p_ref, att_ref, st_ref), (b_ref,), uses, sums = ins
        gain_total, wo_sum, wq_sum = sums
        (down, up), gain_hbm, wo_hbm, wq_hbm = outs
        e_ref, dqkv_ref, dg_ref, wo_buf, wq_buf, gain_buf, sems = scratch
        copies = Copies(sems, is_odd())
        copies.push(b_ref, up.at[0], down.at[0])
        uses = [*uses, (u_ref, dqkv_ref, att_ref, g, dg_ref)]

        def put_wo(cols, value):
            wo_buf[:, cols] = (wo_sum[:, cols] + value).astype(BF16)
            copies.push(wo_buf.at[:, cols], wo_hbm.at[0, :, cols])

        def put_wq(at, value):
            wq_buf[at, :] = (wq_sum[at, :] + value).astype(BF16)
            copies.push(wq_buf.at[at], wq_hbm.at[0, at])

        def done(cols):
            copies.push(e_ref.at[:, cols], down.at[0, :, cols], up.at[0, :, cols])

        attention_reverse(g, wot_ref, qkv_ref, p_ref, dqkv_ref)
        out_weights(uses, width, put_wo)
        in_weights(uses, width, put_wq)
        norm_reverse(g, h, gain_ref, wqt_ref, wg_ref, qkv_ref, st_ref, [e_ref], dqkv_ref, dg_ref, done)
        gain_buf[...] = jnp.sum(gain_total[...] + gain_sum(uses), axis=0, keepdims=True).astype(BF16)
        copies.push(gain_buf, gain_hbm)
        copies.wait()

    return call(
        "finish", body, [g, h, gain, turned, list(saved), back_b, list(uses), list(sums)],
        [
            [jax.ShapeDtypeStruct((1, rows, width), BF16)] * 2,
            jax.ShapeDtypeStruct((1, width), BF16),
            jax.ShapeDtypeStruct((1, hd, width), BF16),
            jax.ShapeDtypeStruct((1, width, 3 * hd), BF16),
        ],
        [
            pltpu.VMEM((rows, width), BF16),
            pltpu.VMEM(qkv.shape, BF16),
            pltpu.VMEM((8, width), F32),
            pltpu.VMEM((hd, width), BF16),
            pltpu.VMEM((width, 3 * hd), BF16),
            pltpu.VMEM((1, width), BF16),
            pltpu.SemaphoreType.DMA((2 + width // 512 * 2 + width // 256,)),
        ],
    )


def shards(acts_down, acts_up, cotangent_down, cotangent_up, ln_gain, w_qkv, w_out, band_offsets):
    sections = lax.axis_size("section")
    near = [(i, i ^ 1) for i in range(sections)]
    far = [(i, (i + (1 if i % 2 else -1)) % sections) for i in range(sections)]

    def swap_near(x):
        return [lax.ppermute(part, "section", near) for part in x]

    def swap_far(x):
        return [lax.ppermute(part, "section", far) for part in x]

    def after(x, other):
        return lax.optimization_barrier((x, other))[0]

    a0, b0, gain, wq, wo, mask, a1_out, a0_saved = first_kernel(
        band_offsets.T, ln_gain, w_qkv, w_out, acts_down, acts_up, 1)
    fixed = [gain, wq, wo]
    a1 = swap_far(a1_out)
    b1_out, b0_saved = forward_kernel(after(b0, a0_saved[4]), fixed, mask, NEAR_PARTS)
    b1 = swap_near(b1_out)
    b2_out, b1_saved = forward_kernel(after(b1, b0_saved[4]), fixed, mask, 1)
    *turned, cot_a, cot_b = prepare_kernel(gain, wq, wo, b1_saved[4], cotangent_down, cotangent_up)
    b2 = swap_far(after(b2_out, turned[2]))
    a2_out, a1_saved = forward_kernel(after(a1, turned[2]), fixed, mask, NEAR_PARTS)
    a2 = swap_near(a2_out)
    out_a, ea2, use_a2 = turn_kernel(after(a2, a1_saved[4]), cot_a, fixed, mask, turned, NEAR_PARTS)
    ca1 = swap_near(ea2)
    (ea1_fore, ea1_rest), use_a1 = backward_kernel(after(ca1, use_a2[4]), a1, gain, turned, a1_saved, FAR_SHARES)
    (ca0_fore,) = swap_far([ea1_fore])
    out_b, eb2, use_b2 = turn_kernel(after(b2, use_a1[4]), cot_b, fixed, mask, turned, 2)
    cb1 = swap_far(eb2)
    use_b2, ca0_fore = lax.optimization_barrier((use_b2, ca0_fore))
    (out_down, out_up), sums = early_weights([use_b2, use_a2, use_a1], out_a, out_b, us=8)
    cb1_fore, ea1_rest, sums = lax.optimization_barrier((cb1[0], ea1_rest, sums))
    (ca0_rest,) = swap_far([ea1_rest])
    eb1, use_b1 = backward_kernel([cb1_fore, cb1[1]], b1, gain, turned, b1_saved, NEAR_PARTS)
    cb0 = swap_near(eb1)
    sums = more_weights([after(use_b1, use_b1[4])], sums)
    back_b, use_b0 = backward_kernel(after(cb0, sums[0]), b0, gain, turned, b0_saved, 1)
    ca0 = [ca0_fore, ca0_rest]
    (back_down, back_up), d_gain, d_wo, d_wq = finish_kernel(
        after(ca0, use_b0[4]), a0, gain, turned, a0_saved, back_b, [use_b0], sums)
    return out_down, out_up, back_down, back_up, d_gain, d_wq, d_wo


def solution(mesh):
    both = ("groups", "section")
    in_specs = (
        P(both, None, None), P(both, None, None), P(both, None, None), P(both, None, None),
        P("section", None), P("section", None, None), P("section", None, None), P(),
    )
    out_specs = (
        P(both, None, None), P(both, None, None), P(both, None, None), P(both, None, None),
        P(both, None), P(both, None, None), P(both, None, None),
    )
    return jax.shard_map(shards, mesh=mesh, in_specs=in_specs, out_specs=out_specs, check_vma=False)
```

```python
import math

import jax
import jax.numpy as jnp
from jax import lax
from jax.experimental import pallas as pl
from jax.experimental.pallas import tpu as pltpu
from jax.sharding import PartitionSpec as P

HEADS_DEV = 2
HEAD_DIM = 128
BLOCK = 32
CHUNK = 16
F32 = jnp.float32
BF16 = jnp.bfloat16
NT = (((1,), (1,)), ((), ()))
TN = (((0,), (0,)), ((), ()))
SCALE = 1.0 / math.sqrt(HEAD_DIM)
VM = pl.BlockSpec(memory_space=pltpu.VMEM)
NEAR_PARTS = 2
NEAR_SMALL = 4
FAR_SHARES = (3, 5)


def dot(a, b, dims=(((1,), (0,)), ((), ()))):
    return lax.dot_general(a, b, dims, preferred_element_type=F32)


def mask_body(odd, offs_ref, rows):
    row = lax.broadcasted_iota(jnp.int32, (rows, rows), 0)
    col = lax.broadcasted_iota(jnp.int32, (rows, rows), 1)
    row_block = row // BLOCK
    col_block = col // BLOCK
    near = row_block == col_block
    for block in range(offs_ref.shape[1]):
        for listed in range(offs_ref.shape[0]):
            near = near | ((row_block == block) & (col_block == block - offs_ref[listed, block]))
    keep = (col <= row) & (near | jnp.logical_not(odd))
    return jnp.where(keep, 1.0, 0.0).astype(F32)


def held(refs, at):
    for ref in refs:
        if at < ref.shape[0]:
            return ref, at
        at -= ref.shape[0]


def read(refs, at, size, cols=slice(None)):
    ref, at = held(refs, at)
    return ref[pl.ds(at, size), cols]


def write(refs, at, size, value, cols=slice(None)):
    ref, at = held(refs, at)
    ref[pl.ds(at, size), cols] = value


def pieces(*arrays):
    cuts = {0}
    for refs in arrays:
        at = 0
        for ref in refs:
            at += ref.shape[0]
            cuts.add(at)
    cuts = sorted(cuts)
    return list(zip(cuts[:-1], cuts[1:]))


def whole(refs, cols=slice(None)):
    return jnp.concatenate([ref[:, cols] for ref in refs], axis=0)


def forward_body(h, gain_ref, wq_ref, wo_ref, mask_ref, out, u_ref, qkv_ref, p_ref, att_ref, st_ref, waits=None):
    rows, width = u_ref.shape
    hd = HEADS_DEV * HEAD_DIM
    gain = gain_ref[...].astype(F32)
    for start in range(0, rows, CHUNK):
        part = pl.ds(start, CHUNK)
        x = read(h, start, CHUNK).astype(F32)
        mean = jnp.sum(x, axis=-1, keepdims=True) * (1.0 / width)
        centred = x - mean
        rstd = lax.rsqrt(jnp.sum(centred * centred, axis=-1, keepdims=True) * (1.0 / width) + 1e-05)
        u_ref[part, :] = (centred * rstd * gain).astype(BF16)
        st_ref[part, :] = jnp.concatenate(
            [jnp.broadcast_to(mean, (CHUNK, 128)), jnp.broadcast_to(rstd, (CHUNK, 128))], axis=1)
    for n in range(3):
        if waits:
            waits[n].wait()
        qkv_ref[:, n * hd:(n + 1) * hd] = dot(u_ref[...], wq_ref[:, n * hd:(n + 1) * hd]).astype(BF16)
    keep = mask_ref[...]
    heads = [pl.ds(head * HEAD_DIM, HEAD_DIM) for head in range(HEADS_DEV)]
    scores = [dot(qkv_ref[:, cols], qkv_ref[:, pl.ds(hd + cols.start, HEAD_DIM)], NT) for cols in heads]
    weighted = [jnp.where(keep > 0.0, jnp.exp(score * SCALE), 0.0) for score in scores]
    mixed = [
        dot(value.astype(BF16), qkv_ref[:, pl.ds(2 * hd + cols.start, HEAD_DIM)]) for value, cols in zip(weighted, heads)
    ]
    inverse = [1.0 / jnp.sum(value, axis=-1, keepdims=True) for value in weighted]
    for head, cols in enumerate(heads):
        att_ref[:, cols] = (mixed[head] * inverse[head]).astype(BF16)
        p_ref[head] = weighted[head] * inverse[head]
    if waits:
        waits[3].wait()
    for n in range(0, width, 512):
        cols = pl.ds(n, 512)
        value = dot(att_ref[...], wo_ref[:, cols])
        for at, end in pieces(out, h):
            size = end - at
            write(out, at, size, (read(h, at, size, cols).astype(F32) + value[at:end]).astype(BF16), cols)


def attention_reverse(g, wot_ref, qkv_ref, p_ref, dqkv_ref):
    hd = HEADS_DEV * HEAD_DIM
    datt = dot(whole(g), wot_ref[...]).astype(BF16)
    heads = [pl.ds(head * HEAD_DIM, HEAD_DIM) for head in range(HEADS_DEV)]
    keys = [pl.ds(hd + cols.start, HEAD_DIM) for cols in heads]
    values = [pl.ds(2 * hd + cols.start, HEAD_DIM) for cols in heads]
    das = [datt[:, cols.start:cols.start + HEAD_DIM] for cols in heads]
    probs = [p_ref[head] for head in range(HEADS_DEV)]
    dps = [dot(da, qkv_ref[:, cols], NT).astype(BF16).astype(F32) for da, cols in zip(das, values)]
    dvs = [dot(prob.astype(BF16), da, TN) for prob, da in zip(probs, das)]
    totals = [jnp.sum(dp * prob, axis=-1, keepdims=True) for dp, prob in zip(dps, probs)]
    dss = [(prob * (dp - total) * SCALE).astype(BF16) for prob, dp, total in zip(probs, dps, totals)]
    dqs = [dot(ds, qkv_ref[:, cols]) for ds, cols in zip(dss, keys)]
    dks = [dot(ds, qkv_ref[:, cols], TN) for ds, cols in zip(dss, heads)]
    for head in range(HEADS_DEV):
        dqkv_ref[:, values[head]] = dvs[head].astype(BF16)
        dqkv_ref[:, heads[head]] = dqs[head].astype(BF16)
        dqkv_ref[:, keys[head]] = dks[head].astype(BF16)


def lanes(column):
    return jnp.broadcast_to(column, (column.shape[0], 128))


def norm_reverse(g, h, gain_ref, wqt_ref, wg_ref, qkv_ref, st_ref, e, dqkv_ref, dg_ref, done=None):
    rows, width = dqkv_ref.shape[0], wqt_ref.shape[1]
    dqkv32 = dqkv_ref[...].astype(F32)
    first = jnp.sum(dqkv32 * wg_ref[...], axis=-1, keepdims=True) * (1.0 / width)
    second = jnp.sum(dqkv32 * qkv_ref[...].astype(F32), axis=-1, keepdims=True) * (1.0 / width)
    mean, rstd = st_ref[:, 0:128], st_ref[:, 128:256]
    first, second = lanes(first) * rstd, lanes(second) * rstd
    for block in range(0, width, 512):
        wide = dot(dqkv_ref[...], wqt_ref[:, block:block + 512])
        for n in range(0, 512, 128):
            cols = pl.ds(block + n, 128)
            du = wide[:, n:n + 128]
            xhat = (whole(h, cols).astype(F32) - mean) * rstd
            dg_ref[:, cols] = jnp.sum((du * xhat).reshape(rows // 8, 8, 128), axis=0)
            gain = gain_ref[:, cols].astype(F32)
            value = (du * gain) * rstd - first - xhat * second + whole(g, cols).astype(F32)
            for at, end in pieces(e):
                write(e, at, end - at, value[at:end].astype(BF16), cols)
        if done:
            done(pl.ds(block, 512))


def backward_body(g, h, gain_ref, wqt_ref, wot_ref, wg_ref, qkv_ref, p_ref, st_ref, e, dqkv_ref, dg_ref):
    attention_reverse(g, wot_ref, qkv_ref, p_ref, dqkv_ref)
    norm_reverse(g, h, gain_ref, wqt_ref, wg_ref, qkv_ref, st_ref, e, dqkv_ref, dg_ref)


def params(mib):
    return pltpu.CompilerParams(vmem_limit_bytes=mib << 20)


def cost(us):
    return pl.CostEstimate(flops=int(us * 1e9), bytes_accessed=int(us * 1e5), transcendentals=0)


def by_place(odd, when_odd, when_even):
    def start():
        pl.when(odd)(when_odd.start)
        pl.when(jnp.logical_not(odd))(when_even.start)

    return start, when_odd.wait


def is_odd():
    return lax.axis_index("section") % 2 == 1


def call(name, body, operands, outs, scratch=(), hbm=(), alias=(), us=0.002, mib=24):
    flat_in, tree_in = jax.tree.flatten(operands, is_leaf=lambda x: isinstance(x, Far))
    flat_out, tree_out = jax.tree.flatten(outs, is_leaf=lambda x: isinstance(x, (jax.ShapeDtypeStruct, Mem)))

    def kernel(*refs):
        a, b = len(flat_in), len(flat_in) + len(flat_out)
        body(jax.tree.unflatten(tree_in, refs[:a]), jax.tree.unflatten(tree_out, refs[a:b]), refs[b:])

    far = pl.BlockSpec(memory_space=pltpu.HBM)
    result = pl.pallas_call(
        kernel,
        in_specs=[far if isinstance(x, Far) else VM for x in flat_in],
        out_specs=[far if isinstance(x, jax.ShapeDtypeStruct) else VM for x in flat_out],
        out_shape=[x if isinstance(x, jax.ShapeDtypeStruct) else pltpu.VMEM(x.shape, x.dtype) for x in flat_out],
        scratch_shapes=list(scratch),
        input_output_aliases=dict(alias),
        compiler_params=params(mib),
        cost_estimate=cost(us),
        name=name,
    )(*[x.array if isinstance(x, Far) else x for x in flat_in])
    return jax.tree.unflatten(tree_out, result)


class Far:
    def __init__(self, array):
        self.array = pltpu.with_memory_space_constraint(array, pltpu.HBM)


class Mem:
    def __init__(self, shape, dtype):
        self.shape, self.dtype = shape, dtype


def stream(rows, width, parts=1):
    shares = parts if isinstance(parts, tuple) else (1,) * parts
    return [Mem((rows * share // sum(shares), width), BF16) for share in shares]


def saved_outs(rows, width):
    hd = HEADS_DEV * HEAD_DIM
    return [
        Mem((rows, width), BF16),
        Mem((rows, 3 * hd), BF16),
        Mem((HEADS_DEV, rows, rows), F32),
        Mem((rows, hd), BF16),
        Mem((rows, 256), F32),
    ]


def first_kernel(offs, gain, wq, wo, down, up, parts):
    _, rows, width = down.shape
    hd = HEADS_DEV * HEAD_DIM

    def body(ins, outs, scratch):
        offs_hbm, gain_hbm, wq_hbm, wo_hbm, down_hbm, up_hbm = ins
        (a_ref,), (b_ref,), gain_ref, wq_ref, wo_ref, mask_ref, out, saved = outs
        offs_ref, sems = scratch
        odd = is_odd()

        def pick(source, target, sem):
            return pltpu.make_async_copy(source, target, sems.at[sem])

        a_start, a_wait = by_place(odd, pick(down_hbm.at[0], a_ref, 0), pick(up_hbm.at[0], a_ref, 0))
        b_start, b_wait = by_place(odd, pick(up_hbm.at[0], b_ref, 1), pick(down_hbm.at[0], b_ref, 1))
        offs_copy = pick(offs_hbm, offs_ref, 2)
        gain_copy = pick(gain_hbm, gain_ref, 3)
        wo_copy = pick(wo_hbm.at[0], wo_ref, 4)
        cols = [pl.ds(n * hd, hd) for n in range(3)]
        wq_copies = [pick(wq_hbm.at[0, :, cols[n]], wq_ref.at[:, cols[n]], 5 + n) for n in range(3)]
        a_start()
        gain_copy.start()
        offs_copy.start()
        for copy in wq_copies:
            copy.start()
        wo_copy.start()
        b_start()
        offs_copy.wait()
        mask_ref[...] = mask_body(odd, offs_ref, rows)
        a_wait()
        gain_copy.wait()
        forward_body([a_ref], gain_ref, wq_ref, wo_ref, mask_ref, out, *saved, waits=wq_copies + [wo_copy])
        b_wait()

    return call(
        "first", body, [Far(x) for x in (offs, gain, wq, wo, down, up)],
        [
            stream(rows, width, 1), stream(rows, width, 1), Mem(gain.shape, BF16), Mem(wq.shape[1:], BF16),
            Mem(wo.shape[1:], BF16), Mem((rows, rows), F32), stream(rows, width, parts), saved_outs(rows, width),
        ],
        [pltpu.SMEM(offs.shape, jnp.int32), pltpu.SemaphoreType.DMA((8,))],
    )


def forward_kernel(h, fixed, mask, parts, us=0.002):
    rows, width = sum(x.shape[0] for x in h), h[0].shape[1]

    def body(ins, outs, scratch):
        h, fixed, mask_ref = ins
        out, saved = outs
        forward_body(h, *fixed, mask_ref, out, *saved)

    return call("forward", body, [h, fixed, mask], [stream(rows, width, parts), saved_outs(rows, width)], us=us)


def prepare_kernel(gain, wq, wo, tie, down, up):
    _, rows, width = down.shape
    hd = HEADS_DEV * HEAD_DIM

    def body(ins, outs, scratch):
        gain_ref, wq_ref, wo_ref, _, down_hbm, up_hbm = ins
        wqt_ref, wot_ref, wg_ref, (a_ref,), (b_ref,) = outs
        (sems,) = scratch
        odd = is_odd()

        def pick(source, target, sem):
            return pltpu.make_async_copy(source.at[0], target, sems.at[sem])

        a_start, a_wait = by_place(odd, pick(down_hbm, a_ref, 0), pick(up_hbm, a_ref, 0))
        b_start, b_wait = by_place(odd, pick(up_hbm, b_ref, 1), pick(down_hbm, b_ref, 1))
        a_start()
        b_start()
        for at in range(0, width, 256):
            wqt_ref[:, at:at + 256] = wq_ref[at:at + 256, :].T
            wot_ref[at:at + 256, :] = wo_ref[:, at:at + 256].T
        wg_ref[...] = dot(gain_ref[...], wq_ref[...])
        a_wait()
        b_wait()

    return call(
        "prepare", body, [gain, wq, wo, tie, Far(down), Far(up)],
        [Mem((3 * hd, width), BF16), Mem((width, hd), BF16), Mem((1, 3 * hd), F32),
         stream(rows, width, 1), stream(rows, width, 1)],
        [pltpu.SemaphoreType.DMA((2,))],
    )


def turn_kernel(h, g, fixed, mask, turned, parts):
    rows, width = sum(x.shape[0] for x in h), h[0].shape[1]
    hd = HEADS_DEV * HEAD_DIM

    def body(ins, outs, scratch):
        h, g, fixed, mask_ref, turned = ins
        out, e, (u_ref, dqkv_ref, att_ref, dg_ref) = outs
        qkv_ref, p_ref, st_ref = scratch
        forward_body(h, *fixed, mask_ref, out, u_ref, qkv_ref, p_ref, att_ref, st_ref)
        backward_body(g, h, fixed[0], *turned, qkv_ref, p_ref, st_ref, e, dqkv_ref, dg_ref)

    out, e, (u, dqkv, att, dgain) = call(
        "turn", body, [h, g, fixed, mask, turned],
        [
            stream(rows, width, 1),
            stream(rows, width, parts),
            [Mem((rows, width), BF16), Mem((rows, 3 * hd), BF16), Mem((rows, hd), BF16), Mem((8, width), F32)],
        ],
        [
            pltpu.VMEM((rows, 3 * hd), BF16),
            pltpu.VMEM((HEADS_DEV, rows, rows), F32),
            pltpu.VMEM((rows, 256), F32),
        ],
    )
    return out, e, (u, dqkv, att, g, dgain)


def backward_kernel(g, h, gain, turned, saved, parts):
    rows, width = saved[0].shape
    u, qkv, probs, att, stats = saved

    def body(ins, outs, scratch):
        g, h, gain_ref, turned, (qkv_ref, p_ref, st_ref) = ins
        e, dqkv_ref, dg_ref = outs
        backward_body(g, h, gain_ref, *turned, qkv_ref, p_ref, st_ref, e, dqkv_ref, dg_ref)

    e, dqkv, dgain = call(
        "backward", body, [g, h, gain, turned, [qkv, probs, stats]],
        [stream(rows, width, parts), Mem(qkv.shape, BF16), Mem((8, width), F32)],
    )
    return e, (u, dqkv, att, g, dgain)


def out_weights(uses, width, put):
    att = jnp.concatenate([use[2][...] for use in uses], axis=0)
    for n in range(0, width, 512):
        cols = pl.ds(n, 512)
        put(cols, dot(att, jnp.concatenate([whole(use[3], cols) for use in uses], axis=0), TN))


def in_weights(uses, width, put):
    dqkv = jnp.concatenate([use[1][...] for use in uses], axis=0)
    for m in range(0, width, 256):
        put(pl.ds(m, 256), dot(jnp.concatenate([use[0][:, m:m + 256] for use in uses], axis=0), dqkv, TN))


def gain_sum(uses):
    total = uses[0][4][...]
    for use in uses[1:]:
        total = total + use[4][...]
    return total


class Copies:
    def __init__(self, sems, odd):
        self.sems, self.odd, self.waits = sems, odd, []

    def push(self, source, target, other=None):
        sem = self.sems.at[len(self.waits)]
        copy = pltpu.make_async_copy(source, target, sem)
        if other is None:
            copy.start()
        else:
            by_place(self.odd, copy, pltpu.make_async_copy(source, other, sem))[0]()
        self.waits.append(copy.wait)

    def wait(self):
        for wait in self.waits:
            wait()


def early_weights(uses, out_a, out_b, us):
    rows, width = uses[0][0].shape
    hd = HEADS_DEV * HEAD_DIM

    def body(ins, outs, scratch):
        uses, (a_ref,), (b_ref,) = ins
        (down, up), gain_out, wo_out, wq_out = outs
        copies = Copies(scratch[0], is_odd())
        copies.push(a_ref, down.at[0], up.at[0])
        copies.push(b_ref, up.at[0], down.at[0])
        gain_out[...] = gain_sum(uses)

        def put_wo(cols, value):
            wo_out[:, cols] = value

        def put_wq(at, value):
            wq_out[at, :] = value

        out_weights(uses, width, put_wo)
        in_weights(uses, width, put_wq)
        copies.wait()

    outs, *sums = call(
        "early_weights", body, [list(uses), out_a, out_b],
        [[jax.ShapeDtypeStruct((1, rows, width), BF16)] * 2,
         Mem((8, width), F32), Mem((hd, width), F32), Mem((width, 3 * hd), F32)],
        [pltpu.SemaphoreType.DMA((2,))], us=us,
    )
    return outs, sums


def more_weights(uses, sums):
    width = uses[0][0].shape[1]

    def body(ins, outs, scratch):
        uses, (gain_in, wo_in, wq_in) = ins
        gain_out, wo_out, wq_out = outs
        gain_out[...] = gain_in[...] + gain_sum(uses)

        def put_wo(cols, value):
            wo_out[:, cols] = wo_in[:, cols] + value

        def put_wq(at, value):
            wq_out[at, :] = wq_in[at, :] + value

        out_weights(uses, width, put_wo)
        in_weights(uses, width, put_wq)

    return call("more_weights", body, [list(uses), list(sums)], [Mem(x.shape, F32) for x in sums])


def finish_kernel(g, h, gain, turned, saved, back_b, uses, sums):
    rows, width = saved[0].shape
    hd = HEADS_DEV * HEAD_DIM
    u, qkv, probs, att, stats = saved

    def body(ins, outs, scratch):
        g, h, gain_ref, (wqt_ref, wot_ref, wg_ref), (u_ref, qkv_ref, p_ref, att_ref, st_ref), (b_ref,), uses, sums = ins
        gain_total, wo_sum, wq_sum = sums
        (down, up), gain_hbm, wo_hbm, wq_hbm = outs
        e_ref, dqkv_ref, dg_ref, wo_buf, wq_buf, gain_buf, sems = scratch
        copies = Copies(sems, is_odd())
        copies.push(b_ref, up.at[0], down.at[0])
        uses = [*uses, (u_ref, dqkv_ref, att_ref, g, dg_ref)]

        def put_wo(cols, value):
            wo_buf[:, cols] = (wo_sum[:, cols] + value).astype(BF16)
            copies.push(wo_buf.at[:, cols], wo_hbm.at[0, :, cols])

        def put_wq(at, value):
            wq_buf[at, :] = (wq_sum[at, :] + value).astype(BF16)
            copies.push(wq_buf.at[at], wq_hbm.at[0, at])

        def done(cols):
            copies.push(e_ref.at[:, cols], down.at[0, :, cols], up.at[0, :, cols])

        attention_reverse(g, wot_ref, qkv_ref, p_ref, dqkv_ref)
        out_weights(uses, width, put_wo)
        in_weights(uses, width, put_wq)
        norm_reverse(g, h, gain_ref, wqt_ref, wg_ref, qkv_ref, st_ref, [e_ref], dqkv_ref, dg_ref, done)
        gain_buf[...] = jnp.sum(gain_total[...] + gain_sum(uses), axis=0, keepdims=True).astype(BF16)
        copies.push(gain_buf, gain_hbm)
        copies.wait()

    return call(
        "finish", body, [g, h, gain, turned, list(saved), back_b, list(uses), list(sums)],
        [
            [jax.ShapeDtypeStruct((1, rows, width), BF16)] * 2,
            jax.ShapeDtypeStruct((1, width), BF16),
            jax.ShapeDtypeStruct((1, hd, width), BF16),
            jax.ShapeDtypeStruct((1, width, 3 * hd), BF16),
        ],
        [
            pltpu.VMEM((rows, width), BF16),
            pltpu.VMEM(qkv.shape, BF16),
            pltpu.VMEM((8, width), F32),
            pltpu.VMEM((hd, width), BF16),
            pltpu.VMEM((width, 3 * hd), BF16),
            pltpu.VMEM((1, width), BF16),
            pltpu.SemaphoreType.DMA((2 + width // 512 * 2 + width // 256,)),
        ],
    )


def shards(acts_down, acts_up, cotangent_down, cotangent_up, ln_gain, w_qkv, w_out, band_offsets):
    sections = lax.axis_size("section")
    near = [(i, i ^ 1) for i in range(sections)]
    far = [(i, (i + (1 if i % 2 else -1)) % sections) for i in range(sections)]

    def swap_near(x):
        return [lax.ppermute(part, "section", near) for part in x]

    def swap_far(x):
        return [lax.ppermute(part, "section", far) for part in x]

    def after(x, other):
        return lax.optimization_barrier((x, other))[0]

    a0, b0, gain, wq, wo, mask, a1_out, a0_saved = first_kernel(
        band_offsets.T, ln_gain, w_qkv, w_out, acts_down, acts_up, 1)
    fixed = [gain, wq, wo]
    a1 = swap_far(a1_out)
    b1_out, b0_saved = forward_kernel(after(b0, a0_saved[4]), fixed, mask, NEAR_PARTS)
    b1 = swap_near(b1_out)
    b2_out, b1_saved = forward_kernel(after(b1, b0_saved[4]), fixed, mask, 1)
    *turned, cot_a, cot_b = prepare_kernel(gain, wq, wo, b1_saved[4], cotangent_down, cotangent_up)
    b2 = swap_far(after(b2_out, turned[2]))
    a2_out, a1_saved = forward_kernel(after(a1, turned[2]), fixed, mask, NEAR_SMALL)
    a2 = swap_near(a2_out)
    out_a, ea2, use_a2 = turn_kernel(after(a2, a1_saved[4]), cot_a, fixed, mask, turned, NEAR_SMALL)
    ca1 = swap_near(ea2)
    (ea1_fore, ea1_rest), use_a1 = backward_kernel(after(ca1, use_a2[4]), a1, gain, turned, a1_saved, FAR_SHARES)
    (ca0_fore,) = swap_far([ea1_fore])
    out_b, eb2, use_b2 = turn_kernel(after(b2, use_a1[4]), cot_b, fixed, mask, turned, 2)
    cb1 = swap_far(eb2)
    use_b2, ca0_fore = lax.optimization_barrier((use_b2, ca0_fore))
    (out_down, out_up), sums = early_weights([use_b2, use_a2, use_a1], out_a, out_b, us=8)
    cb1_fore, ea1_rest, sums = lax.optimization_barrier((cb1[0], ea1_rest, sums))
    (ca0_rest,) = swap_far([ea1_rest])
    eb1, use_b1 = backward_kernel([cb1_fore, cb1[1]], b1, gain, turned, b1_saved, NEAR_PARTS)
    cb0 = swap_near(eb1)
    sums = more_weights([after(use_b1, use_b1[4])], sums)
    back_b, use_b0 = backward_kernel(after(cb0, sums[0]), b0, gain, turned, b0_saved, 1)
    ca0 = [ca0_fore, ca0_rest]
    (back_down, back_up), d_gain, d_wo, d_wq = finish_kernel(
        after(ca0, use_b0[4]), a0, gain, turned, a0_saved, back_b, [use_b0], sums)
    return out_down, out_up, back_down, back_up, d_gain, d_wq, d_wo


def solution(mesh):
    both = ("groups", "section")
    in_specs = (
        P(both, None, None), P(both, None, None), P(both, None, None), P(both, None, None),
        P("section", None), P("section", None, None), P("section", None, None), P(),
    )
    out_specs = (
        P(both, None, None), P(both, None, None), P(both, None, None), P(both, None, None),
        P(both, None), P(both, None, None), P(both, None, None),
    )
    return jax.shard_map(shards, mesh=mesh, in_specs=in_specs, out_specs=out_specs, check_vma=False)
```

```python
import math

import jax
import jax.numpy as jnp
from jax import lax
from jax.experimental import pallas as pl
from jax.experimental.pallas import tpu as pltpu
from jax.sharding import PartitionSpec as P

HEADS_DEV = 2
HEAD_DIM = 128
BLOCK = 32
CHUNK = 16
F32 = jnp.float32
BF16 = jnp.bfloat16
NT = (((1,), (1,)), ((), ()))
TN = (((0,), (0,)), ((), ()))
SCALE = 1.0 / math.sqrt(HEAD_DIM)
VM = pl.BlockSpec(memory_space=pltpu.VMEM)
NEAR_PARTS = 2


def dot(a, b, dims=(((1,), (0,)), ((), ()))):
    return lax.dot_general(a, b, dims, preferred_element_type=F32)


def mask_body(odd, offs_ref, rows):
    row = lax.broadcasted_iota(jnp.int32, (rows, rows), 0)
    col = lax.broadcasted_iota(jnp.int32, (rows, rows), 1)
    row_block = row // BLOCK
    col_block = col // BLOCK
    near = row_block == col_block
    for block in range(offs_ref.shape[1]):
        for listed in range(offs_ref.shape[0]):
            near = near | ((row_block == block) & (col_block == block - offs_ref[listed, block]))
    keep = (col <= row) & (near | jnp.logical_not(odd))
    return jnp.where(keep, 1.0, 0.0).astype(F32)


def read(refs, at, size, cols=slice(None)):
    held = refs[0].shape[0]
    return refs[at // held][pl.ds(at % held, size), cols]


def write(refs, at, size, value, cols=slice(None)):
    held = refs[0].shape[0]
    refs[at // held][pl.ds(at % held, size), cols] = value


def whole(refs, cols=slice(None)):
    return jnp.concatenate([ref[:, cols] for ref in refs], axis=0)


def attend(h, gain_ref, wq_ref, mask_ref, u_ref, qkv_ref, p_ref, att_ref, st_ref, waits=None):
    rows, width = u_ref.shape
    hd = HEADS_DEV * HEAD_DIM
    gain = gain_ref[...].astype(F32)
    for start in range(0, rows, CHUNK):
        part = pl.ds(start, CHUNK)
        x = read(h, start, CHUNK).astype(F32)
        mean = jnp.sum(x, axis=-1, keepdims=True) * (1.0 / width)
        centred = x - mean
        rstd = lax.rsqrt(jnp.sum(centred * centred, axis=-1, keepdims=True) * (1.0 / width) + 1e-05)
        u_ref[part, :] = (centred * rstd * gain).astype(BF16)
        st_ref[part, :] = jnp.concatenate(
            [jnp.broadcast_to(mean, (CHUNK, 128)), jnp.broadcast_to(rstd, (CHUNK, 128))], axis=1)
    for n in range(3):
        if waits:
            waits[n].wait()
        qkv_ref[:, n * hd:(n + 1) * hd] = dot(u_ref[...], wq_ref[:, n * hd:(n + 1) * hd]).astype(BF16)
    keep = mask_ref[...]
    heads = [pl.ds(head * HEAD_DIM, HEAD_DIM) for head in range(HEADS_DEV)]
    scores = [dot(qkv_ref[:, cols], qkv_ref[:, pl.ds(hd + cols.start, HEAD_DIM)], NT) for cols in heads]
    weighted = [jnp.where(keep > 0.0, jnp.exp(score * SCALE), 0.0) for score in scores]
    inverse = [1.0 / jnp.sum(value, axis=-1, keepdims=True) for value in weighted]
    probs = [value * scale for value, scale in zip(weighted, inverse)]
    mixed = [
        dot(value.astype(BF16), qkv_ref[:, pl.ds(2 * hd + cols.start, HEAD_DIM)]) for value, cols in zip(probs, heads)
    ]
    for head, cols in enumerate(heads):
        p_ref[head] = probs[head]
        att_ref[:, cols] = mixed[head].astype(BF16)


def project_out(h, att_ref, wo_ref, out):
    rows, width = att_ref.shape[0], wo_ref.shape[1]
    for n in range(0, width, 512):
        cols = pl.ds(n, 512)
        value = dot(att_ref[...], wo_ref[:, cols])
        size = min(out[0].shape[0], h[0].shape[0])
        for at in range(0, rows, size):
            write(out, at, size, (read(h, at, size, cols).astype(F32) + value[at:at + size]).astype(BF16), cols)


def forward_body(h, gain_ref, wq_ref, wo_ref, mask_ref, out, u_ref, qkv_ref, p_ref, att_ref, st_ref, waits=None):
    attend(h, gain_ref, wq_ref, mask_ref, u_ref, qkv_ref, p_ref, att_ref, st_ref, waits)
    if waits:
        waits[3].wait()
    project_out(h, att_ref, wo_ref, out)


def attention_reverse(datt, qkv_ref, p_ref, dqkv_ref):
    hd = HEADS_DEV * HEAD_DIM
    heads = [pl.ds(head * HEAD_DIM, HEAD_DIM) for head in range(HEADS_DEV)]
    keys = [pl.ds(hd + cols.start, HEAD_DIM) for cols in heads]
    values = [pl.ds(2 * hd + cols.start, HEAD_DIM) for cols in heads]
    das = [datt[:, cols.start:cols.start + HEAD_DIM] for cols in heads]
    probs = [p_ref[head] for head in range(HEADS_DEV)]
    dps = [dot(da, qkv_ref[:, cols], NT).astype(BF16).astype(F32) for da, cols in zip(das, values)]
    dvs = [dot(prob.astype(BF16), da, TN) for prob, da in zip(probs, das)]
    totals = [jnp.sum(dp * prob, axis=-1, keepdims=True) for dp, prob in zip(dps, probs)]
    dss = [(prob * (dp - total) * SCALE).astype(BF16) for prob, dp, total in zip(probs, dps, totals)]
    dqs = [dot(ds, qkv_ref[:, cols]) for ds, cols in zip(dss, keys)]
    dks = [dot(ds, qkv_ref[:, cols], TN) for ds, cols in zip(dss, heads)]
    for head in range(HEADS_DEV):
        dqkv_ref[:, values[head]] = dvs[head].astype(BF16)
        dqkv_ref[:, heads[head]] = dqs[head].astype(BF16)
        dqkv_ref[:, keys[head]] = dks[head].astype(BF16)


def lanes(column):
    return jnp.broadcast_to(column, (column.shape[0], 128))


def norm_reverse(g, h, gain_ref, wqt_ref, wg_ref, qkv_ref, st_ref, e, dqkv_ref, dg_ref, done=None):
    rows, width = dqkv_ref.shape[0], wqt_ref.shape[1]
    dqkv32 = dqkv_ref[...].astype(F32)
    first = jnp.sum(dqkv32 * wg_ref[...], axis=-1, keepdims=True) * (1.0 / width)
    second = jnp.sum(dqkv32 * qkv_ref[...].astype(F32), axis=-1, keepdims=True) * (1.0 / width)
    mean, rstd = st_ref[:, 0:128], st_ref[:, 128:256]
    first, second = lanes(first) * rstd, lanes(second) * rstd
    for block in range(0, width, 512):
        wide = dot(dqkv_ref[...], wqt_ref[:, block:block + 512])
        for n in range(0, 512, 128):
            cols = pl.ds(block + n, 128)
            du = wide[:, n:n + 128]
            xhat = (whole(h, cols).astype(F32) - mean) * rstd
            dg_ref[:, cols] = jnp.sum((du * xhat).reshape(rows // 8, 8, 128), axis=0)
            gain = gain_ref[:, cols].astype(F32)
            value = (du * gain) * rstd - first - xhat * second + whole(g, cols).astype(F32)
            size = e[0].shape[0]
            for part in range(len(e)):
                e[part][:, cols] = value[part * size:(part + 1) * size].astype(BF16)
        if done:
            done(pl.ds(block, 512))


def backward_body(g, h, gain_ref, wqt_ref, wot_ref, wg_ref, qkv_ref, p_ref, st_ref, e, dqkv_ref, dg_ref):
    attention_reverse(dot(whole(g), wot_ref[...]).astype(BF16), qkv_ref, p_ref, dqkv_ref)
    norm_reverse(g, h, gain_ref, wqt_ref, wg_ref, qkv_ref, st_ref, e, dqkv_ref, dg_ref)


def params(mib):
    return pltpu.CompilerParams(vmem_limit_bytes=mib << 20)


def cost(us):
    return pl.CostEstimate(flops=int(us * 1e9), bytes_accessed=int(us * 1e5), transcendentals=0)


def by_place(odd, when_odd, when_even):
    def start():
        pl.when(odd)(when_odd.start)
        pl.when(jnp.logical_not(odd))(when_even.start)

    return start, when_odd.wait


def is_odd():
    return lax.axis_index("section") % 2 == 1


def call(name, body, operands, outs, scratch=(), hbm=(), alias=(), us=0.002, mib=24):
    flat_in, tree_in = jax.tree.flatten(operands, is_leaf=lambda x: isinstance(x, Far))
    flat_out, tree_out = jax.tree.flatten(outs, is_leaf=lambda x: isinstance(x, (jax.ShapeDtypeStruct, Mem)))

    def kernel(*refs):
        a, b = len(flat_in), len(flat_in) + len(flat_out)
        body(jax.tree.unflatten(tree_in, refs[:a]), jax.tree.unflatten(tree_out, refs[a:b]), refs[b:])

    far = pl.BlockSpec(memory_space=pltpu.HBM)
    result = pl.pallas_call(
        kernel,
        in_specs=[far if isinstance(x, Far) else VM for x in flat_in],
        out_specs=[far if isinstance(x, jax.ShapeDtypeStruct) else VM for x in flat_out],
        out_shape=[x if isinstance(x, jax.ShapeDtypeStruct) else pltpu.VMEM(x.shape, x.dtype) for x in flat_out],
        scratch_shapes=list(scratch),
        input_output_aliases=dict(alias),
        compiler_params=params(mib),
        cost_estimate=cost(us),
        name=name,
    )(*[x.array if isinstance(x, Far) else x for x in flat_in])
    return jax.tree.unflatten(tree_out, result)


class Far:
    def __init__(self, array):
        self.array = pltpu.with_memory_space_constraint(array, pltpu.HBM)


class Mem:
    def __init__(self, shape, dtype):
        self.shape, self.dtype = shape, dtype


def stream(rows, width, parts):
    return [Mem((rows // parts, width), BF16) for _ in range(parts)]


def saved_outs(rows, width):
    hd = HEADS_DEV * HEAD_DIM
    return [
        Mem((rows, width), BF16),
        Mem((rows, 3 * hd), BF16),
        Mem((HEADS_DEV, rows, rows), F32),
        Mem((rows, hd), BF16),
        Mem((rows, 256), F32),
    ]


def first_kernel(offs, gain, wq, wo, down, up, parts):
    _, rows, width = down.shape
    hd = HEADS_DEV * HEAD_DIM

    def body(ins, outs, scratch):
        offs_hbm, gain_hbm, wq_hbm, wo_hbm, down_hbm, up_hbm = ins
        (a_ref,), (b_ref,), gain_ref, wq_ref, wo_ref, mask_ref, out, saved = outs
        offs_ref, sems = scratch
        odd = is_odd()

        def pick(source, target, sem):
            return pltpu.make_async_copy(source, target, sems.at[sem])

        a_start, a_wait = by_place(odd, pick(down_hbm.at[0], a_ref, 0), pick(up_hbm.at[0], a_ref, 0))
        b_start, b_wait = by_place(odd, pick(up_hbm.at[0], b_ref, 1), pick(down_hbm.at[0], b_ref, 1))
        offs_copy = pick(offs_hbm, offs_ref, 2)
        gain_copy = pick(gain_hbm, gain_ref, 3)
        wo_copy = pick(wo_hbm.at[0], wo_ref, 4)
        cols = [pl.ds(n * hd, hd) for n in range(3)]
        wq_copies = [pick(wq_hbm.at[0, :, cols[n]], wq_ref.at[:, cols[n]], 5 + n) for n in range(3)]
        a_start()
        gain_copy.start()
        offs_copy.start()
        for copy in wq_copies:
            copy.start()
        wo_copy.start()
        b_start()
        offs_copy.wait()
        mask_ref[...] = mask_body(odd, offs_ref, rows)
        a_wait()
        gain_copy.wait()
        forward_body([a_ref], gain_ref, wq_ref, wo_ref, mask_ref, out, *saved, waits=wq_copies + [wo_copy])
        b_wait()

    return call(
        "first", body, [Far(x) for x in (offs, gain, wq, wo, down, up)],
        [
            stream(rows, width, 1), stream(rows, width, 1), Mem(gain.shape, BF16), Mem(wq.shape[1:], BF16),
            Mem(wo.shape[1:], BF16), Mem((rows, rows), F32), stream(rows, width, parts), saved_outs(rows, width),
        ],
        [pltpu.SMEM(offs.shape, jnp.int32), pltpu.SemaphoreType.DMA((8,))],
    )


def forward_kernel(h, fixed, mask, parts, us=0.002):
    rows, width = h[0].shape[0] * len(h), h[0].shape[1]

    def body(ins, outs, scratch):
        h, fixed, mask_ref = ins
        out, saved = outs
        forward_body(h, *fixed, mask_ref, out, *saved)

    return call("forward", body, [h, fixed, mask], [stream(rows, width, parts), saved_outs(rows, width)], us=us)


def prepare_kernel(gain, wq, wo, tie, down, up):
    _, rows, width = down.shape
    hd = HEADS_DEV * HEAD_DIM

    def body(ins, outs, scratch):
        gain_ref, wq_ref, wo_ref, _, down_hbm, up_hbm = ins
        wqt_ref, wot_ref, wg_ref, (a_ref,), (b_ref,), da_ref, db_ref = outs
        (sems,) = scratch
        odd = is_odd()

        def pick(source, target, sem):
            return pltpu.make_async_copy(source.at[0], target, sems.at[sem])

        a_start, a_wait = by_place(odd, pick(down_hbm, a_ref, 0), pick(up_hbm, a_ref, 0))
        b_start, b_wait = by_place(odd, pick(up_hbm, b_ref, 1), pick(down_hbm, b_ref, 1))
        a_start()
        b_start()
        for at in range(0, width, 256):
            wqt_ref[:, at:at + 256] = wq_ref[at:at + 256, :].T
            wot_ref[at:at + 256, :] = wo_ref[:, at:at + 256].T
        wg_ref[...] = dot(gain_ref[...], wq_ref[...])
        a_wait()
        b_wait()
        both = dot(jnp.concatenate([a_ref[...], b_ref[...]], axis=0), wot_ref[...]).astype(BF16)
        da_ref[...] = both[:rows]
        db_ref[...] = both[rows:]

    return call(
        "prepare", body, [gain, wq, wo, tie, Far(down), Far(up)],
        [Mem((3 * hd, width), BF16), Mem((width, hd), BF16), Mem((1, 3 * hd), F32),
         stream(rows, width, 1), stream(rows, width, 1), Mem((rows, hd), BF16), Mem((rows, hd), BF16)],
        [pltpu.SemaphoreType.DMA((2,))],
    )


def turn_kernel(h, g, datt, fixed, mask, turned, parts):
    rows, width = h[0].shape[0] * len(h), h[0].shape[1]
    hd = HEADS_DEV * HEAD_DIM

    def body(ins, outs, scratch):
        h, g, datt_ref, (gain_ref, wq_ref), mask_ref, (wqt_ref, wg_ref) = ins
        e, (u_ref, dqkv_ref, att_ref, dg_ref) = outs
        qkv_ref, p_ref, st_ref = scratch
        attend(h, gain_ref, wq_ref, mask_ref, u_ref, qkv_ref, p_ref, att_ref, st_ref)
        attention_reverse(datt_ref[...], qkv_ref, p_ref, dqkv_ref)
        norm_reverse(g, h, gain_ref, wqt_ref, wg_ref, qkv_ref, st_ref, e, dqkv_ref, dg_ref)

    e, (u, dqkv, att, dgain) = call(
        "turn", body, [h, g, datt, fixed[:2], mask, [turned[0], turned[2]]],
        [
            stream(rows, width, parts),
            [Mem((rows, width), BF16), Mem((rows, 3 * hd), BF16), Mem((rows, hd), BF16), Mem((8, width), F32)],
        ],
        [
            pltpu.VMEM((rows, 3 * hd), BF16),
            pltpu.VMEM((HEADS_DEV, rows, rows), F32),
            pltpu.VMEM((rows, 256), F32),
        ],
    )
    return e, (u, dqkv, att, g, dgain)


def backward_kernel(g, h, gain, turned, saved, parts):
    rows, width = saved[0].shape
    u, qkv, probs, att, stats = saved

    def body(ins, outs, scratch):
        g, h, gain_ref, turned, (qkv_ref, p_ref, st_ref) = ins
        e, dqkv_ref, dg_ref = outs
        backward_body(g, h, gain_ref, *turned, qkv_ref, p_ref, st_ref, e, dqkv_ref, dg_ref)

    e, dqkv, dgain = call(
        "backward", body, [g, h, gain, turned, [qkv, probs, stats]],
        [stream(rows, width, parts), Mem(qkv.shape, BF16), Mem((8, width), F32)],
    )
    return e, (u, dqkv, att, g, dgain)


def out_weights(uses, width, put):
    att = jnp.concatenate([use[2][...] for use in uses], axis=0)
    for n in range(0, width, 512):
        cols = pl.ds(n, 512)
        put(cols, dot(att, jnp.concatenate([whole(use[3], cols) for use in uses], axis=0), TN))


def in_weights(uses, width, put):
    dqkv = jnp.concatenate([use[1][...] for use in uses], axis=0)
    for m in range(0, width, 256):
        put(pl.ds(m, 256), dot(jnp.concatenate([use[0][:, m:m + 256] for use in uses], axis=0), dqkv, TN))


def gain_sum(uses):
    total = uses[0][4][...]
    for use in uses[1:]:
        total = total + use[4][...]
    return total


class Copies:
    def __init__(self, sems, odd):
        self.sems, self.odd, self.waits = sems, odd, []

    def push(self, source, target, other=None):
        sem = self.sems.at[len(self.waits)]
        copy = pltpu.make_async_copy(source, target, sem)
        if other is None:
            copy.start()
        else:
            by_place(self.odd, copy, pltpu.make_async_copy(source, other, sem))[0]()
        self.waits.append(copy.wait)

    def wait(self):
        for wait in self.waits:
            wait()


def early_weights(uses, h_a, att_a, h_b, att_b, wo):
    rows, width = uses[0][0].shape
    hd = HEADS_DEV * HEAD_DIM

    def body(ins, outs, scratch):
        uses, h_a, att_a_ref, h_b, att_b_ref, wo_ref = ins
        (down, up), gain_out, wo_out, wq_out = outs
        a_ref, b_ref, sems = scratch
        copies = Copies(sems, is_odd())
        project_out(h_a, att_a_ref, wo_ref, [a_ref])
        copies.push(a_ref, down.at[0], up.at[0])
        project_out(h_b, att_b_ref, wo_ref, [b_ref])
        copies.push(b_ref, up.at[0], down.at[0])
        gain_out[...] = gain_sum(uses)

        def put_wo(cols, value):
            wo_out[:, cols] = value

        def put_wq(at, value):
            wq_out[at, :] = value

        out_weights(uses, width, put_wo)
        in_weights(uses, width, put_wq)
        copies.wait()

    outs, *sums = call(
        "early_weights", body, [list(uses), h_a, att_a, h_b, att_b, wo],
        [[jax.ShapeDtypeStruct((1, rows, width), BF16)] * 2,
         Mem((8, width), F32), Mem((hd, width), F32), Mem((width, 3 * hd), F32)],
        [pltpu.VMEM((rows, width), BF16), pltpu.VMEM((rows, width), BF16), pltpu.SemaphoreType.DMA((2,))],
    )
    return outs, sums


def more_weights(uses, sums):
    width = uses[0][0].shape[1]

    def body(ins, outs, scratch):
        uses, (gain_in, wo_in, wq_in) = ins
        gain_out, wo_out, wq_out = outs
        gain_out[...] = gain_in[...] + gain_sum(uses)

        def put_wo(cols, value):
            wo_out[:, cols] = wo_in[:, cols] + value

        def put_wq(at, value):
            wq_out[at, :] = wq_in[at, :] + value

        out_weights(uses, width, put_wo)
        in_weights(uses, width, put_wq)

    return call("more_weights", body, [list(uses), list(sums)], [Mem(x.shape, F32) for x in sums])


def finish_kernel(g, h, gain, turned, saved, back_b, uses, sums):
    rows, width = saved[0].shape
    hd = HEADS_DEV * HEAD_DIM
    u, qkv, probs, att, stats = saved

    def body(ins, outs, scratch):
        g, h, gain_ref, (wqt_ref, wot_ref, wg_ref), (u_ref, qkv_ref, p_ref, att_ref, st_ref), (b_ref,), uses, sums = ins
        gain_total, wo_sum, wq_sum = sums
        (down, up), gain_hbm, wo_hbm, wq_hbm = outs
        e_ref, dqkv_ref, dg_ref, wo_buf, wq_buf, gain_buf, sems = scratch
        copies = Copies(sems, is_odd())
        copies.push(b_ref, up.at[0], down.at[0])
        uses = [*uses, (u_ref, dqkv_ref, att_ref, g, dg_ref)]

        def put_wo(cols, value):
            wo_buf[:, cols] = (wo_sum[:, cols] + value).astype(BF16)
            copies.push(wo_buf.at[:, cols], wo_hbm.at[0, :, cols])

        def put_wq(at, value):
            wq_buf[at, :] = (wq_sum[at, :] + value).astype(BF16)
            copies.push(wq_buf.at[at], wq_hbm.at[0, at])

        def done(cols):
            copies.push(e_ref.at[:, cols], down.at[0, :, cols], up.at[0, :, cols])

        out_weights(uses, width, put_wo)
        attention_reverse(dot(whole(g), wot_ref[...]).astype(BF16), qkv_ref, p_ref, dqkv_ref)
        in_weights(uses, width, put_wq)
        norm_reverse(g, h, gain_ref, wqt_ref, wg_ref, qkv_ref, st_ref, [e_ref], dqkv_ref, dg_ref, done)
        gain_buf[...] = jnp.sum(gain_total[...] + gain_sum(uses), axis=0, keepdims=True).astype(BF16)
        copies.push(gain_buf, gain_hbm)
        copies.wait()

    return call(
        "finish", body, [g, h, gain, turned, list(saved), back_b, list(uses), list(sums)],
        [
            [jax.ShapeDtypeStruct((1, rows, width), BF16)] * 2,
            jax.ShapeDtypeStruct((1, width), BF16),
            jax.ShapeDtypeStruct((1, hd, width), BF16),
            jax.ShapeDtypeStruct((1, width, 3 * hd), BF16),
        ],
        [
            pltpu.VMEM((rows, width), BF16),
            pltpu.VMEM(qkv.shape, BF16),
            pltpu.VMEM((8, width), F32),
            pltpu.VMEM((hd, width), BF16),
            pltpu.VMEM((width, 3 * hd), BF16),
            pltpu.VMEM((1, width), BF16),
            pltpu.SemaphoreType.DMA((2 + width // 512 * 2 + width // 256,)),
        ],
    )


def shards(acts_down, acts_up, cotangent_down, cotangent_up, ln_gain, w_qkv, w_out, band_offsets):
    sections = lax.axis_size("section")
    near = [(i, i ^ 1) for i in range(sections)]
    far = [(i, (i + (1 if i % 2 else -1)) % sections) for i in range(sections)]

    def swap_near(x):
        return [lax.ppermute(part, "section", near) for part in x]

    def swap_far(x):
        return [lax.ppermute(part, "section", far) for part in x]

    def after(x, other):
        return lax.optimization_barrier((x, other))[0]

    a0, b0, gain, wq, wo, mask, a1_out, a0_saved = first_kernel(
        band_offsets.T, ln_gain, w_qkv, w_out, acts_down, acts_up, 1)
    fixed = [gain, wq, wo]
    a1 = swap_far(a1_out)
    b1_out, b0_saved = forward_kernel(after(b0, a0_saved[4]), fixed, mask, NEAR_PARTS)
    b1 = swap_near(b1_out)
    b2_out, b1_saved = forward_kernel(after(b1, b0_saved[4]), fixed, mask, 1)
    b2 = swap_far(b2_out)
    *turned, cot_a, cot_b, datt_a, datt_b = prepare_kernel(gain, wq, wo, b1_saved[4], cotangent_down, cotangent_up)
    a2_out, a1_saved = forward_kernel(after(a1, turned[2]), fixed, mask, NEAR_PARTS, us=8)
    a2 = swap_near(a2_out)
    eb2, use_b2 = turn_kernel(after(b2, a1_saved[4]), cot_b, datt_b, fixed, mask, turned, 1)
    cb1 = swap_far(eb2)
    ea2, use_a2 = turn_kernel(after(a2, use_b2[4]), cot_a, datt_a, fixed, mask, turned, NEAR_PARTS)
    ca1 = swap_near(ea2)
    ea1, use_a1 = backward_kernel(after(ca1, use_a2[4]), a1, gain, turned, a1_saved, 1)
    ca0 = swap_far(ea1)
    (out_down, out_up), sums = early_weights(
        [use_b2, use_a2, after(use_a1, use_a1[4])], a2, use_a2[2], b2, use_b2[2], wo)
    eb1, use_b1 = backward_kernel(after(cb1, sums[0]), b1, gain, turned, b1_saved, NEAR_PARTS)
    cb0 = swap_near(eb1)
    sums = more_weights([after(use_b1, use_b1[4])], sums)
    back_b, use_b0 = backward_kernel(after(cb0, sums[0]), b0, gain, turned, b0_saved, 1)
    (back_down, back_up), d_gain, d_wo, d_wq = finish_kernel(
        after(ca0, use_b0[4]), a0, gain, turned, a0_saved, back_b, [use_b0], sums)
    return out_down, out_up, back_down, back_up, d_gain, d_wq, d_wo


def solution(mesh):
    both = ("groups", "section")
    in_specs = (
        P(both, None, None), P(both, None, None), P(both, None, None), P(both, None, None),
        P("section", None), P("section", None, None), P("section", None, None), P(),
    )
    out_specs = (
        P(both, None, None), P(both, None, None), P(both, None, None), P(both, None, None),
        P(both, None), P(both, None, None), P(both, None, None),
    )
    return jax.shard_map(shards, mesh=mesh, in_specs=in_specs, out_specs=out_specs, check_vma=False)
```

```python
import math

import jax
import jax.numpy as jnp
from jax import lax
from jax.experimental import pallas as pl
from jax.experimental.pallas import tpu as pltpu
from jax.sharding import PartitionSpec as P

HEADS_DEV = 2
HEAD_DIM = 128
BLOCK = 32
CHUNK = 16
F32 = jnp.float32
BF16 = jnp.bfloat16
NT = (((1,), (1,)), ((), ()))
TN = (((0,), (0,)), ((), ()))
SCALE = 1.0 / math.sqrt(HEAD_DIM)
VM = pl.BlockSpec(memory_space=pltpu.VMEM)
NEAR_PARTS = 2


def dot(a, b, dims=(((1,), (0,)), ((), ()))):
    return lax.dot_general(a, b, dims, preferred_element_type=F32)


def mask_body(odd, offs_ref, rows):
    row = lax.broadcasted_iota(jnp.int32, (rows, rows), 0)
    col = lax.broadcasted_iota(jnp.int32, (rows, rows), 1)
    row_block = row // BLOCK
    col_block = col // BLOCK
    near = row_block == col_block
    for block in range(offs_ref.shape[1]):
        for listed in range(offs_ref.shape[0]):
            near = near | ((row_block == block) & (col_block == block - offs_ref[listed, block]))
    keep = (col <= row) & (near | jnp.logical_not(odd))
    return jnp.where(keep, 1.0, 0.0).astype(F32)


def read(refs, at, size, cols=slice(None)):
    held = refs[0].shape[0]
    return refs[at // held][pl.ds(at % held, size), cols]


def write(refs, at, size, value, cols=slice(None)):
    held = refs[0].shape[0]
    refs[at // held][pl.ds(at % held, size), cols] = value


def whole(refs, cols=slice(None)):
    return jnp.concatenate([ref[:, cols] for ref in refs], axis=0)


def attend(h, gain_ref, wq_ref, mask_ref, u_ref, qkv_ref, p_ref, att_ref, st_ref, waits=None):
    rows, width = u_ref.shape
    hd = HEADS_DEV * HEAD_DIM
    gain = gain_ref[...].astype(F32)
    for start in range(0, rows, CHUNK):
        part = pl.ds(start, CHUNK)
        x = read(h, start, CHUNK).astype(F32)
        mean = jnp.sum(x, axis=-1, keepdims=True) * (1.0 / width)
        centred = x - mean
        rstd = lax.rsqrt(jnp.sum(centred * centred, axis=-1, keepdims=True) * (1.0 / width) + 1e-05)
        u_ref[part, :] = (centred * rstd * gain).astype(BF16)
        st_ref[part, :] = jnp.concatenate(
            [jnp.broadcast_to(mean, (CHUNK, 128)), jnp.broadcast_to(rstd, (CHUNK, 128))], axis=1)
    if waits:
        total = None
        depth = width // (len(waits) - 1)
        for n in range(len(waits) - 1):
            waits[n].wait()
            at = n * depth
            part = dot(u_ref[:, at:at + depth], wq_ref[at:at + depth, :])
            total = part if total is None else total + part
        qkv_ref[...] = total.astype(BF16)
    else:
        for n in range(3):
            qkv_ref[:, n * hd:(n + 1) * hd] = dot(u_ref[...], wq_ref[:, n * hd:(n + 1) * hd]).astype(BF16)
    keep = mask_ref[...]
    heads = [pl.ds(head * HEAD_DIM, HEAD_DIM) for head in range(HEADS_DEV)]
    scores = [dot(qkv_ref[:, cols], qkv_ref[:, pl.ds(hd + cols.start, HEAD_DIM)], NT) for cols in heads]
    weighted = [jnp.where(keep > 0.0, jnp.exp(score * SCALE), 0.0) for score in scores]
    probs = [value / jnp.sum(value, axis=-1, keepdims=True) for value in weighted]
    mixed = [
        dot(value.astype(BF16), qkv_ref[:, pl.ds(2 * hd + cols.start, HEAD_DIM)]) for value, cols in zip(probs, heads)
    ]
    for head, cols in enumerate(heads):
        p_ref[head] = probs[head]
        att_ref[:, cols] = mixed[head].astype(BF16)


def project_out(h, att_ref, wo_ref, out):
    rows, width = att_ref.shape[0], wo_ref.shape[1]
    for n in range(0, width, 512):
        cols = pl.ds(n, 512)
        value = dot(att_ref[...], wo_ref[:, cols])
        size = min(out[0].shape[0], h[0].shape[0])
        for at in range(0, rows, size):
            write(out, at, size, (read(h, at, size, cols).astype(F32) + value[at:at + size]).astype(BF16), cols)


def forward_body(h, gain_ref, wq_ref, wo_ref, mask_ref, out, u_ref, qkv_ref, p_ref, att_ref, st_ref, waits=None):
    attend(h, gain_ref, wq_ref, mask_ref, u_ref, qkv_ref, p_ref, att_ref, st_ref, waits)
    if waits:
        waits[-1].wait()
    project_out(h, att_ref, wo_ref, out)


def attention_reverse(datt, qkv_ref, p_ref, dqkv_ref):
    hd = HEADS_DEV * HEAD_DIM
    heads = [pl.ds(head * HEAD_DIM, HEAD_DIM) for head in range(HEADS_DEV)]
    keys = [pl.ds(hd + cols.start, HEAD_DIM) for cols in heads]
    values = [pl.ds(2 * hd + cols.start, HEAD_DIM) for cols in heads]
    das = [datt[:, cols.start:cols.start + HEAD_DIM] for cols in heads]
    probs = [p_ref[head] for head in range(HEADS_DEV)]
    dps = [dot(da, qkv_ref[:, cols], NT).astype(BF16).astype(F32) for da, cols in zip(das, values)]
    dvs = [dot(prob.astype(BF16), da, TN) for prob, da in zip(probs, das)]
    totals = [jnp.sum(dp * prob, axis=-1, keepdims=True) for dp, prob in zip(dps, probs)]
    dss = [(prob * (dp - total) * SCALE).astype(BF16) for prob, dp, total in zip(probs, dps, totals)]
    dqs = [dot(ds, qkv_ref[:, cols]) for ds, cols in zip(dss, keys)]
    dks = [dot(ds, qkv_ref[:, cols], TN) for ds, cols in zip(dss, heads)]
    for head in range(HEADS_DEV):
        dqkv_ref[:, values[head]] = dvs[head].astype(BF16)
        dqkv_ref[:, heads[head]] = dqs[head].astype(BF16)
        dqkv_ref[:, keys[head]] = dks[head].astype(BF16)


def lanes(column):
    return jnp.broadcast_to(column, (column.shape[0], 128))


def norm_reverse(g, h, gain_ref, wqt_ref, wg_ref, qkv_ref, st_ref, e, dqkv_ref, dg_ref, done=None):
    rows, width = dqkv_ref.shape[0], wqt_ref.shape[1]
    dqkv32 = dqkv_ref[...].astype(F32)
    first = jnp.sum(dqkv32 * wg_ref[...], axis=-1, keepdims=True) * (1.0 / width)
    second = jnp.sum(dqkv32 * qkv_ref[...].astype(F32), axis=-1, keepdims=True) * (1.0 / width)
    mean, rstd = st_ref[:, 0:128], st_ref[:, 128:256]
    first, second = lanes(first) * rstd, lanes(second) * rstd
    for block in range(0, width, 512):
        wide = dot(dqkv_ref[...], wqt_ref[:, block:block + 512])
        for n in range(0, 512, 128):
            cols = pl.ds(block + n, 128)
            du = wide[:, n:n + 128]
            xhat = (whole(h, cols).astype(F32) - mean) * rstd
            dg_ref[:, cols] = jnp.sum((du * xhat).reshape(rows // 8, 8, 128), axis=0)
            gain = gain_ref[:, cols].astype(F32)
            value = (du * gain) * rstd - first - xhat * second + whole(g, cols).astype(F32)
            size = e[0].shape[0]
            for part in range(len(e)):
                e[part][:, cols] = value[part * size:(part + 1) * size].astype(BF16)
        if done:
            done(pl.ds(block, 512))


def backward_body(g, h, gain_ref, wqt_ref, wot_ref, wg_ref, qkv_ref, p_ref, st_ref, e, dqkv_ref, dg_ref):
    attention_reverse(dot(whole(g), wot_ref[...]).astype(BF16), qkv_ref, p_ref, dqkv_ref)
    norm_reverse(g, h, gain_ref, wqt_ref, wg_ref, qkv_ref, st_ref, e, dqkv_ref, dg_ref)


def params(mib):
    return pltpu.CompilerParams(vmem_limit_bytes=mib << 20)


def cost(us):
    return pl.CostEstimate(flops=int(us * 1e9), bytes_accessed=int(us * 1e5), transcendentals=0)


def by_place(odd, when_odd, when_even):
    def start():
        pl.when(odd)(when_odd.start)
        pl.when(jnp.logical_not(odd))(when_even.start)

    return start, when_odd.wait


def is_odd():
    return lax.axis_index("section") % 2 == 1


def call(name, body, operands, outs, scratch=(), hbm=(), alias=(), us=0.002, mib=24):
    flat_in, tree_in = jax.tree.flatten(operands, is_leaf=lambda x: isinstance(x, Far))
    flat_out, tree_out = jax.tree.flatten(outs, is_leaf=lambda x: isinstance(x, (jax.ShapeDtypeStruct, Mem)))

    def kernel(*refs):
        a, b = len(flat_in), len(flat_in) + len(flat_out)
        body(jax.tree.unflatten(tree_in, refs[:a]), jax.tree.unflatten(tree_out, refs[a:b]), refs[b:])

    far = pl.BlockSpec(memory_space=pltpu.HBM)
    result = pl.pallas_call(
        kernel,
        in_specs=[far if isinstance(x, Far) else VM for x in flat_in],
        out_specs=[far if isinstance(x, jax.ShapeDtypeStruct) else VM for x in flat_out],
        out_shape=[x if isinstance(x, jax.ShapeDtypeStruct) else pltpu.VMEM(x.shape, x.dtype) for x in flat_out],
        scratch_shapes=list(scratch),
        input_output_aliases=dict(alias),
        compiler_params=params(mib),
        cost_estimate=cost(us),
        name=name,
    )(*[x.array if isinstance(x, Far) else x for x in flat_in])
    return jax.tree.unflatten(tree_out, result)


class Far:
    def __init__(self, array):
        self.array = pltpu.with_memory_space_constraint(array, pltpu.HBM)


class Mem:
    def __init__(self, shape, dtype):
        self.shape, self.dtype = shape, dtype


def stream(rows, width, parts):
    return [Mem((rows // parts, width), BF16) for _ in range(parts)]


def saved_outs(rows, width):
    hd = HEADS_DEV * HEAD_DIM
    return [
        Mem((rows, width), BF16),
        Mem((rows, 3 * hd), BF16),
        Mem((HEADS_DEV, rows, rows), F32),
        Mem((rows, hd), BF16),
        Mem((rows, 256), F32),
    ]


def first_kernel(offs, gain, wq, wo, down, up, parts):
    _, rows, width = down.shape
    hd = HEADS_DEV * HEAD_DIM

    def body(ins, outs, scratch):
        offs_hbm, gain_hbm, wq_hbm, wo_hbm, down_hbm, up_hbm = ins
        (a_ref,), (b_ref,), gain_ref, wq_ref, wo_ref, mask_ref, out, saved = outs
        offs_ref, sems = scratch
        odd = is_odd()

        def pick(source, target, sem):
            return pltpu.make_async_copy(source, target, sems.at[sem])

        a_start, a_wait = by_place(odd, pick(down_hbm.at[0], a_ref, 0), pick(up_hbm.at[0], a_ref, 0))
        b_start, b_wait = by_place(odd, pick(up_hbm.at[0], b_ref, 1), pick(down_hbm.at[0], b_ref, 1))
        offs_copy = pick(offs_hbm, offs_ref, 2)
        gain_copy = pick(gain_hbm, gain_ref, 3)
        wo_copy = pick(wo_hbm.at[0], wo_ref, 4)
        spans = [pl.ds(n * (width // 4), width // 4) for n in range(4)]
        wq_copies = [pick(wq_hbm.at[0, span], wq_ref.at[span], 5 + n) for n, span in enumerate(spans)]
        a_start()
        gain_copy.start()
        offs_copy.start()
        for copy in wq_copies:
            copy.start()
        wo_copy.start()
        b_start()
        offs_copy.wait()
        mask_ref[...] = mask_body(odd, offs_ref, rows)
        a_wait()
        gain_copy.wait()
        forward_body([a_ref], gain_ref, wq_ref, wo_ref, mask_ref, out, *saved, waits=wq_copies + [wo_copy])
        b_wait()

    return call(
        "first", body, [Far(x) for x in (offs, gain, wq, wo, down, up)],
        [
            stream(rows, width, 1), stream(rows, width, 1), Mem(gain.shape, BF16), Mem(wq.shape[1:], BF16),
            Mem(wo.shape[1:], BF16), Mem((rows, rows), F32), stream(rows, width, parts), saved_outs(rows, width),
        ],
        [pltpu.SMEM(offs.shape, jnp.int32), pltpu.SemaphoreType.DMA((9,))],
    )


def forward_kernel(h, fixed, mask, parts, us=0.002):
    rows, width = h[0].shape[0] * len(h), h[0].shape[1]

    def body(ins, outs, scratch):
        h, fixed, mask_ref = ins
        out, saved = outs
        forward_body(h, *fixed, mask_ref, out, *saved)

    return call("forward", body, [h, fixed, mask], [stream(rows, width, parts), saved_outs(rows, width)], us=us)


def prepare_kernel(gain, wq, wo, tie, down, up):
    _, rows, width = down.shape
    hd = HEADS_DEV * HEAD_DIM

    def body(ins, outs, scratch):
        gain_ref, wq_ref, wo_ref, _, down_hbm, up_hbm = ins
        wqt_ref, wot_ref, wg_ref, (a_ref,), (b_ref,), da_ref, db_ref = outs
        (sems,) = scratch
        odd = is_odd()

        def pick(source, target, sem):
            return pltpu.make_async_copy(source.at[0], target, sems.at[sem])

        a_start, a_wait = by_place(odd, pick(down_hbm, a_ref, 0), pick(up_hbm, a_ref, 0))
        b_start, b_wait = by_place(odd, pick(up_hbm, b_ref, 1), pick(down_hbm, b_ref, 1))
        a_start()
        b_start()
        for at in range(0, width, 256):
            wqt_ref[:, at:at + 256] = wq_ref[at:at + 256, :].T
            wot_ref[at:at + 256, :] = wo_ref[:, at:at + 256].T
        wg_ref[...] = dot(gain_ref[...], wq_ref[...])
        a_wait()
        b_wait()
        both = dot(jnp.concatenate([a_ref[...], b_ref[...]], axis=0), wot_ref[...]).astype(BF16)
        da_ref[...] = both[:rows]
        db_ref[...] = both[rows:]

    return call(
        "prepare", body, [gain, wq, wo, tie, Far(down), Far(up)],
        [Mem((3 * hd, width), BF16), Mem((width, hd), BF16), Mem((1, 3 * hd), F32),
         stream(rows, width, 1), stream(rows, width, 1), Mem((rows, hd), BF16), Mem((rows, hd), BF16)],
        [pltpu.SemaphoreType.DMA((2,))],
    )


def turn_kernel(h, g, datt, fixed, mask, turned, parts):
    rows, width = h[0].shape[0] * len(h), h[0].shape[1]
    hd = HEADS_DEV * HEAD_DIM

    def body(ins, outs, scratch):
        h, g, datt_ref, (gain_ref, wq_ref), mask_ref, (wqt_ref, wg_ref) = ins
        e, (u_ref, dqkv_ref, att_ref, dg_ref) = outs
        qkv_ref, p_ref, st_ref = scratch
        attend(h, gain_ref, wq_ref, mask_ref, u_ref, qkv_ref, p_ref, att_ref, st_ref)
        attention_reverse(datt_ref[...], qkv_ref, p_ref, dqkv_ref)
        norm_reverse(g, h, gain_ref, wqt_ref, wg_ref, qkv_ref, st_ref, e, dqkv_ref, dg_ref)

    e, (u, dqkv, att, dgain) = call(
        "turn", body, [h, g, datt, fixed[:2], mask, [turned[0], turned[2]]],
        [
            stream(rows, width, parts),
            [Mem((rows, width), BF16), Mem((rows, 3 * hd), BF16), Mem((rows, hd), BF16), Mem((8, width), F32)],
        ],
        [
            pltpu.VMEM((rows, 3 * hd), BF16),
            pltpu.VMEM((HEADS_DEV, rows, rows), F32),
            pltpu.VMEM((rows, 256), F32),
        ],
    )
    return e, (u, dqkv, att, g, dgain)


def backward_kernel(g, h, gain, turned, saved, parts):
    rows, width = saved[0].shape
    u, qkv, probs, att, stats = saved

    def body(ins, outs, scratch):
        g, h, gain_ref, turned, (qkv_ref, p_ref, st_ref) = ins
        e, dqkv_ref, dg_ref = outs
        backward_body(g, h, gain_ref, *turned, qkv_ref, p_ref, st_ref, e, dqkv_ref, dg_ref)

    e, dqkv, dgain = call(
        "backward", body, [g, h, gain, turned, [qkv, probs, stats]],
        [stream(rows, width, parts), Mem(qkv.shape, BF16), Mem((8, width), F32)],
    )
    return e, (u, dqkv, att, g, dgain)


def out_weights(uses, width, put):
    att = jnp.concatenate([use[2][...] for use in uses], axis=0)
    for n in range(0, width, 512):
        cols = pl.ds(n, 512)
        put(cols, dot(att, jnp.concatenate([whole(use[3], cols) for use in uses], axis=0), TN))


def in_weights(uses, width, put):
    dqkv = jnp.concatenate([use[1][...] for use in uses], axis=0)
    for m in range(0, width, 256):
        put(pl.ds(m, 256), dot(jnp.concatenate([use[0][:, m:m + 256] for use in uses], axis=0), dqkv, TN))


def gain_sum(uses):
    total = uses[0][4][...]
    for use in uses[1:]:
        total = total + use[4][...]
    return total


class Copies:
    def __init__(self, sems, odd):
        self.sems, self.odd, self.waits = sems, odd, []

    def push(self, source, target, other=None):
        sem = self.sems.at[len(self.waits)]
        copy = pltpu.make_async_copy(source, target, sem)
        if other is None:
            copy.start()
        else:
            by_place(self.odd, copy, pltpu.make_async_copy(source, other, sem))[0]()
        self.waits.append(copy.wait)

    def wait(self):
        for wait in self.waits:
            wait()


def early_weights(uses, h_a, att_a, h_b, att_b, wo):
    rows, width = uses[0][0].shape
    hd = HEADS_DEV * HEAD_DIM

    def body(ins, outs, scratch):
        uses, h_a, att_a_ref, h_b, att_b_ref, wo_ref = ins
        (down, up), gain_out, wo_out, wq_out = outs
        a_ref, b_ref, sems = scratch
        copies = Copies(sems, is_odd())
        project_out(h_a, att_a_ref, wo_ref, [a_ref])
        copies.push(a_ref, down.at[0], up.at[0])
        project_out(h_b, att_b_ref, wo_ref, [b_ref])
        copies.push(b_ref, up.at[0], down.at[0])
        gain_out[...] = gain_sum(uses)

        def put_wo(cols, value):
            wo_out[:, cols] = value

        def put_wq(at, value):
            wq_out[at, :] = value

        out_weights(uses, width, put_wo)
        in_weights(uses, width, put_wq)
        copies.wait()

    outs, *sums = call(
        "early_weights", body, [list(uses), h_a, att_a, h_b, att_b, wo],
        [[jax.ShapeDtypeStruct((1, rows, width), BF16)] * 2,
         Mem((8, width), F32), Mem((hd, width), F32), Mem((width, 3 * hd), F32)],
        [pltpu.VMEM((rows, width), BF16), pltpu.VMEM((rows, width), BF16), pltpu.SemaphoreType.DMA((2,))],
    )
    return outs, sums


def more_weights(uses, sums):
    width = uses[0][0].shape[1]

    def body(ins, outs, scratch):
        uses, (gain_in, wo_in, wq_in) = ins
        gain_out, wo_out, wq_out = outs
        gain_out[...] = gain_in[...] + gain_sum(uses)

        def put_wo(cols, value):
            wo_out[:, cols] = wo_in[:, cols] + value

        def put_wq(at, value):
            wq_out[at, :] = wq_in[at, :] + value

        out_weights(uses, width, put_wo)
        in_weights(uses, width, put_wq)

    return call("more_weights", body, [list(uses), list(sums)], [Mem(x.shape, F32) for x in sums])


def finish_kernel(g, h, gain, turned, saved, back_b, uses, sums):
    rows, width = saved[0].shape
    hd = HEADS_DEV * HEAD_DIM
    u, qkv, probs, att, stats = saved

    def body(ins, outs, scratch):
        g, h, gain_ref, (wqt_ref, wot_ref, wg_ref), (u_ref, qkv_ref, p_ref, att_ref, st_ref), (b_ref,), uses, sums = ins
        gain_total, wo_sum, wq_sum = sums
        (down, up), gain_hbm, wo_hbm, wq_hbm = outs
        e_ref, dqkv_ref, dg_ref, wo_buf, wq_buf, gain_buf, sems = scratch
        copies = Copies(sems, is_odd())
        copies.push(b_ref, up.at[0], down.at[0])
        uses = [*uses, (u_ref, dqkv_ref, att_ref, g, dg_ref)]

        def put_wo(cols, value):
            wo_buf[:, cols] = (wo_sum[:, cols] + value).astype(BF16)
            copies.push(wo_buf.at[:, cols], wo_hbm.at[0, :, cols])

        def put_wq(at, value):
            wq_buf[at, :] = (wq_sum[at, :] + value).astype(BF16)
            copies.push(wq_buf.at[at], wq_hbm.at[0, at])

        def done(cols):
            copies.push(e_ref.at[:, cols], down.at[0, :, cols], up.at[0, :, cols])

        out_weights(uses, width, put_wo)
        attention_reverse(dot(whole(g), wot_ref[...]).astype(BF16), qkv_ref, p_ref, dqkv_ref)
        in_weights(uses, width, put_wq)
        norm_reverse(g, h, gain_ref, wqt_ref, wg_ref, qkv_ref, st_ref, [e_ref], dqkv_ref, dg_ref, done)
        gain_buf[...] = jnp.sum(gain_total[...] + gain_sum(uses), axis=0, keepdims=True).astype(BF16)
        copies.push(gain_buf, gain_hbm)
        copies.wait()

    return call(
        "finish", body, [g, h, gain, turned, list(saved), back_b, list(uses), list(sums)],
        [
            [jax.ShapeDtypeStruct((1, rows, width), BF16)] * 2,
            jax.ShapeDtypeStruct((1, width), BF16),
            jax.ShapeDtypeStruct((1, hd, width), BF16),
            jax.ShapeDtypeStruct((1, width, 3 * hd), BF16),
        ],
        [
            pltpu.VMEM((rows, width), BF16),
            pltpu.VMEM(qkv.shape, BF16),
            pltpu.VMEM((8, width), F32),
            pltpu.VMEM((hd, width), BF16),
            pltpu.VMEM((width, 3 * hd), BF16),
            pltpu.VMEM((1, width), BF16),
            pltpu.SemaphoreType.DMA((2 + width // 512 * 2 + width // 256,)),
        ],
    )


def shards(acts_down, acts_up, cotangent_down, cotangent_up, ln_gain, w_qkv, w_out, band_offsets):
    sections = lax.axis_size("section")
    near = [(i, i ^ 1) for i in range(sections)]
    far = [(i, (i + (1 if i % 2 else -1)) % sections) for i in range(sections)]

    def swap_near(x):
        return [lax.ppermute(part, "section", near) for part in x]

    def swap_far(x):
        return [lax.ppermute(part, "section", far) for part in x]

    def after(x, other):
        return lax.optimization_barrier((x, other))[0]

    a0, b0, gain, wq, wo, mask, a1_out, a0_saved = first_kernel(
        band_offsets.T, ln_gain, w_qkv, w_out, acts_down, acts_up, 1)
    fixed = [gain, wq, wo]
    a1 = swap_far(a1_out)
    b1_out, b0_saved = forward_kernel(after(b0, a0_saved[4]), fixed, mask, NEAR_PARTS)
    b1 = swap_near(b1_out)
    b2_out, b1_saved = forward_kernel(after(b1, b0_saved[4]), fixed, mask, 1)
    b2 = swap_far(b2_out)
    *turned, cot_a, cot_b, datt_a, datt_b = prepare_kernel(gain, wq, wo, b1_saved[4], cotangent_down, cotangent_up)
    a2_out, a1_saved = forward_kernel(after(a1, turned[2]), fixed, mask, 1, us=8)
    a2 = swap_near(a2_out)
    eb2, use_b2 = turn_kernel(after(b2, a1_saved[4]), cot_b, datt_b, fixed, mask, turned, 1)
    cb1 = swap_far(eb2)
    ea2, use_a2 = turn_kernel(after(a2, use_b2[4]), cot_a, datt_a, fixed, mask, turned, NEAR_PARTS)
    ca1 = swap_near(ea2)
    ea1, use_a1 = backward_kernel(after(ca1, use_a2[4]), a1, gain, turned, a1_saved, 1)
    ca0 = swap_far(ea1)
    (out_down, out_up), sums = early_weights(
        [use_b2, use_a2, after(use_a1, use_a1[4])], a2, use_a2[2], b2, use_b2[2], wo)
    eb1, use_b1 = backward_kernel(after(cb1, sums[0]), b1, gain, turned, b1_saved, NEAR_PARTS)
    cb0 = swap_near(eb1)
    sums = more_weights([after(use_b1, use_b1[4])], sums)
    back_b, use_b0 = backward_kernel(after(cb0, sums[0]), b0, gain, turned, b0_saved, 1)
    (back_down, back_up), d_gain, d_wo, d_wq = finish_kernel(
        after(ca0, use_b0[4]), a0, gain, turned, a0_saved, back_b, [use_b0], sums)
    return out_down, out_up, back_down, back_up, d_gain, d_wq, d_wo


def solution(mesh):
    both = ("groups", "section")
    in_specs = (
        P(both, None, None), P(both, None, None), P(both, None, None), P(both, None, None),
        P("section", None), P("section", None, None), P("section", None, None), P(),
    )
    out_specs = (
        P(both, None, None), P(both, None, None), P(both, None, None), P(both, None, None),
        P(both, None), P(both, None, None), P(both, None, None),
    )
    return jax.shard_map(shards, mesh=mesh, in_specs=in_specs, out_specs=out_specs, check_vma=False)
```

```python
import math

import jax
import jax.numpy as jnp
from jax import lax
from jax.experimental import pallas as pl
from jax.experimental.pallas import tpu as pltpu
from jax.sharding import PartitionSpec as P

HEADS_DEV = 2
HEAD_DIM = 128
BLOCK = 32
CHUNK = 16
F32 = jnp.float32
BF16 = jnp.bfloat16
NT = (((1,), (1,)), ((), ()))
TN = (((0,), (0,)), ((), ()))
SCALE = 1.0 / math.sqrt(HEAD_DIM)
VM = pl.BlockSpec(memory_space=pltpu.VMEM)
NEAR_PARTS = 2


def dot(a, b, dims=(((1,), (0,)), ((), ()))):
    return lax.dot_general(a, b, dims, preferred_element_type=F32)


def mask_body(odd, offs_ref, rows):
    row = lax.broadcasted_iota(jnp.int32, (rows, rows), 0)
    col = lax.broadcasted_iota(jnp.int32, (rows, rows), 1)
    row_block = row // BLOCK
    col_block = col // BLOCK
    near = row_block == col_block
    for block in range(offs_ref.shape[1]):
        for listed in range(offs_ref.shape[0]):
            near = near | ((row_block == block) & (col_block == block - offs_ref[listed, block]))
    keep = (col <= row) & (near | jnp.logical_not(odd))
    return jnp.where(keep, 1.0, 0.0).astype(F32)


def read(refs, at, size, cols=slice(None)):
    held = refs[0].shape[0]
    return refs[at // held][pl.ds(at % held, size), cols]


def write(refs, at, size, value, cols=slice(None)):
    held = refs[0].shape[0]
    refs[at // held][pl.ds(at % held, size), cols] = value


def whole(refs, cols=slice(None)):
    return jnp.concatenate([ref[:, cols] for ref in refs], axis=0)


def attend(h, gain_ref, wq_ref, mask_ref, u_ref, qkv_ref, p_ref, att_ref, st_ref, waits=None):
    rows, width = u_ref.shape
    hd = HEADS_DEV * HEAD_DIM
    gain = gain_ref[...].astype(F32)
    for start in range(0, rows, CHUNK):
        part = pl.ds(start, CHUNK)
        x = read(h, start, CHUNK).astype(F32)
        mean = jnp.sum(x, axis=-1, keepdims=True) * (1.0 / width)
        centred = x - mean
        rstd = lax.rsqrt(jnp.sum(centred * centred, axis=-1, keepdims=True) * (1.0 / width) + 1e-05)
        u_ref[part, :] = (centred * rstd * gain).astype(BF16)
        st_ref[part, :] = jnp.concatenate(
            [jnp.broadcast_to(mean, (CHUNK, 128)), jnp.broadcast_to(rstd, (CHUNK, 128))], axis=1)
    if waits:
        total = None
        depth = width // (len(waits) - 1)
        for n in range(len(waits) - 1):
            waits[n].wait()
            at = n * depth
            part = dot(u_ref[:, at:at + depth], wq_ref[at:at + depth, :])
            total = part if total is None else total + part
        qkv_ref[...] = total.astype(BF16)
    else:
        for n in range(3):
            qkv_ref[:, n * hd:(n + 1) * hd] = dot(u_ref[...], wq_ref[:, n * hd:(n + 1) * hd]).astype(BF16)
    keep = mask_ref[...]
    heads = [pl.ds(head * HEAD_DIM, HEAD_DIM) for head in range(HEADS_DEV)]
    scores = [dot(qkv_ref[:, cols], qkv_ref[:, pl.ds(hd + cols.start, HEAD_DIM)], NT) for cols in heads]
    weighted = [jnp.where(keep > 0.0, jnp.exp(score * SCALE), 0.0) for score in scores]
    probs = [value / jnp.sum(value, axis=-1, keepdims=True) for value in weighted]
    mixed = [
        dot(value.astype(BF16), qkv_ref[:, pl.ds(2 * hd + cols.start, HEAD_DIM)]) for value, cols in zip(probs, heads)
    ]
    for head, cols in enumerate(heads):
        p_ref[head] = probs[head]
        att_ref[:, cols] = mixed[head].astype(BF16)


def project_out(h, att_ref, wo_ref, out):
    rows, width = att_ref.shape[0], wo_ref.shape[1]
    for n in range(0, width, 512):
        cols = pl.ds(n, 512)
        value = dot(att_ref[...], wo_ref[:, cols])
        size = min(out[0].shape[0], h[0].shape[0])
        for at in range(0, rows, size):
            write(out, at, size, (read(h, at, size, cols).astype(F32) + value[at:at + size]).astype(BF16), cols)


def forward_body(h, gain_ref, wq_ref, wo_ref, mask_ref, out, u_ref, qkv_ref, p_ref, att_ref, st_ref, waits=None):
    attend(h, gain_ref, wq_ref, mask_ref, u_ref, qkv_ref, p_ref, att_ref, st_ref, waits)
    if waits:
        waits[-1].wait()
    project_out(h, att_ref, wo_ref, out)


def attention_reverse(datt, qkv_ref, p_ref, dqkv_ref):
    hd = HEADS_DEV * HEAD_DIM
    heads = [pl.ds(head * HEAD_DIM, HEAD_DIM) for head in range(HEADS_DEV)]
    keys = [pl.ds(hd + cols.start, HEAD_DIM) for cols in heads]
    values = [pl.ds(2 * hd + cols.start, HEAD_DIM) for cols in heads]
    das = [datt[:, cols.start:cols.start + HEAD_DIM] for cols in heads]
    probs = [p_ref[head] for head in range(HEADS_DEV)]
    dps = [dot(da, qkv_ref[:, cols], NT).astype(BF16).astype(F32) for da, cols in zip(das, values)]
    dvs = [dot(prob.astype(BF16), da, TN) for prob, da in zip(probs, das)]
    totals = [jnp.sum(dp * prob, axis=-1, keepdims=True) for dp, prob in zip(dps, probs)]
    dss = [(prob * (dp - total) * SCALE).astype(BF16) for prob, dp, total in zip(probs, dps, totals)]
    dqs = [dot(ds, qkv_ref[:, cols]) for ds, cols in zip(dss, keys)]
    dks = [dot(ds, qkv_ref[:, cols], TN) for ds, cols in zip(dss, heads)]
    for head in range(HEADS_DEV):
        dqkv_ref[:, values[head]] = dvs[head].astype(BF16)
        dqkv_ref[:, heads[head]] = dqs[head].astype(BF16)
        dqkv_ref[:, keys[head]] = dks[head].astype(BF16)


def lanes(column):
    return jnp.broadcast_to(column, (column.shape[0], 128))


def norm_reverse(g, h, gain_ref, wqt_ref, wg_ref, qkv_ref, st_ref, e, dqkv_ref, dg_ref, done=None):
    rows, width = dqkv_ref.shape[0], wqt_ref.shape[1]
    dqkv32 = dqkv_ref[...].astype(F32)
    first = jnp.sum(dqkv32 * wg_ref[...], axis=-1, keepdims=True) * (1.0 / width)
    second = jnp.sum(dqkv32 * qkv_ref[...].astype(F32), axis=-1, keepdims=True) * (1.0 / width)
    mean, rstd = st_ref[:, 0:128], st_ref[:, 128:256]
    first, second = lanes(first) * rstd, lanes(second) * rstd * rstd
    for block in range(0, width, 512):
        wide = dot(dqkv_ref[...], wqt_ref[:, block:block + 512])
        for n in range(0, 512, 128):
            cols = pl.ds(block + n, 128)
            du = wide[:, n:n + 128]
            centred = whole(h, cols).astype(F32) - mean
            du = du * rstd
            if dg_ref is not None:
                dg_ref[:, cols] = jnp.sum((du * centred).reshape(rows // 8, 8, 128), axis=0)
            gain = gain_ref[:, cols].astype(F32)
            value = du * gain - centred * second - first + whole(g, cols).astype(F32)
            size = e[0].shape[0]
            for part in range(len(e)):
                e[part][:, cols] = value[part * size:(part + 1) * size].astype(BF16)
        if done:
            done(pl.ds(block, 512))


def backward_body(g, h, gain_ref, wqt_ref, wot_ref, wg_ref, qkv_ref, p_ref, st_ref, e, dqkv_ref, dg_ref):
    attention_reverse(dot(whole(g), wot_ref[...]).astype(BF16), qkv_ref, p_ref, dqkv_ref)
    norm_reverse(g, h, gain_ref, wqt_ref, wg_ref, qkv_ref, st_ref, e, dqkv_ref, dg_ref)


def params(mib):
    return pltpu.CompilerParams(vmem_limit_bytes=mib << 20)


def cost(us):
    return pl.CostEstimate(flops=int(us * 1e9), bytes_accessed=int(us * 1e5), transcendentals=0)


def by_place(odd, when_odd, when_even):
    def start():
        pl.when(odd)(when_odd.start)
        pl.when(jnp.logical_not(odd))(when_even.start)

    return start, when_odd.wait


def is_odd():
    return lax.axis_index("section") % 2 == 1


def call(name, body, operands, outs, scratch=(), hbm=(), alias=(), us=0.002, mib=24):
    flat_in, tree_in = jax.tree.flatten(operands, is_leaf=lambda x: isinstance(x, Far))
    flat_out, tree_out = jax.tree.flatten(outs, is_leaf=lambda x: isinstance(x, (jax.ShapeDtypeStruct, Mem)))

    def kernel(*refs):
        a, b = len(flat_in), len(flat_in) + len(flat_out)
        body(jax.tree.unflatten(tree_in, refs[:a]), jax.tree.unflatten(tree_out, refs[a:b]), refs[b:])

    far = pl.BlockSpec(memory_space=pltpu.HBM)
    result = pl.pallas_call(
        kernel,
        in_specs=[far if isinstance(x, Far) else VM for x in flat_in],
        out_specs=[far if isinstance(x, jax.ShapeDtypeStruct) else VM for x in flat_out],
        out_shape=[x if isinstance(x, jax.ShapeDtypeStruct) else pltpu.VMEM(x.shape, x.dtype) for x in flat_out],
        scratch_shapes=list(scratch),
        input_output_aliases=dict(alias),
        compiler_params=params(mib),
        cost_estimate=cost(us),
        name=name,
    )(*[x.array if isinstance(x, Far) else x for x in flat_in])
    return jax.tree.unflatten(tree_out, result)


class Far:
    def __init__(self, array):
        self.array = pltpu.with_memory_space_constraint(array, pltpu.HBM)


class Mem:
    def __init__(self, shape, dtype):
        self.shape, self.dtype = shape, dtype


def stream(rows, width, parts):
    return [Mem((rows // parts, width), BF16) for _ in range(parts)]


def saved_outs(rows, width):
    hd = HEADS_DEV * HEAD_DIM
    return [
        Mem((rows, width), BF16),
        Mem((rows, 3 * hd), BF16),
        Mem((HEADS_DEV, rows, rows), F32),
        Mem((rows, hd), BF16),
        Mem((rows, 256), F32),
    ]


def first_kernel(offs, gain, wq, wo, down, up, parts):
    _, rows, width = down.shape
    hd = HEADS_DEV * HEAD_DIM

    def body(ins, outs, scratch):
        offs_hbm, gain_hbm, wq_hbm, wo_hbm, down_hbm, up_hbm = ins
        (a_ref,), (b_ref,), gain_ref, wq_ref, wo_ref, mask_ref, out, saved = outs
        offs_ref, sems = scratch
        odd = is_odd()

        def pick(source, target, sem):
            return pltpu.make_async_copy(source, target, sems.at[sem])

        a_start, a_wait = by_place(odd, pick(down_hbm.at[0], a_ref, 0), pick(up_hbm.at[0], a_ref, 0))
        b_start, b_wait = by_place(odd, pick(up_hbm.at[0], b_ref, 1), pick(down_hbm.at[0], b_ref, 1))
        offs_copy = pick(offs_hbm, offs_ref, 2)
        gain_copy = pick(gain_hbm, gain_ref, 3)
        wo_copy = pick(wo_hbm.at[0], wo_ref, 4)
        spans = [pl.ds(n * (width // 4), width // 4) for n in range(4)]
        wq_copies = [pick(wq_hbm.at[0, span], wq_ref.at[span], 5 + n) for n, span in enumerate(spans)]
        a_start()
        gain_copy.start()
        offs_copy.start()
        for copy in wq_copies:
            copy.start()
        wo_copy.start()
        b_start()
        offs_copy.wait()
        mask_ref[...] = mask_body(odd, offs_ref, rows)
        a_wait()
        gain_copy.wait()
        forward_body([a_ref], gain_ref, wq_ref, wo_ref, mask_ref, out, *saved, waits=wq_copies + [wo_copy])
        b_wait()

    return call(
        "first", body, [Far(x) for x in (offs, gain, wq, wo, down, up)],
        [
            stream(rows, width, 1), stream(rows, width, 1), Mem(gain.shape, BF16), Mem(wq.shape[1:], BF16),
            Mem(wo.shape[1:], BF16), Mem((rows, rows), F32), stream(rows, width, parts), saved_outs(rows, width),
        ],
        [pltpu.SMEM(offs.shape, jnp.int32), pltpu.SemaphoreType.DMA((9,))],
    )


def forward_kernel(h, fixed, mask, parts, us=0.002):
    rows, width = h[0].shape[0] * len(h), h[0].shape[1]

    def body(ins, outs, scratch):
        h, fixed, mask_ref = ins
        out, saved = outs
        forward_body(h, *fixed, mask_ref, out, *saved)

    return call("forward", body, [h, fixed, mask], [stream(rows, width, parts), saved_outs(rows, width)], us=us)


def prepare_kernel(gain, wq, wo, tie, down, up):
    _, rows, width = down.shape
    hd = HEADS_DEV * HEAD_DIM

    def body(ins, outs, scratch):
        gain_ref, wq_ref, wo_ref, _, down_hbm, up_hbm = ins
        wqt_ref, wot_ref, wg_ref, (a_ref,), (b_ref,), da_ref, db_ref = outs
        (sems,) = scratch
        odd = is_odd()

        def pick(source, target, sem):
            return pltpu.make_async_copy(source.at[0], target, sems.at[sem])

        a_start, a_wait = by_place(odd, pick(down_hbm, a_ref, 0), pick(up_hbm, a_ref, 0))
        b_start, b_wait = by_place(odd, pick(up_hbm, b_ref, 1), pick(down_hbm, b_ref, 1))
        a_start()
        b_start()
        for at in range(0, width, 256):
            wqt_ref[:, at:at + 256] = wq_ref[at:at + 256, :].T
            wot_ref[at:at + 256, :] = wo_ref[:, at:at + 256].T
        wg_ref[...] = dot(gain_ref[...], wq_ref[...])
        a_wait()
        b_wait()
        both = dot(jnp.concatenate([a_ref[...], b_ref[...]], axis=0), wot_ref[...]).astype(BF16)
        da_ref[...] = both[:rows]
        db_ref[...] = both[rows:]

    return call(
        "prepare", body, [gain, wq, wo, tie, Far(down), Far(up)],
        [Mem((3 * hd, width), BF16), Mem((width, hd), BF16), Mem((1, 3 * hd), F32),
         stream(rows, width, 1), stream(rows, width, 1), Mem((rows, hd), BF16), Mem((rows, hd), BF16)],
        [pltpu.SemaphoreType.DMA((2,))],
    )


def turn_kernel(h, g, datt, fixed, mask, turned, parts):
    rows, width = h[0].shape[0] * len(h), h[0].shape[1]
    hd = HEADS_DEV * HEAD_DIM

    def body(ins, outs, scratch):
        h, g, datt_ref, (gain_ref, wq_ref), mask_ref, (wqt_ref, wg_ref) = ins
        e, (u_ref, dqkv_ref, att_ref, st_ref) = outs
        qkv_ref, p_ref = scratch
        attend(h, gain_ref, wq_ref, mask_ref, u_ref, qkv_ref, p_ref, att_ref, st_ref)
        attention_reverse(datt_ref[...], qkv_ref, p_ref, dqkv_ref)
        norm_reverse(g, h, gain_ref, wqt_ref, wg_ref, qkv_ref, st_ref, e, dqkv_ref, None)

    e, (u, dqkv, att, stats) = call(
        "turn", body, [h, g, datt, fixed[:2], mask, [turned[0], turned[2]]],
        [
            stream(rows, width, parts),
            [Mem((rows, width), BF16), Mem((rows, 3 * hd), BF16), Mem((rows, hd), BF16), Mem((rows, 256), F32)],
        ],
        [
            pltpu.VMEM((rows, 3 * hd), BF16),
            pltpu.VMEM((HEADS_DEV, rows, rows), F32),
        ],
    )
    return e, (u, dqkv, att, g, stats)


def backward_kernel(g, h, gain, turned, saved, parts):
    rows, width = saved[0].shape
    u, qkv, probs, att, stats = saved

    def body(ins, outs, scratch):
        g, h, gain_ref, turned, (qkv_ref, p_ref, st_ref) = ins
        e, dqkv_ref, dg_ref = outs
        backward_body(g, h, gain_ref, *turned, qkv_ref, p_ref, st_ref, e, dqkv_ref, dg_ref)

    e, dqkv, dgain = call(
        "backward", body, [g, h, gain, turned, [qkv, probs, stats]],
        [stream(rows, width, parts), Mem(qkv.shape, BF16), Mem((8, width), F32)],
    )
    return e, (u, dqkv, att, g, dgain)


def out_weights(uses, width, put):
    att = jnp.concatenate([use[2][...] for use in uses], axis=0)
    for n in range(0, width, 512):
        cols = pl.ds(n, 512)
        put(cols, dot(att, jnp.concatenate([whole(use[3], cols) for use in uses], axis=0), TN))


def in_weights(uses, width, put):
    dqkv = jnp.concatenate([use[1][...] for use in uses], axis=0)
    for m in range(0, width, 256):
        put(pl.ds(m, 256), dot(jnp.concatenate([use[0][:, m:m + 256] for use in uses], axis=0), dqkv, TN))


def gain_sum(uses):
    total = uses[0][4][...]
    for use in uses[1:]:
        total = total + use[4][...]
    return total


class Copies:
    def __init__(self, sems, odd):
        self.sems, self.odd, self.waits = sems, odd, []

    def push(self, source, target, other=None):
        sem = self.sems.at[len(self.waits)]
        copy = pltpu.make_async_copy(source, target, sem)
        if other is None:
            copy.start()
        else:
            by_place(self.odd, copy, pltpu.make_async_copy(source, other, sem))[0]()
        self.waits.append(copy.wait)

    def wait(self):
        for wait in self.waits:
            wait()


def early_weights(uses, h_a, h_b, wo, wqt):
    rows, width = uses[0][0].shape
    hd = HEADS_DEV * HEAD_DIM

    def body(ins, outs, scratch):
        uses, h_a, h_b, wo_ref, wqt_ref = ins
        (down, up), gain_out, wo_out, wq_out = outs
        a_ref, b_ref, sems = scratch
        copies = Copies(sems, is_odd())
        project_out(h_a, uses[1][2], wo_ref, [a_ref])
        copies.push(a_ref, down.at[0], up.at[0])
        project_out(h_b, uses[0][2], wo_ref, [b_ref])
        copies.push(b_ref, up.at[0], down.at[0])
        for block in range(0, width, 512):
            wide = [dot(use[1][...], wqt_ref[:, block:block + 512]) for use in uses[:2]]
            for n in range(0, 512, 128):
                cols = pl.ds(block + n, 128)
                total = uses[2][4][:, cols]
                for use, h, du in zip(uses, (h_b, h_a), wide):
                    xhat = (whole(h, cols).astype(F32) - use[4][:, 0:128]) * use[4][:, 128:256]
                    total = total + jnp.sum((du[:, n:n + 128] * xhat).reshape(rows // 8, 8, 128), axis=0)
                gain_out[:, cols] = total

        def put_wo(cols, value):
            wo_out[:, cols] = value

        def put_wq(at, value):
            wq_out[at, :] = value

        out_weights(uses, width, put_wo)
        in_weights(uses, width, put_wq)
        copies.wait()

    outs, *sums = call(
        "early_weights", body, [list(uses), h_a, h_b, wo, wqt],
        [[jax.ShapeDtypeStruct((1, rows, width), BF16)] * 2,
         Mem((8, width), F32), Mem((hd, width), F32), Mem((width, 3 * hd), F32)],
        [pltpu.VMEM((rows, width), BF16), pltpu.VMEM((rows, width), BF16), pltpu.SemaphoreType.DMA((2,))],
    )
    return outs, sums


def more_weights(uses, sums):
    width = uses[0][0].shape[1]

    def body(ins, outs, scratch):
        uses, (gain_in, wo_in, wq_in) = ins
        gain_out, wo_out, wq_out = outs
        gain_out[...] = gain_in[...] + gain_sum(uses)

        def put_wo(cols, value):
            wo_out[:, cols] = wo_in[:, cols] + value

        def put_wq(at, value):
            wq_out[at, :] = wq_in[at, :] + value

        out_weights(uses, width, put_wo)
        in_weights(uses, width, put_wq)

    return call("more_weights", body, [list(uses), list(sums)], [Mem(x.shape, F32) for x in sums])


def finish_kernel(g, h, gain, turned, saved, back_b, uses, sums):
    rows, width = saved[0].shape
    hd = HEADS_DEV * HEAD_DIM
    u, qkv, probs, att, stats = saved

    def body(ins, outs, scratch):
        g, h, gain_ref, (wqt_ref, wot_ref, wg_ref), (u_ref, qkv_ref, p_ref, att_ref, st_ref), (b_ref,), uses, sums = ins
        gain_total, wo_sum, wq_sum = sums
        (down, up), gain_hbm, wo_hbm, wq_hbm = outs
        e_ref, dqkv_ref, dg_ref, wo_buf, wq_buf, gain_buf, sems = scratch
        copies = Copies(sems, is_odd())
        copies.push(b_ref, up.at[0], down.at[0])
        uses = [*uses, (u_ref, dqkv_ref, att_ref, g, dg_ref)]

        def put_wo(cols, value):
            wo_buf[:, cols] = (wo_sum[:, cols] + value).astype(BF16)
            copies.push(wo_buf.at[:, cols], wo_hbm.at[0, :, cols])

        def put_wq(at, value):
            wq_buf[at, :] = (wq_sum[at, :] + value).astype(BF16)
            copies.push(wq_buf.at[at], wq_hbm.at[0, at])

        def done(cols):
            copies.push(e_ref.at[:, cols], down.at[0, :, cols], up.at[0, :, cols])

        out_weights(uses, width, put_wo)
        attention_reverse(dot(whole(g), wot_ref[...]).astype(BF16), qkv_ref, p_ref, dqkv_ref)
        in_weights(uses, width, put_wq)
        norm_reverse(g, h, gain_ref, wqt_ref, wg_ref, qkv_ref, st_ref, [e_ref], dqkv_ref, dg_ref, done)
        gain_buf[...] = jnp.sum(gain_total[...] + gain_sum(uses), axis=0, keepdims=True).astype(BF16)
        copies.push(gain_buf, gain_hbm)
        copies.wait()

    return call(
        "finish", body, [g, h, gain, turned, list(saved), back_b, list(uses), list(sums)],
        [
            [jax.ShapeDtypeStruct((1, rows, width), BF16)] * 2,
            jax.ShapeDtypeStruct((1, width), BF16),
            jax.ShapeDtypeStruct((1, hd, width), BF16),
            jax.ShapeDtypeStruct((1, width, 3 * hd), BF16),
        ],
        [
            pltpu.VMEM((rows, width), BF16),
            pltpu.VMEM(qkv.shape, BF16),
            pltpu.VMEM((8, width), F32),
            pltpu.VMEM((hd, width), BF16),
            pltpu.VMEM((width, 3 * hd), BF16),
            pltpu.VMEM((1, width), BF16),
            pltpu.SemaphoreType.DMA((2 + width // 512 * 2 + width // 256,)),
        ],
    )


def shards(acts_down, acts_up, cotangent_down, cotangent_up, ln_gain, w_qkv, w_out, band_offsets):
    sections = lax.axis_size("section")
    near = [(i, i ^ 1) for i in range(sections)]
    far = [(i, (i + (1 if i % 2 else -1)) % sections) for i in range(sections)]

    def swap_near(x):
        return [lax.ppermute(part, "section", near) for part in x]

    def swap_far(x):
        return [lax.ppermute(part, "section", far) for part in x]

    def after(x, other):
        return lax.optimization_barrier((x, other))[0]

    a0, b0, gain, wq, wo, mask, a1_out, a0_saved = first_kernel(
        band_offsets.T, ln_gain, w_qkv, w_out, acts_down, acts_up, 1)
    fixed = [gain, wq, wo]
    a1 = swap_far(a1_out)
    b1_out, b0_saved = forward_kernel(after(b0, a0_saved[4]), fixed, mask, NEAR_PARTS)
    b1 = swap_near(b1_out)
    b2_out, b1_saved = forward_kernel(after(b1, b0_saved[4]), fixed, mask, 1)
    b2 = swap_far(b2_out)
    *turned, cot_a, cot_b, datt_a, datt_b = prepare_kernel(gain, wq, wo, b1_saved[4], cotangent_down, cotangent_up)
    a2_out, a1_saved = forward_kernel(after(a1, turned[2]), fixed, mask, 1, us=8)
    a2 = swap_near(a2_out)
    eb2, use_b2 = turn_kernel(after(b2, a1_saved[4]), cot_b, datt_b, fixed, mask, turned, 1)
    cb1 = swap_far(eb2)
    ea2, use_a2 = turn_kernel(after(a2, use_b2[4]), cot_a, datt_a, fixed, mask, turned, NEAR_PARTS)
    ca1 = swap_near(ea2)
    ea1, use_a1 = backward_kernel(after(ca1, use_a2[4]), a1, gain, turned, a1_saved, 1)
    ca0 = swap_far(ea1)
    (out_down, out_up), sums = early_weights(
        [use_b2, use_a2, after(use_a1, use_a1[4])], a2, b2, wo, turned[0])
    eb1, use_b1 = backward_kernel(after(cb1, sums[0]), b1, gain, turned, b1_saved, NEAR_PARTS)
    cb0 = swap_near(eb1)
    sums = more_weights([after(use_b1, use_b1[4])], sums)
    back_b, use_b0 = backward_kernel(after(cb0, sums[0]), b0, gain, turned, b0_saved, 1)
    (back_down, back_up), d_gain, d_wo, d_wq = finish_kernel(
        after(ca0, use_b0[4]), a0, gain, turned, a0_saved, back_b, [use_b0], sums)
    return out_down, out_up, back_down, back_up, d_gain, d_wq, d_wo


def solution(mesh):
    both = ("groups", "section")
    in_specs = (
        P(both, None, None), P(both, None, None), P(both, None, None), P(both, None, None),
        P("section", None), P("section", None, None), P("section", None, None), P(),
    )
    out_specs = (
        P(both, None, None), P(both, None, None), P(both, None, None), P(both, None, None),
        P(both, None), P(both, None, None), P(both, None, None),
    )
    return jax.shard_map(shards, mesh=mesh, in_specs=in_specs, out_specs=out_specs, check_vma=False)
```
